32 devices in a mesh: seq: 4 (over y, x), ctx: 8 (over z, core).
Axes of the slice: x: 2, y: 2, z: 4, core: 2. Of those that a mesh axis runs over, the one named last changes fastest.
Arguments:
- inputs: bfloat16 [4096, 1152], P(('seq', 'ctx')), may hold values from -140 to 140
- positions: int32 [4096], P(('seq', 'ctx')), may hold values from 0 to 1023, as said below
- attention_gain: bfloat16 [1152], P(('seq', 'ctx')), may hold values from 0.3984375 to 1.59375
- query_weight: bfloat16 [1152, 1024], P(('seq', 'ctx')), may hold values from -0.1875 to 0.1875
- key_weight: bfloat16 [1152, 256], P(('seq', 'ctx')), may hold values from -0.1875 to 0.1875
- value_weight: bfloat16 [1152, 256], P(('seq', 'ctx')), may hold values from -0.1875 to 0.1875
- query_gain: bfloat16 [256], P(('seq', 'ctx')), may hold values from 0.5 to 1.5
- key_gain: bfloat16 [256], P(('seq', 'ctx')), may hold values from 0.5 to 1.5
- output_weight: bfloat16 [1024, 1152], P(('seq', 'ctx')), may hold values from -0.1875 to 0.1875
- attention_post: bfloat16 [1152], P(('seq', 'ctx')), may hold values from 0.3984375 to 1.59375
- feedfwd_gain: bfloat16 [1152], P(('seq', 'ctx')), may hold values from 0.3984375 to 1.59375
- gate_weight: bfloat16 [1152, 6912], P(('seq', 'ctx')), may hold values from -0.1875 to 0.1875
- up_weight: bfloat16 [1152, 6912], P(('seq', 'ctx')), may hold values from -0.1875 to 0.1875
- down_weight: bfloat16 [6912, 1152], P(('seq', 'ctx')), may hold values from -0.078125 to 0.078125
- feedfwd_post: bfloat16 [1152], P(('seq', 'ctx')), may hold values from 0.3984375 to 1.59375
- cotangent: bfloat16 [4096, 1152], P(('seq', 'ctx')), may hold values from -6 to 6
Outputs:
- block_out: bfloat16 [4096, 1152], P(('seq', 'ctx'))
- input_grad: float32 [4096, 1152], P(('seq', 'ctx'))
- attention_gain_grad: float32 [1152], P(('seq', 'ctx'))
- query_grad: float32 [1152, 1024], P(('seq', 'ctx'))
- key_grad: float32 [1152, 256], P(('seq', 'ctx'))
- value_grad: float32 [1152, 256], P(('seq', 'ctx'))
- query_gain_grad: float32 [256], P(('seq', 'ctx'))
- key_gain_grad: float32 [256], P(('seq', 'ctx'))
- output_grad: float32 [1024, 1152], P(('seq', 'ctx'))
- attention_post_grad: float32 [1152], P(('seq', 'ctx'))
- feedfwd_gain_grad: float32 [1152], P(('seq', 'ctx'))
- gate_grad: float32 [1152, 6912], P(('seq', 'ctx'))
- up_grad: float32 [1152, 6912], P(('seq', 'ctx'))
- down_grad: float32 [6912, 1152], P(('seq', 'ctx'))
- feedfwd_post_grad: float32 [1152], P(('seq', 'ctx'))
The draws below stay inside these ranges and needn't reach their ends.
Inputs may be any that keep to these rules, and one draw needn't show every extreme that they name: Within each sequence of 1024 tokens, the 128 tokens of each ctx index hold the consecutive positions k * 128 to k * 128 + 127, where the block numbers k of one sequence's ctx indices are a permutation of 0 to 7, drawn afresh for every sequence.
All inputs are finite; a program needn't handle non-finite values.
Results may differ from the reference program's by a relative error of at most 0.038.
Values may be sent and summed in bfloat16 or wider, within the bound.
A program may use at most 448 MiB of HBM per device.

```python
import math
import jax
import jax.numpy as jnp
from jax import lax

D = 1152
H = 4
DH = 256
FF = 6912
TOK_DEV = 128
LENGTH = 1024
SEQS = 4
TOKENS = 4096


def draw_positions(key, part):
    block_total = LENGTH // TOK_DEV
    subkeys = jax.random.split(key, SEQS)
    orders = jax.vmap(lambda subkey: jax.random.permutation(subkey, block_total))(subkeys)
    offsets = jnp.arange(TOK_DEV, dtype=jnp.int32)
    table = orders.astype(jnp.int32)[:, :, None] * TOK_DEV + offsets[None, None, :]
    return table.reshape(TOKENS)


def draw_inputs(key, part):
    key_base, key_rows, key_cols, key_pair = jax.random.split(jax.random.fold_in(key, 7), 4)
    device_total = TOKENS // TOK_DEV
    base = jax.random.truncated_normal(key_base, -3.0, 3.0, (TOKENS, D), jnp.float32)
    row_scale = jnp.exp(jax.random.uniform(key_rows, (TOKENS, 1), jnp.float32, math.log(0.3), math.log(3.0)))
    col_scale = jnp.exp(jax.random.uniform(key_cols, (1, D), jnp.float32, math.log(0.3), math.log(3.0)))
    pairing = jax.random.permutation(key_pair, device_total)
    row_block = jnp.arange(TOKENS, dtype=jnp.int32) // TOK_DEV
    col_block = jnp.arange(D, dtype=jnp.int32) // (D // device_total)
    spiked = col_block[None, :] == pairing[row_block][:, None]
    values = base * row_scale * col_scale * jnp.where(spiked, 2.5, 1.0)
    return values.astype(jnp.bfloat16)


def level_of(stream_key, shape, cuts, least, top_value):
    def one(position, blocks):
        heights = jax.random.uniform(jax.random.fold_in(jax.random.fold_in(stream_key, 6), position), (blocks,), jnp.float32, least / len(cuts), top_value / len(cuts))
        return jnp.repeat(jnp.exp(heights), shape[position] // blocks).reshape((-1,) + (1,) * (len(shape) - position - 1))

    loudness = one(*cuts[0])
    for cut in cuts[1:]:
        loudness = loudness * one(*cut)
    return loudness


def noise(key, shape, deviation, most, cuts=(), held_as=jnp.bfloat16):
    level = level_of(key, shape, cuts, -0.22, 0.18) if cuts else 1.0
    result = jax.random.normal(key, shape, jnp.float32) * deviation * level
    return jnp.minimum(jnp.maximum(result, -most), most).astype(held_as)


def setup_inputs(seed: int = 0) -> dict:
    key_of = jax.random.split(jax.random.key(seed), 17)
    return {
        "inputs": draw_inputs(jax.random.fold_in(key_of[16], 71), 0),
        "positions": draw_positions(jax.random.fold_in(key_of[16], 71), 0),
        "attention_gain": jnp.clip(1.0 + 0.12 * jax.random.normal(key_of[2], (D,), jnp.float32), 0.3984375, 1.59375).astype(jnp.bfloat16),
        "query_weight": noise(key_of[3], (D, H * DH), D ** -0.5, 0.1875, ((0, 32),)),
        "key_weight": noise(key_of[4], (D, DH), D ** -0.5, 0.1875, ((0, 32),)),
        "value_weight": noise(key_of[5], (D, DH), D ** -0.5, 0.1875, ((0, 32),)),
        "query_gain": jnp.clip(1.0 + 0.1 * jax.random.normal(key_of[6], (DH,), jnp.float32), 0.5, 1.5).astype(jnp.bfloat16),
        "key_gain": jnp.clip(1.0 + 0.1 * jax.random.normal(key_of[7], (DH,), jnp.float32), 0.5, 1.5).astype(jnp.bfloat16),
        "output_weight": noise(key_of[8], (H * DH, D), (H * DH) ** -0.5, 0.1875, ((0, 32),)),
        "attention_post": jnp.clip(1.0 + 0.12 * jax.random.normal(key_of[9], (D,), jnp.float32), 0.3984375, 1.59375).astype(jnp.bfloat16),
        "feedfwd_gain": jnp.clip(1.0 + 0.12 * jax.random.normal(key_of[10], (D,), jnp.float32), 0.3984375, 1.59375).astype(jnp.bfloat16),
        "gate_weight": noise(key_of[11], (D, FF), D ** -0.5, 0.1875, ((0, 32),)),
        "up_weight": noise(key_of[12], (D, FF), D ** -0.5, 0.1875, ((0, 32),)),
        "down_weight": noise(key_of[13], (FF, D), FF ** -0.5, 0.078125, ((0, 32),)),
        "feedfwd_post": jnp.clip(1.0 + 0.12 * jax.random.normal(key_of[14], (D,), jnp.float32), 0.3984375, 1.59375).astype(jnp.bfloat16),
        "cotangent": noise(key_of[15], (TOKENS, D), 1.0, 6.0, ((0, 32),)),
    }


EPSILON = 1e-06
THETA = 1000000.0
GELU_COEF = math.sqrt(2.0 / math.pi)

def rounded(values):
    return lax.optimization_barrier(values.astype(jnp.bfloat16))

def widened(values):
    return values.astype(jnp.float32)

def rms_factor(values):
    return lax.rsqrt(lax.optimization_barrier(jnp.mean(values * values, axis=-1, keepdims=True)) + EPSILON)

def norm_back(values, factor, gain_vector, upstream):
    scaled = gain_vector * upstream
    cubed = factor * factor * factor
    return factor * scaled - values * cubed * lax.optimization_barrier(jnp.mean(scaled * values, axis=-1, keepdims=True))

def rotary(places):
    half_width = DH // 2
    exponent = jnp.arange(half_width, dtype=jnp.float32) * (-2.0 / DH)
    frequency = jnp.power(jnp.float32(THETA), exponent)
    angles = places.astype(jnp.float32)[:, None] * frequency[None, :]
    return (jnp.cos(angles), jnp.sin(angles))

def rotate(values, cosine, sinus):
    half_width = values.shape[-1] // 2
    first = values[..., :half_width]
    second = values[..., half_width:]
    return jnp.concatenate([first * cosine - second * sinus, second * cosine + first * sinus], axis=-1)

def rotate_back(upstream, cosine, sinus):
    half_width = upstream.shape[-1] // 2
    first = upstream[..., :half_width]
    second = upstream[..., half_width:]
    return jnp.concatenate([first * cosine + second * sinus, second * cosine - first * sinus], axis=-1)

def gelu_tanh(values):
    inner = GELU_COEF * (values + 0.044715 * values * values * values)
    return 0.5 * values * (1.0 + jnp.tanh(inner))

def gelu_slope(values):
    inner = GELU_COEF * (values + 0.044715 * values * values * values)
    tangent = jnp.tanh(inner)
    return 0.5 * (1.0 + tangent) + 0.5 * values * (1.0 - tangent * tangent) * GELU_COEF * (1.0 + 3.0 * 0.044715 * values * values)

def times_right(left_side, right_side):
    return jnp.dot(left_side, right_side, preferred_element_type=jnp.float32)

def times_transposed(left_side, right_side):
    return lax.dot_general(left_side, right_side, (((1,), (1,)), ((), ())), preferred_element_type=jnp.float32)

def transposed_times(left_side, right_side):
    return lax.dot_general(left_side, right_side, (((0,), (0,)), ((), ())), preferred_element_type=jnp.float32)

def attend(query_part, place_part, key_rot, value_rows, key_places):
    scaling = 1.0 / math.sqrt(DH)
    scores = jnp.einsum('qhd,kd->hqk', widened(query_part), widened(key_rot)) * scaling
    allowed = key_places[None, None, :] <= place_part[None, :, None]
    expscore = jnp.where(allowed, jnp.exp(scores), 0.0)
    weight_sum = lax.optimization_barrier(jnp.sum(expscore, axis=-1))
    summed = jnp.einsum('hqk,kd->qhd', widened(rounded(expscore)), widened(value_rows))
    attended = rounded(summed / jnp.transpose(weight_sum)[:, :, None])
    return (attended, jnp.transpose(jnp.log(weight_sum)))

def attend_back(query_part, place_part, output_part, logsum_part, upper_part, key_rot, value_rows, key_places):
    scaling = 1.0 / math.sqrt(DH)
    upper_round = widened(rounded(upper_part))
    row_delta = lax.optimization_barrier(jnp.sum(upper_part * widened(output_part), axis=-1))
    scores = jnp.einsum('qhd,kd->hqk', widened(query_part), widened(key_rot)) * scaling
    allowed = key_places[None, None, :] <= place_part[None, :, None]
    probability = jnp.where(allowed, jnp.exp(scores - jnp.transpose(logsum_part)[:, :, None]), 0.0)
    value_sum = jnp.einsum('hqk,qhd->kd', widened(rounded(probability)), upper_round)
    prob_back = jnp.einsum('qhd,kd->hqk', upper_round, widened(value_rows))
    score_back = widened(rounded(probability * (prob_back - jnp.transpose(row_delta)[:, :, None]) * scaling))
    query_back = jnp.einsum('hqk,kd->qhd', score_back, widened(key_rot))
    key_back = jnp.einsum('hqk,qhd->kd', score_back, widened(query_part))
    return (query_back, key_back, value_sum)

def reference(inputs, positions, attention_gain, query_weight, key_weight, value_weight, query_gain, key_gain, output_weight, attention_post, feedfwd_gain, gate_weight, up_weight, down_weight, feedfwd_post, cotangent):
    gain_attention = widened(attention_gain)
    gain_query = widened(query_gain)
    gain_key = widened(key_gain)
    gain_post = widened(attention_post)
    gain_feed = widened(feedfwd_gain)
    gain_final = widened(feedfwd_post)
    block_len = min(LENGTH, 512)
    block_count = LENGTH // block_len

    def one_sequence(grad_state, packet):
        seq_inputs, seq_places, seq_cot = packet
        input_wide = widened(seq_inputs)
        input_factor = rms_factor(input_wide)
        normed = rounded(input_wide * input_factor * gain_attention)
        queries = times_right(normed, query_weight).reshape(LENGTH, H, DH)
        key_rows = times_right(normed, key_weight)
        value_rows = rounded(times_right(normed, value_weight))
        cosine, sinus = rotary(seq_places)
        query_factor = rms_factor(queries)
        query_rot = rounded(rotate(queries * query_factor * gain_query, cosine[:, None, :], sinus[:, None, :]))
        key_factor = rms_factor(key_rows)
        key_rot = rounded(rotate(key_rows * key_factor * gain_key, cosine, sinus))
        query_blocks = query_rot.reshape(block_count, block_len, H, DH)
        place_blocks = seq_places.reshape(block_count, block_len)
        attended_blocks, logsum_blocks = lax.map(lambda pair: attend(pair[0], pair[1], key_rot, value_rows, seq_places), (query_blocks, place_blocks))
        attended = attended_blocks.reshape(LENGTH, H * DH)
        mixed_values = times_right(attended, output_weight)
        mixed_factor = rms_factor(mixed_values)
        residual = input_wide + mixed_values * mixed_factor * gain_post
        residual_factor = rms_factor(residual)
        fed_rows = rounded(residual * residual_factor * gain_feed)
        gate_values = times_right(fed_rows, gate_weight)
        up_values = times_right(fed_rows, up_weight)
        hidden = rounded(gelu_tanh(gate_values) * up_values)
        down_values = times_right(hidden, down_weight)
        down_factor = rms_factor(down_values)
        block_out = rounded(residual + down_values * down_factor * gain_final)
        cot_wide = widened(seq_cot)
        grad_final = lax.optimization_barrier(jnp.sum(cot_wide * down_values * down_factor, axis=0))
        down_back = rounded(norm_back(down_values, down_factor, gain_final, cot_wide))
        grad_down = transposed_times(hidden, down_back)
        hidden_back = times_transposed(down_back, down_weight)
        gate_back = rounded(hidden_back * up_values * gelu_slope(gate_values))
        up_back = rounded(hidden_back * gelu_tanh(gate_values))
        grad_gate = transposed_times(fed_rows, gate_back)
        grad_up = transposed_times(fed_rows, up_back)
        fed_back = times_transposed(gate_back, gate_weight) + times_transposed(up_back, up_weight)
        grad_feed = lax.optimization_barrier(jnp.sum(fed_back * residual * residual_factor, axis=0))
        residual_back = cot_wide + norm_back(residual, residual_factor, gain_feed, fed_back)
        grad_post = lax.optimization_barrier(jnp.sum(residual_back * mixed_values * mixed_factor, axis=0))
        mixed_back = rounded(norm_back(mixed_values, mixed_factor, gain_post, residual_back))
        grad_output = transposed_times(attended, mixed_back)
        attended_back = times_transposed(mixed_back, output_weight).reshape(LENGTH, H, DH)

        def back_block(state_now, pieces):
            query_part, place_part, output_part, logsum_part, upper_part = pieces
            query_back, key_back, value_sum = attend_back(query_part, place_part, output_part, logsum_part, upper_part, key_rot, value_rows, seq_places)
            return ((state_now[0] + key_back, state_now[1] + value_sum), query_back)
        zero_rows = jnp.zeros((LENGTH, DH), jnp.float32)
        (key_rot_back, value_sum), query_parts = lax.scan(back_block, (zero_rows, zero_rows), (query_blocks, place_blocks, attended_blocks, logsum_blocks, attended_back.reshape(block_count, block_len, H, DH)))
        query_rot_back = query_parts.reshape(LENGTH, H, DH)
        query_up = rotate_back(query_rot_back, cosine[:, None, :], sinus[:, None, :])
        grad_qgain = lax.optimization_barrier(jnp.sum(query_up * queries * query_factor, axis=(0, 1)))
        query_back = rounded(norm_back(queries, query_factor, gain_query, query_up)).reshape(LENGTH, H * DH)
        key_up = rotate_back(key_rot_back, cosine, sinus)
        grad_kgain = lax.optimization_barrier(jnp.sum(key_up * key_rows * key_factor, axis=0))
        key_back = rounded(norm_back(key_rows, key_factor, gain_key, key_up))
        value_back = rounded(value_sum)
        grad_query = transposed_times(normed, query_back)
        grad_key = transposed_times(normed, key_back)
        grad_value = transposed_times(normed, value_back)
        normed_back = times_transposed(query_back, query_weight) + times_transposed(key_back, key_weight) + times_transposed(value_back, value_weight)
        grad_attention = lax.optimization_barrier(jnp.sum(normed_back * input_wide * input_factor, axis=0))
        input_grad = residual_back + norm_back(input_wide, input_factor, gain_attention, normed_back)
        terms = (grad_attention, grad_query, grad_key, grad_value, grad_qgain, grad_kgain, grad_output, grad_post, grad_feed, grad_gate, grad_up, grad_down, grad_final)
        updated = tuple((before + term for before, term in zip(grad_state, terms)))
        return (updated, (block_out, input_grad))
    initial = (jnp.zeros((D,), jnp.float32), jnp.zeros((D, H * DH), jnp.float32), jnp.zeros((D, DH), jnp.float32), jnp.zeros((D, DH), jnp.float32), jnp.zeros((DH,), jnp.float32), jnp.zeros((DH,), jnp.float32), jnp.zeros((H * DH, D), jnp.float32), jnp.zeros((D,), jnp.float32), jnp.zeros((D,), jnp.float32), jnp.zeros((D, FF), jnp.float32), jnp.zeros((D, FF), jnp.float32), jnp.zeros((FF, D), jnp.float32), jnp.zeros((D,), jnp.float32))
    packets = (inputs.reshape(SEQS, LENGTH, D), positions.reshape(SEQS, LENGTH), cotangent.reshape(SEQS, LENGTH, D))
    grads_all, (outputs_all, input_grads) = lax.scan(one_sequence, initial, packets)
    return (outputs_all.reshape(TOKENS, D), input_grads.reshape(TOKENS, D), grads_all[0], grads_all[1], grads_all[2], grads_all[3], grads_all[4], grads_all[5], grads_all[6], grads_all[7], grads_all[8], grads_all[9], grads_all[10], grads_all[11], grads_all[12])
```

```python
import functools
import math

import jax
import jax.numpy as jnp
from jax import lax
from jax.experimental import pallas as pl
from jax.experimental.pallas import tpu as pltpu
from jax.sharding import PartitionSpec as P

D = 1152
H = 4
DH = 256
FF = 6912


EPSILON = 1e-06
THETA = 1000000.0
GELU_COEF = math.sqrt(2.0 / math.pi)


def rms_factor(values):
    return lax.rsqrt(jnp.mean(values * values, axis=-1, keepdims=True) + EPSILON)


def norm_back(values, factor, gain_vector, upstream):
    scaled = gain_vector * upstream
    cubed = factor * factor * factor
    return factor * scaled - values * cubed * jnp.mean(scaled * values, axis=-1, keepdims=True)


def rotary(places):
    half_width = DH // 2
    exponent = jnp.arange(half_width, dtype=jnp.float32) * (-2.0 / DH)
    frequency = jnp.power(jnp.float32(THETA), exponent)
    angles = places.astype(jnp.float32)[:, None] * frequency[None, :]
    return (jnp.cos(angles), jnp.sin(angles))


def rotate(values, cosine, sinus):
    half_width = values.shape[-1] // 2
    first = values[..., :half_width]
    second = values[..., half_width:]
    return jnp.concatenate(
        [first * cosine - second * sinus, second * cosine + first * sinus], axis=-1
    )


def rotate_back(upstream, cosine, sinus):
    half_width = upstream.shape[-1] // 2
    first = upstream[..., :half_width]
    second = upstream[..., half_width:]
    return jnp.concatenate(
        [first * cosine + second * sinus, second * cosine - first * sinus], axis=-1
    )


def gelu_tanh(values):
    inner = GELU_COEF * (values + 0.044715 * values * values * values)
    return 0.5 * values * (1.0 + jnp.tanh(inner))


def gelu_slope(values):
    inner = GELU_COEF * (values + 0.044715 * values * values * values)
    tangent = jnp.tanh(inner)
    return 0.5 * (1.0 + tangent) + 0.5 * values * (1.0 - tangent * tangent) * GELU_COEF * (
        1.0 + 3.0 * 0.044715 * values * values
    )


def times_right(left_side, right_side):
    return jnp.dot(left_side, right_side, preferred_element_type=jnp.float32)


def times_transposed(left_side, right_side):
    return lax.dot_general(
        left_side, right_side, (((1,), (1,)), ((), ())), preferred_element_type=jnp.float32
    )


def transposed_times(left_side, right_side):
    return lax.dot_general(
        left_side, right_side, (((0,), (0,)), ((), ())), preferred_element_type=jnp.float32
    )


BOTH = ("seq", "ctx")
MESH = pl.DeviceIdType.MESH


def peers():
    seq = lax.axis_index("seq")
    ctx = lax.axis_index("ctx")
    return seq, ctx // 2, lax.rem(ctx, 2)


def greet(seq, place, core, chips):
    barrier = pltpu.get_barrier_semaphore()
    pl.semaphore_signal(
        barrier, inc=1, device_id=(seq, place * 2 + 1 - core), device_id_type=MESH
    )
    for k in range(1, chips):
        other = lax.rem(place + k, chips) * 2 + core
        pl.semaphore_signal(barrier, inc=1, device_id=(seq, other), device_id_type=MESH)
    pl.semaphore_wait(barrier, chips)


def send_to(source, target, send_sem, recv_sem, device):
    return pltpu.make_async_remote_copy(
        src_ref=source,
        dst_ref=target,
        send_sem=send_sem,
        recv_sem=recv_sem,
        device_id=device,
        device_id_type=MESH,
    )


def feed_kernel(
    chips,
    fed_ref,
    residual_ref,
    cot_ref,
    gain_ref,
    gate_ref,
    up_ref,
    down_ref,
    block_ref,
    grad_final_ref,
    fed_back_ref,
    hidden_ref,
    gate_back_ref,
    up_back_ref,
    fed_all,
    back_all,
    gate_values,
    up_values,
    part,
    hidden_back,
    own,
    back_own,
    to_sibling,
    from_sibling,
    to_chip,
    from_chip,
    gather_sems,
    forward_sems,
    sibling_sems,
    chip_sems,
):
    seq, place, core = peers()
    sibling = (seq, place * 2 + 1 - core)
    count = fed_ref.shape[0]
    pair_count = 2 * count
    chunk = min(64, pair_count)
    greet(seq, place, core, chips)

    def rows_of(chip, which):
        return pl.ds(pl.multiple_of((chip * 2 + which) * count, count), count)

    def pair_of(chip):
        return pl.ds(pl.multiple_of(chip * pair_count, pair_count), pair_count)

    def phase(index, source, rows_all, work):
        mine = rows_of(place, core)
        rows_all[mine, :] = source[...]

        def gather_copy(k):
            chip = lax.rem(place + k, chips)
            return send_to(
                source,
                rows_all.at[mine],
                gather_sems.at[0, index, k],
                gather_sems.at[1, index, k],
                (seq, chip * 2 + core),
            )

        def forward_copy(k):
            chip = lax.rem(place - k + chips, chips)
            block = rows_all.at[rows_of(chip, core)]
            return send_to(
                block,
                block,
                forward_sems.at[0, index, k],
                forward_sems.at[1, index, k],
                sibling,
            )

        def sibling_copy(k):
            return send_to(
                to_sibling.at[index, k],
                from_sibling.at[index, k],
                sibling_sems.at[0, index, k],
                sibling_sems.at[1, index, k],
                sibling,
            )

        def chip_copy(k):
            chip = lax.rem(place - k + chips, chips)
            return send_to(
                to_chip.at[index, k],
                from_chip.at[index, k],
                chip_sems.at[0, index, k],
                chip_sems.at[1, index, k],
                (seq, chip * 2 + core),
            )

        forward_copy(0).start()
        for k in range(1, chips):
            gather_copy(k).start()

        def step(k, carry):
            chip = lax.rem(place - k + chips, chips)

            @pl.when(k > 0)
            def _():
                gather_copy(k).wait_recv()
                forward_copy(k).start()

            forward_copy(k).wait_recv()
            work(pair_of(chip))
            other_rows = pl.ds(pl.multiple_of((1 - core) * count, count), count)
            own_rows = pl.ds(pl.multiple_of(core * count, count), count)
            to_sibling[index, k] = part[other_rows, :].astype(jnp.bfloat16)
            sibling_copy(k).start()
            sibling_copy(k).wait_recv()
            total = part[own_rows, :] + from_sibling[index, k].astype(jnp.float32)

            @pl.when(k == 0)
            def _():
                own[...] = total

            @pl.when(k > 0)
            def _():
                to_chip[index, k] = total.astype(jnp.bfloat16)
                chip_copy(k).start()

            return carry

        lax.fori_loop(0, chips, step, 0)
        for k in range(1, chips):
            chip_copy(k).wait_recv()
            own[...] += from_chip[index, k].astype(jnp.float32)
        for k in range(chips):
            forward_copy(k).wait_send()
            sibling_copy(k).wait_send()
        for k in range(1, chips):
            gather_copy(k).wait_send()
            chip_copy(k).wait_send()

    def forward_work(rows):
        block = fed_all[rows, :]
        gate_values[rows, :] = times_right(block, gate_ref[...])
        up_values[rows, :] = times_right(block, up_ref[...])

        def gated(j, carry):
            here = pl.ds(pl.multiple_of(rows.start + j * chunk, chunk), chunk)
            hidden_ref[here, :] = (gelu_tanh(gate_values[here, :]) * up_values[here, :]).astype(
                jnp.bfloat16
            )
            return carry

        lax.fori_loop(0, pair_count // chunk, gated, 0)
        part[...] = times_right(hidden_ref[rows, :], down_ref[...])

    def backward_work(rows):
        hidden_back[...] = times_transposed(back_all[rows, :], down_ref[...])

        def gated(j, carry):
            here = pl.ds(pl.multiple_of(rows.start + j * chunk, chunk), chunk)
            local = pl.ds(pl.multiple_of(j * chunk, chunk), chunk)
            gate_now = gate_values[here, :]
            upper = hidden_back[local, :]
            gate_back_ref[here, :] = (upper * up_values[here, :] * gelu_slope(gate_now)).astype(
                jnp.bfloat16
            )
            up_back_ref[here, :] = (upper * gelu_tanh(gate_now)).astype(jnp.bfloat16)
            return carry

        lax.fori_loop(0, pair_count // chunk, gated, 0)
        part[...] = times_transposed(gate_back_ref[rows, :], gate_ref[...])
        part[...] += times_transposed(up_back_ref[rows, :], up_ref[...])

    phase(0, fed_ref, fed_all, forward_work)
    down_values = own[...]
    down_factor = rms_factor(down_values)
    gain_final = gain_ref[...]
    block_ref[...] = (residual_ref[...] + down_values * down_factor * gain_final).astype(
        jnp.bfloat16
    )
    cot_wide = cot_ref[...].astype(jnp.float32)
    grad_final_ref[...] = jnp.sum(cot_wide * down_values * down_factor, axis=0, keepdims=True)
    back_own[...] = norm_back(down_values, down_factor, gain_final, cot_wide).astype(jnp.bfloat16)
    phase(1, back_own, back_all, backward_work)
    fed_back_ref[...] = own[...]


def feed_call(fed, residual, cot, gain, gate, up, down, chips):
    count, width = fed.shape
    total = 2 * chips * count
    units = down.shape[0]
    wide = jnp.float32
    half = jnp.bfloat16
    dma = pltpu.SemaphoreType.DMA
    shape = jax.ShapeDtypeStruct
    vmem = pl.BlockSpec(memory_space=pltpu.VMEM)
    flops = 12 * total * width * units
    return pl.pallas_call(
        functools.partial(feed_kernel, chips),
        out_shape=(
            shape((count, width), half),
            shape((1, width), wide),
            shape((count, width), wide),
            shape((total, units), half),
            shape((total, units), half),
            shape((total, units), half),
            shape((total, width), half),
            shape((total, width), half),
        ),
        in_specs=[vmem] * 7,
        out_specs=(vmem,) * 8,
        scratch_shapes=[
            pltpu.VMEM((total, units), wide),
            pltpu.VMEM((total, units), wide),
            pltpu.VMEM((2 * count, width), wide),
            pltpu.VMEM((2 * count, units), wide),
            pltpu.VMEM((count, width), wide),
            pltpu.VMEM((count, width), half),
            pltpu.VMEM((2, chips, count, width), half),
            pltpu.VMEM((2, chips, count, width), half),
            pltpu.VMEM((2, chips, count, width), half),
            pltpu.VMEM((2, chips, count, width), half),
            dma((2, 2, chips)),
            dma((2, 2, chips)),
            dma((2, 2, chips)),
            dma((2, 2, chips)),
        ],
        compiler_params=pltpu.CompilerParams(
            collective_id=1, has_side_effects=True, vmem_limit_bytes=56 * 2**20
        ),
        cost_estimate=pl.CostEstimate(
            flops=flops, bytes_accessed=8 * total * width * 2, transcendentals=total * units
        ),
        name="feed",
    )(fed, residual, cot, gain, gate, up, down)


def to_heads(rows):
    return jnp.concatenate([rows[:, h * DH : (h + 1) * DH] for h in range(H)], axis=0)


def from_heads(stacked):
    count = stacked.shape[0] // H
    return jnp.concatenate([stacked[h * count : (h + 1) * count] for h in range(H)], axis=1)


def sum_to_owner(term):
    columns = term.shape[1]
    first = lax.psum_scatter(
        term.astype(jnp.bfloat16), "seq", scatter_dimension=0, tiled=True
    )
    ctx_total = lax.axis_size("ctx")
    own = first.shape[0] // ctx_total
    padded = -(-own // 16) * 16
    if padded != own:
        first = first.reshape(ctx_total, own, columns)
        first = jnp.pad(first, ((0, 0), (0, padded - own), (0, 0)))
        first = first.reshape(ctx_total * padded, columns)
    second = lax.psum_scatter(first, "ctx", scatter_dimension=0, tiled=True)
    return second[:own].astype(jnp.float32)


def per_device(
    inputs,
    positions,
    attention_gain,
    query_weight,
    key_weight,
    value_weight,
    query_gain,
    key_gain,
    output_weight,
    attention_post,
    feedfwd_gain,
    gate_weight,
    up_weight,
    down_weight,
    feedfwd_post,
    cotangent,
):
    seq_total = lax.axis_size("seq")
    ctx_total = lax.axis_size("ctx")
    device_total = seq_total * ctx_total
    token_count = inputs.shape[0]
    width_rows = query_weight.shape[0]
    head_rows = query_gain.shape[0]
    unit_rows = down_weight.shape[0]
    scaling = 1.0 / math.sqrt(DH)

    block_number = (positions[:1] // token_count).astype(jnp.bfloat16)
    small = jnp.concatenate(
        [attention_gain, attention_post, feedfwd_gain, feedfwd_post, query_gain, key_gain]
        + [block_number]
    )
    small_row = jnp.pad(small, (0, (H + 2) * DH - small.shape[0]))[None]
    packet = jnp.concatenate(
        [jnp.concatenate([query_weight, key_weight, value_weight], axis=1), small_row], axis=0
    )
    packets = lax.all_gather(packet, BOTH, axis=0, tiled=False)
    joint_weight = packets[:, :width_rows].reshape(D, (H + 2) * DH)
    smalls = packets[:, width_rows]

    def gain_of(start, size):
        return smalls[:, start : start + size].reshape(-1).astype(jnp.float32)

    gain_attention = gain_of(0, width_rows)
    gain_post = gain_of(width_rows, width_rows)
    gain_feed = gain_of(2 * width_rows, width_rows)
    gain_final = gain_of(3 * width_rows, width_rows)
    gain_query = gain_of(4 * width_rows, head_rows)
    gain_key = gain_of(4 * width_rows + head_rows, head_rows)
    numbers = smalls[:, 4 * width_rows + 2 * head_rows].astype(jnp.int32)
    own_numbers = lax.dynamic_slice(numbers, (lax.axis_index("seq") * ctx_total,), (ctx_total,))
    place_all = (
        own_numbers[:, None] * token_count + jnp.arange(token_count, dtype=jnp.int32)[None, :]
    ).reshape(-1)

    pair = jnp.stack([gate_weight, up_weight]).reshape(
        2, width_rows, seq_total, ctx_total, unit_rows
    )
    pair = jnp.transpose(pair, (3, 0, 1, 2, 4)).reshape(
        ctx_total, 2, width_rows, seq_total * unit_rows
    )
    pair = lax.all_to_all(pair, "ctx", 0, 0, tiled=False)
    unit_count = seq_total * unit_rows
    pair = jnp.transpose(pair, (1, 0, 2, 3)).reshape(2 * ctx_total * width_rows, unit_count)

    input_wide = inputs.astype(jnp.float32)
    input_factor = rms_factor(input_wide)
    normed = (input_wide * input_factor * gain_attention).astype(jnp.bfloat16)
    joint = times_right(normed, joint_weight)
    queries = to_heads(joint[:, : H * DH])
    key_rows = joint[:, H * DH : (H + 1) * DH]
    value_rows = joint[:, (H + 1) * DH :].astype(jnp.bfloat16)
    cosine, sinus = rotary(positions)
    cosine_heads = jnp.concatenate([cosine] * H, axis=0)
    sinus_heads = jnp.concatenate([sinus] * H, axis=0)
    query_factor = rms_factor(queries)
    query_rot = rotate(queries * query_factor * gain_query, cosine_heads, sinus_heads).astype(
        jnp.bfloat16
    )
    key_factor = rms_factor(key_rows)
    key_rot = rotate(key_rows * key_factor * gain_key, cosine, sinus).astype(jnp.bfloat16)
    both_rows = lax.all_gather(
        jnp.concatenate([key_rot, value_rows], axis=1), "ctx", axis=0, tiled=True
    )
    output_all = lax.all_gather(output_weight, BOTH, axis=0, tiled=True)
    both_rows, pair, down_own = lax.optimization_barrier((both_rows, pair, down_weight))
    pair_all = lax.all_gather(pair, "seq", axis=0, tiled=True).reshape(
        seq_total, 2, ctx_total * width_rows, unit_count
    )
    gate_all = pair_all[:, 0].reshape(D, unit_count)
    up_all = pair_all[:, 1].reshape(D, unit_count)
    down_all = lax.all_gather(down_own, "seq", axis=0, tiled=True)

    key_all = both_rows[:, :DH]
    value_all = both_rows[:, DH:]
    place_heads = jnp.concatenate([positions] * H, axis=0)
    allowed = place_all[None, :] <= place_heads[:, None]
    scores = times_transposed(query_rot, key_all) * scaling
    expscore = jnp.where(allowed, jnp.exp(scores), 0.0)
    weight_sum = jnp.sum(expscore, axis=-1, keepdims=True)
    summed = times_right(expscore.astype(jnp.bfloat16), value_all)
    attended_heads = (summed / weight_sum).astype(jnp.bfloat16)
    logsum = jnp.log(weight_sum)
    attended = from_heads(attended_heads)
    mixed_values = times_right(attended, output_all)
    mixed_factor = rms_factor(mixed_values)
    residual = input_wide + mixed_values * mixed_factor * gain_post
    residual_factor = rms_factor(residual)
    fed_own = (residual * residual_factor * gain_feed).astype(jnp.bfloat16)

    cot_wide = cotangent.astype(jnp.float32)
    block_out, grad_final, fed_back, late_hidden, late_gate, late_up, late_fed, late_down = feed_call(
        fed_own,
        residual,
        cotangent,
        gain_final[None],
        gate_all,
        up_all,
        down_all,
        ctx_total // 2,
    )
    grad_final = grad_final[0]
    grad_down = lax.psum_scatter(
        transposed_times(late_hidden, late_down).astype(jnp.bfloat16),
        "seq",
        scatter_dimension=0,
        tiled=True,
    ).astype(jnp.float32)
    seq_rows = ctx_total * width_rows
    pair_term = jnp.stack(
        [
            transposed_times(late_fed, late_gate).astype(jnp.bfloat16).reshape(
                seq_total, seq_rows, unit_count
            ),
            transposed_times(late_fed, late_up).astype(jnp.bfloat16).reshape(
                seq_total, seq_rows, unit_count
            ),
        ],
        axis=1,
    ).reshape(seq_total * 2 * seq_rows, unit_count)
    pair_sum = lax.psum_scatter(pair_term, "seq", scatter_dimension=0, tiled=True)

    grad_feed = jnp.sum(fed_back * residual * residual_factor, axis=0)
    residual_back = cot_wide + norm_back(residual, residual_factor, gain_feed, fed_back)
    grad_post = jnp.sum(residual_back * mixed_values * mixed_factor, axis=0)
    mixed_back = norm_back(mixed_values, mixed_factor, gain_post, residual_back).astype(
        jnp.bfloat16
    )
    attended_back = to_heads(times_transposed(mixed_back, output_all))
    upper_round = attended_back.astype(jnp.bfloat16)
    row_delta = jnp.sum(attended_back * attended_heads.astype(jnp.float32), axis=-1, keepdims=True)
    probability = jnp.where(allowed, jnp.exp(scores - logsum), 0.0)
    value_terms = transposed_times(probability.astype(jnp.bfloat16), upper_round)
    prob_back = times_transposed(upper_round, value_all)
    score_back = (probability * (prob_back - row_delta) * scaling).astype(jnp.bfloat16)
    query_rot_back = times_right(score_back, key_all)
    key_terms = transposed_times(score_back, query_rot)
    own_rows = lax.psum_scatter(
        jnp.concatenate([key_terms, value_terms], axis=1).astype(jnp.bfloat16),
        "ctx",
        scatter_dimension=0,
        tiled=True,
    ).astype(jnp.float32)
    grad_output = sum_to_owner(transposed_times(attended, mixed_back))
    key_rot_back = own_rows[:, :DH]
    value_back = own_rows[:, DH:].astype(jnp.bfloat16)
    query_up = rotate_back(query_rot_back, cosine_heads, sinus_heads)
    grad_qgain = jnp.sum(query_up * queries * query_factor, axis=0)
    query_back = from_heads(
        norm_back(queries, query_factor, gain_query, query_up).astype(jnp.bfloat16)
    )
    key_up = rotate_back(key_rot_back, cosine, sinus)
    grad_kgain = jnp.sum(key_up * key_rows * key_factor, axis=0)
    key_back = norm_back(key_rows, key_factor, gain_key, key_up).astype(jnp.bfloat16)
    joint_back = jnp.concatenate([query_back, key_back, value_back], axis=1)
    normed_back = times_transposed(joint_back, joint_weight)
    grad_attention = jnp.sum(normed_back * input_wide * input_factor, axis=0)
    input_grad = residual_back + norm_back(input_wide, input_factor, gain_attention, normed_back)
    grad_joint = sum_to_owner(transposed_times(normed, joint_back))
    grad_query = grad_joint[:, : H * DH]
    grad_key = grad_joint[:, H * DH : (H + 1) * DH]
    grad_value = grad_joint[:, (H + 1) * DH :]
    pair_back = jnp.transpose(
        pair_sum.reshape(2, ctx_total, width_rows, unit_count), (1, 0, 2, 3)
    )
    pair_back = lax.all_to_all(pair_back, "ctx", 0, 0, tiled=False)
    pair_back = jnp.transpose(
        pair_back.reshape(ctx_total, 2, width_rows, seq_total, unit_rows), (1, 2, 3, 0, 4)
    ).reshape(2, width_rows, FF)
    grad_gate = pair_back[0].astype(jnp.float32)
    grad_up = pair_back[1].astype(jnp.float32)
    gains_summed = tuple(
        lax.psum_scatter(term, BOTH, scatter_dimension=0, tiled=True)
        for term in (grad_attention, grad_qgain, grad_kgain, grad_post, grad_feed, grad_final)
    )
    return (
        block_out,
        input_grad,
        gains_summed[0],
        grad_query,
        grad_key,
        grad_value,
        gains_summed[1],
        gains_summed[2],
        grad_output,
        gains_summed[3],
        gains_summed[4],
        grad_gate,
        grad_up,
        grad_down,
        gains_summed[5],
    )


def solution(mesh):
    return jax.shard_map(
        per_device,
        mesh=mesh,
        in_specs=(
            P(("seq", "ctx"), None),
            P(("seq", "ctx")),
            P(("seq", "ctx")),
            P(("seq", "ctx"), None),
            P(("seq", "ctx"), None),
            P(("seq", "ctx"), None),
            P(("seq", "ctx")),
            P(("seq", "ctx")),
            P(("seq", "ctx"), None),
            P(("seq", "ctx")),
            P(("seq", "ctx")),
            P(("seq", "ctx"), None),
            P(("seq", "ctx"), None),
            P(("seq", "ctx"), None),
            P(("seq", "ctx")),
            P(("seq", "ctx"), None),
        ),
        out_specs=(
            P(("seq", "ctx"), None),
            P(("seq", "ctx"), None),
            P(("seq", "ctx")),
            P(("seq", "ctx"), None),
            P(("seq", "ctx"), None),
            P(("seq", "ctx"), None),
            P(("seq", "ctx")),
            P(("seq", "ctx")),
            P(("seq", "ctx"), None),
            P(("seq", "ctx")),
            P(("seq", "ctx")),
            P(("seq", "ctx"), None),
            P(("seq", "ctx"), None),
            P(("seq", "ctx"), None),
            P(("seq", "ctx")),
        ),
        check_vma=False,
    )
```

```python
import functools
import math

import jax
import jax.numpy as jnp
from jax import lax
from jax.experimental import pallas as pl
from jax.experimental.pallas import tpu as pltpu
from jax.sharding import PartitionSpec as P

D = 1152
H = 4
DH = 256
FF = 6912


EPSILON = 1e-06
THETA = 1000000.0
GELU_COEF = math.sqrt(2.0 / math.pi)


def rms_factor(values):
    return lax.rsqrt(jnp.mean(values * values, axis=-1, keepdims=True) + EPSILON)


def norm_back(values, factor, gain_vector, upstream):
    scaled = gain_vector * upstream
    cubed = factor * factor * factor
    return factor * scaled - values * cubed * jnp.mean(scaled * values, axis=-1, keepdims=True)


def rotary(places):
    half_width = DH // 2
    exponent = jnp.arange(half_width, dtype=jnp.float32) * (-2.0 / DH)
    frequency = jnp.power(jnp.float32(THETA), exponent)
    angles = places.astype(jnp.float32)[:, None] * frequency[None, :]
    return (jnp.cos(angles), jnp.sin(angles))


def rotate(values, cosine, sinus):
    half_width = values.shape[-1] // 2
    first = values[..., :half_width]
    second = values[..., half_width:]
    return jnp.concatenate(
        [first * cosine - second * sinus, second * cosine + first * sinus], axis=-1
    )


def rotate_back(upstream, cosine, sinus):
    half_width = upstream.shape[-1] // 2
    first = upstream[..., :half_width]
    second = upstream[..., half_width:]
    return jnp.concatenate(
        [first * cosine + second * sinus, second * cosine - first * sinus], axis=-1
    )


def gelu_tanh(values):
    inner = GELU_COEF * (values + 0.044715 * values * values * values)
    return 0.5 * values * (1.0 + jnp.tanh(inner))


def gelu_slope(values):
    inner = GELU_COEF * (values + 0.044715 * values * values * values)
    tangent = jnp.tanh(inner)
    return 0.5 * (1.0 + tangent) + 0.5 * values * (1.0 - tangent * tangent) * GELU_COEF * (
        1.0 + 3.0 * 0.044715 * values * values
    )


def times_right(left_side, right_side):
    return jnp.dot(left_side, right_side, preferred_element_type=jnp.float32)


def times_transposed(left_side, right_side):
    return lax.dot_general(
        left_side, right_side, (((1,), (1,)), ((), ())), preferred_element_type=jnp.float32
    )


def transposed_times(left_side, right_side):
    return lax.dot_general(
        left_side, right_side, (((0,), (0,)), ((), ())), preferred_element_type=jnp.float32
    )


BOTH = ("seq", "ctx")
MESH = pl.DeviceIdType.MESH


def peers():
    seq = lax.axis_index("seq")
    ctx = lax.axis_index("ctx")
    return seq, ctx // 2, lax.rem(ctx, 2)


def greet(seq, place, core, chips):
    barrier = pltpu.get_barrier_semaphore()
    pl.semaphore_signal(
        barrier, inc=1, device_id=(seq, place * 2 + 1 - core), device_id_type=MESH
    )
    for k in range(1, chips):
        other = lax.rem(place + k, chips) * 2 + core
        pl.semaphore_signal(barrier, inc=1, device_id=(seq, other), device_id_type=MESH)
    pl.semaphore_wait(barrier, chips)


def send_to(source, target, send_sem, recv_sem, device):
    return pltpu.make_async_remote_copy(
        src_ref=source,
        dst_ref=target,
        send_sem=send_sem,
        recv_sem=recv_sem,
        device_id=device,
        device_id_type=MESH,
    )


def feed_kernel(
    chips,
    fed_ref,
    residual_ref,
    cot_ref,
    gain_ref,
    gate_ref,
    up_ref,
    down_ref,
    block_ref,
    grad_final_ref,
    fed_back_ref,
    grad_down_ref,
    grad_pair_ref,
    hidden_ref,
    gate_back_ref,
    up_back_ref,
    fed_all,
    back_all,
    gate_values,
    up_values,
    part,
    hidden_back,
    own,
    back_own,
    grad_part,
    to_sibling,
    from_sibling,
    to_chip,
    from_chip,
    gather_sems,
    forward_sems,
    sibling_sems,
    chip_sems,
):
    seq, place, core = peers()
    sibling = (seq, place * 2 + 1 - core)
    count = fed_ref.shape[0]
    pair_count = 2 * count
    chunk = min(64, pair_count)
    greet(seq, place, core, chips)

    def rows_of(chip, which):
        return pl.ds(pl.multiple_of((chip * 2 + which) * count, count), count)

    def pair_of(chip):
        return pl.ds(pl.multiple_of(chip * pair_count, pair_count), pair_count)

    def phase(index, source, rows_all, work, later):
        mine = rows_of(place, core)
        rows_all[mine, :] = source[...]

        def gather_copy(k):
            chip = lax.rem(place + k, chips)
            return send_to(
                source,
                rows_all.at[mine],
                gather_sems.at[0, index, k],
                gather_sems.at[1, index, k],
                (seq, chip * 2 + core),
            )

        def forward_copy(k):
            chip = lax.rem(place - k + chips, chips)
            block = rows_all.at[rows_of(chip, core)]
            return send_to(
                block,
                block,
                forward_sems.at[0, index, k],
                forward_sems.at[1, index, k],
                sibling,
            )

        def sibling_copy(k):
            return send_to(
                to_sibling.at[k],
                from_sibling.at[index, k],
                sibling_sems.at[0, index, k],
                sibling_sems.at[1, index, k],
                sibling,
            )

        def chip_copy(k):
            chip = lax.rem(place - k + chips, chips)
            return send_to(
                to_chip.at[k],
                from_chip.at[index, k],
                chip_sems.at[0, index, k],
                chip_sems.at[1, index, k],
                (seq, chip * 2 + core),
            )

        forward_copy(0).start()
        for k in range(1, chips):
            gather_copy(k).start()

        def step(k, carry):
            chip = lax.rem(place - k + chips, chips)

            @pl.when(k > 0)
            def _():
                gather_copy(k).wait_recv()
                forward_copy(k).start()

            forward_copy(k).wait_recv()
            work(pair_of(chip))
            other_rows = pl.ds(pl.multiple_of((1 - core) * count, count), count)
            own_rows = pl.ds(pl.multiple_of(core * count, count), count)
            to_sibling[k] = part[other_rows, :].astype(jnp.bfloat16)
            sibling_copy(k).start()
            sibling_copy(k).wait_recv()
            total = part[own_rows, :] + from_sibling[index, k].astype(jnp.float32)

            @pl.when(k == 0)
            def _():
                own[...] = total

            @pl.when(k > 0)
            def _():
                to_chip[k] = total.astype(jnp.bfloat16)
                chip_copy(k).start()

            return carry

        lax.fori_loop(0, chips, step, 0)
        later()
        for k in range(1, chips):
            chip_copy(k).wait_recv()
            own[...] += from_chip[index, k].astype(jnp.float32)
        for k in range(chips):
            forward_copy(k).wait_send()
            sibling_copy(k).wait_send()
        for k in range(1, chips):
            gather_copy(k).wait_send()
            chip_copy(k).wait_send()

    def forward_work(rows):
        block = fed_all[rows, :]
        gate_values[rows, :] = times_right(block, gate_ref[...])
        up_values[rows, :] = times_right(block, up_ref[...])

        def gated(j, carry):
            here = pl.ds(pl.multiple_of(rows.start + j * chunk, chunk), chunk)
            hidden_ref[here, :] = (gelu_tanh(gate_values[here, :]) * up_values[here, :]).astype(
                jnp.bfloat16
            )
            return carry

        lax.fori_loop(0, pair_count // chunk, gated, 0)
        part[...] = times_right(hidden_ref[rows, :], down_ref[...])

    def backward_work(rows):
        hidden_back[...] = times_transposed(back_all[rows, :], down_ref[...])

        def gated(j, carry):
            here = pl.ds(pl.multiple_of(rows.start + j * chunk, chunk), chunk)
            local = pl.ds(pl.multiple_of(j * chunk, chunk), chunk)
            gate_now = gate_values[here, :]
            upper = hidden_back[local, :]
            gate_back_ref[here, :] = (upper * up_values[here, :] * gelu_slope(gate_now)).astype(
                jnp.bfloat16
            )
            up_back_ref[here, :] = (upper * gelu_tanh(gate_now)).astype(jnp.bfloat16)
            return carry

        lax.fori_loop(0, pair_count // chunk, gated, 0)
        part[...] = times_transposed(gate_back_ref[rows, :], gate_ref[...])
        part[...] += times_transposed(up_back_ref[rows, :], up_ref[...])

    def weight_terms():
        grad_down_ref[...] = transposed_times(hidden_ref[...], back_all[...]).astype(jnp.bfloat16)
        slabs = grad_pair_ref.shape[0]
        slab_rows = grad_pair_ref.shape[2]
        for b, source in ((0, gate_back_ref), (1, up_back_ref)):
            grad_part[...] = transposed_times(fed_all[...], source[...])
            for s in range(slabs):
                grad_pair_ref[s, b] = grad_part[s * slab_rows : (s + 1) * slab_rows, :].astype(
                    jnp.bfloat16
                )

    phase(0, fed_ref, fed_all, forward_work, lambda: None)
    down_values = own[...]
    down_factor = rms_factor(down_values)
    gain_final = gain_ref[...]
    block_ref[...] = (residual_ref[...] + down_values * down_factor * gain_final).astype(
        jnp.bfloat16
    )
    cot_wide = cot_ref[...].astype(jnp.float32)
    grad_final_ref[...] = jnp.sum(cot_wide * down_values * down_factor, axis=0, keepdims=True)
    back_own[...] = norm_back(down_values, down_factor, gain_final, cot_wide).astype(jnp.bfloat16)
    phase(1, back_own, back_all, backward_work, weight_terms)
    fed_back_ref[...] = own[...]


def feed_call(fed, residual, cot, gain, gate, up, down, seqs, chips):
    count, width = fed.shape
    total = 2 * chips * count
    units = down.shape[0]
    wide = jnp.float32
    half = jnp.bfloat16
    dma = pltpu.SemaphoreType.DMA
    shape = jax.ShapeDtypeStruct
    vmem = pl.BlockSpec(memory_space=pltpu.VMEM)
    flops = 18 * total * width * units
    return pl.pallas_call(
        functools.partial(feed_kernel, chips),
        out_shape=(
            shape((count, width), half),
            shape((1, width), wide),
            shape((count, width), wide),
            shape((units, width), half),
            shape((seqs, 2, width // seqs, units), half),
        ),
        in_specs=[vmem] * 7,
        out_specs=(vmem,) * 5,
        scratch_shapes=[
            pltpu.VMEM((total, units), half),
            pltpu.VMEM((total, units), half),
            pltpu.VMEM((total, units), half),
            pltpu.VMEM((total, width), half),
            pltpu.VMEM((total, width), half),
            pltpu.VMEM((total, units), wide),
            pltpu.VMEM((total, units), wide),
            pltpu.VMEM((2 * count, width), wide),
            pltpu.VMEM((2 * count, units), wide),
            pltpu.VMEM((count, width), wide),
            pltpu.VMEM((count, width), half),
            pltpu.VMEM((width, units), wide),
            pltpu.VMEM((chips, count, width), half),
            pltpu.VMEM((2, chips, count, width), half),
            pltpu.VMEM((chips, count, width), half),
            pltpu.VMEM((2, chips, count, width), half),
            dma((2, 2, chips)),
            dma((2, 2, chips)),
            dma((2, 2, chips)),
            dma((2, 2, chips)),
        ],
        compiler_params=pltpu.CompilerParams(
            collective_id=1, has_side_effects=True, vmem_limit_bytes=56 * 2**20
        ),
        cost_estimate=pl.CostEstimate(
            flops=flops, bytes_accessed=8 * total * width * 2, transcendentals=total * units
        ),
        name="feed",
    )(fed, residual, cot, gain, gate, up, down)


def start_kernel(
    seqs,
    chips,
    packet_ref,
    output_ref,
    gate_ref,
    up_ref,
    packets,
    outputs,
    pair_ref,
    to_ctx,
    from_ctx,
    joined,
    packed,
    line_sems,
    plane_sems,
    core_sems,
    swap_sems,
):
    seq, place, core = peers()
    ctx = place * 2 + core
    sibling = (seq, place * 2 + 1 - core)
    ctxs = 2 * chips
    barrier = pltpu.get_barrier_semaphore()
    for k in range(1, ctxs):
        pl.semaphore_signal(
            barrier, inc=1, device_id=(seq, lax.rem(ctx + k, ctxs)), device_id_type=MESH
        )
    for j in range(1, seqs):
        pl.semaphore_signal(
            barrier, inc=1, device_id=(lax.rem(seq + j, seqs), ctx), device_id_type=MESH
        )
    pl.semaphore_wait(barrier, ctxs + seqs - 2)

    def index_of(row, chip, which):
        return row * ctxs + chip * 2 + which

    both = ((0, packet_ref, packets), (1, output_ref, outputs))

    def line_copy(b, k):
        _, own, everything = both[b]
        chip = lax.rem(place + k, chips)
        return send_to(
            own,
            everything.at[index_of(seq, place, core)],
            line_sems.at[0, b, k],
            line_sems.at[1, b, k],
            (seq, chip * 2 + core),
        )

    def plane_copy(b, j, k):
        everything = both[b][2]
        chip = lax.rem(place - k + chips, chips)
        block = everything.at[index_of(seq, chip, core)]
        return send_to(
            block,
            block,
            plane_sems.at[0, b, j, k],
            plane_sems.at[1, b, j, k],
            (lax.rem(seq + j, seqs), ctx),
        )

    def core_copy(b, j, k):
        everything = both[b][2]
        row = lax.rem(seq - j + seqs, seqs)
        chip = lax.rem(place - k + chips, chips)
        block = everything.at[index_of(row, chip, core)]
        return send_to(
            block, block, core_sems.at[0, b, j, k], core_sems.at[1, b, j, k], sibling
        )

    def swap_copy(k):
        target = lax.rem(ctx + k, ctxs)
        return send_to(
            to_ctx.at[target],
            from_ctx.at[ctx],
            swap_sems.at[0, k],
            swap_sems.at[1, k],
            (seq, target),
        )

    for b in range(2):
        _, own, everything = both[b]
        for k in range(1, chips):
            line_copy(b, k).start()
        everything[index_of(seq, place, core)] = own[...]
    for b in range(2):
        for j in range(1, seqs):
            plane_copy(b, j, 0).start()
        core_copy(b, 0, 0).start()

    rows = gate_ref.shape[0]
    units = gate_ref.shape[1] // (seqs * ctxs)
    for c in range(ctxs):
        for b, source in ((0, gate_ref), (1, up_ref)):
            for s in range(seqs):
                first = (s * ctxs + c) * units
                low = first // 128 * 128
                high = min(-(-(first + units) // 128) * 128, gate_ref.shape[1])
                wide = source[:, low:high].astype(jnp.float32)
                joined[b * rows : (b + 1) * rows, s * units : (s + 1) * units] = wide[
                    :, first - low : first - low + units
                ]
        to_ctx[c] = joined[...].astype(jnp.bfloat16)
    for k in range(1, ctxs):
        swap_copy(k).start()
    from_ctx[ctx] = to_ctx[ctx]

    def line_step(k, carry):
        for b in range(2):
            line_copy(b, k).wait_recv()
            for j in range(1, seqs):
                plane_copy(b, j, k).start()
            core_copy(b, 0, k).start()
        return carry

    lax.fori_loop(1, chips, line_step, 0)

    def plane_step(k, carry):
        for j in range(1, seqs):
            for b in range(2):
                plane_copy(b, j, k).wait_recv()
                core_copy(b, j, k).start()
        return carry

    lax.fori_loop(0, chips, plane_step, 0)

    for k in range(1, ctxs):
        swap_copy(k).wait_recv()
    for c in range(ctxs):
        joined[...] = from_ctx[c].astype(jnp.float32)
        for b in range(2):
            packed[b, c * rows : (c + 1) * rows, :] = joined[b * rows : (b + 1) * rows, :]
    pair_ref[...] = packed[...].astype(jnp.bfloat16)

    def core_step(k, carry):
        for j in range(seqs):
            for b in range(2):
                core_copy(b, j, k).wait()
                if j > 0:
                    plane_copy(b, j, k).wait_send()
        return carry

    lax.fori_loop(0, chips, core_step, 0)
    for k in range(1, chips):
        for b in range(2):
            line_copy(b, k).wait_send()
    for k in range(1, ctxs):
        swap_copy(k).wait_send()


def start_call(packet, output, gate, up, seqs, chips):
    half = jnp.bfloat16
    dma = pltpu.SemaphoreType.DMA
    shape = jax.ShapeDtypeStruct
    vmem = pl.BlockSpec(memory_space=pltpu.VMEM)
    ctxs = 2 * chips
    total = seqs * ctxs
    rows = gate.shape[0]
    unit_count = gate.shape[1] // ctxs
    padded = -(-2 * rows // 16) * 16
    return pl.pallas_call(
        functools.partial(start_kernel, seqs, chips),
        out_shape=(
            shape((total,) + packet.shape, half),
            shape((total,) + output.shape, half),
            shape((2, ctxs * rows, unit_count), half),
        ),
        in_specs=[vmem] * 4,
        out_specs=(vmem,) * 3,
        scratch_shapes=[
            pltpu.VMEM((ctxs, padded, unit_count), half),
            pltpu.VMEM((ctxs, padded, unit_count), half),
            pltpu.VMEM((padded, unit_count), jnp.float32),
            pltpu.VMEM((2, ctxs * rows, unit_count), jnp.float32),
            dma((2, 2, chips)),
            dma((2, 2, seqs, chips)),
            dma((2, 2, seqs, chips)),
            dma((2, ctxs)),
        ],
        compiler_params=pltpu.CompilerParams(
            collective_id=2, has_side_effects=True, vmem_limit_bytes=56 * 2**20
        ),
        cost_estimate=pl.CostEstimate(flops=0, bytes_accessed=60 * 2**20, transcendentals=0),
        name="start",
    )(packet, output, gate, up)


def attend_kernel(
    chips,
    blocks,
    inputs_ref,
    joint_ref,
    output_ref,
    gain_attention_ref,
    gain_query_ref,
    gain_key_ref,
    gain_post_ref,
    gain_feed_ref,
    cosine_ref,
    sinus_ref,
    place_ref,
    places_ref,
    spread_ref,
    queries_ref,
    key_rows_ref,
    query_rot_ref,
    both_ref,
    attended_ref,
    logsum_ref,
    mixed_ref,
    residual_ref,
    fed_ref,
    own,
    spread,
    gather_sems,
    forward_sems,
):
    seq, place, core = peers()
    sibling = (seq, place * 2 + 1 - core)
    count = inputs_ref.shape[0]
    greet(seq, place, core, chips)

    def rows_of(chip):
        return pl.ds(pl.multiple_of((chip * 2 + core) * count, count), count)

    def gather_copy(k):
        chip = lax.rem(place + k, chips)
        return send_to(
            own,
            both_ref.at[rows_of(place)],
            gather_sems.at[0, k],
            gather_sems.at[1, k],
            (seq, chip * 2 + core),
        )

    def forward_copy(k):
        chip = lax.rem(place - k + chips, chips)
        block = both_ref.at[rows_of(chip)]
        return send_to(block, block, forward_sems.at[0, k], forward_sems.at[1, k], sibling)

    input_wide = inputs_ref[...].astype(jnp.float32)
    normed = (input_wide * rms_factor(input_wide) * gain_attention_ref[...]).astype(jnp.bfloat16)
    cosine = cosine_ref[...]
    sinus = sinus_ref[...]
    pair = times_right(normed, joint_ref[:, H * DH :])
    key_rows = pair[:, :DH]
    key_rows_ref[...] = key_rows
    key_rot = rotate(key_rows * rms_factor(key_rows) * gain_key_ref[...], cosine, sinus)
    own[:, :DH] = key_rot.astype(jnp.bfloat16)
    own[:, DH:] = pair[:, DH:].astype(jnp.bfloat16)
    both_ref[rows_of(place), :] = own[...]
    for k in range(1, chips):
        gather_copy(k).start()
    forward_copy(0).start()
    for h in range(H):
        rows = slice(h * count, (h + 1) * count)
        queries = times_right(normed, joint_ref[:, h * DH : (h + 1) * DH])
        queries_ref[rows, :] = queries
        query_rot_ref[rows, :] = rotate(
            queries * rms_factor(queries) * gain_query_ref[...], cosine, sinus
        ).astype(jnp.bfloat16)
    spread[...] = jnp.zeros_like(spread)
    normed_wide = normed.astype(jnp.float32)
    for i in range(blocks):
        part = normed_wide.shape[1] // blocks
        step = spread_ref.shape[1] // blocks
        spread[:, i * step : i * step + part] = normed_wide[:, i * part : (i + 1) * part]
    spread_ref[...] = spread[...].astype(jnp.bfloat16)
    for k in range(1, chips):
        gather_copy(k).wait_recv()
        forward_copy(k).start()
    for k in range(chips):
        forward_copy(k).wait_recv()
    scaling = 1.0 / math.sqrt(DH)

    def head(h, carry):
        rows = pl.ds(pl.multiple_of(h * count, count), count)
        columns = pl.ds(pl.multiple_of(h * DH, DH), DH)
        allowed = places_ref[...] <= place_ref[...]
        scores = times_transposed(query_rot_ref[rows, :], both_ref[:, :DH]) * scaling
        expscore = jnp.where(allowed, jnp.exp(scores), 0.0)
        weight_sum = jnp.sum(expscore, axis=-1, keepdims=True)
        summed = times_right(expscore.astype(jnp.bfloat16), both_ref[:, DH:])
        attended_ref[:, columns] = (summed / weight_sum).astype(jnp.bfloat16)
        logsum_ref[rows, :] = jnp.log(weight_sum)
        return carry

    lax.fori_loop(0, H, head, 0)
    mixed_ref[...] = times_right(attended_ref[...], output_ref[...])
    mixed = mixed_ref[...]
    residual = input_wide + mixed * rms_factor(mixed) * gain_post_ref[...]
    residual_ref[...] = residual
    fed_ref[...] = (residual * rms_factor(residual) * gain_feed_ref[...]).astype(jnp.bfloat16)
    for k in range(chips):
        forward_copy(k).wait_send()
    for k in range(1, chips):
        gather_copy(k).wait_send()


def attend_call(chips, blocks, padded_rows, inputs, *rest):
    count, width = inputs.shape
    total = 2 * chips * count
    wide = jnp.float32
    half = jnp.bfloat16
    dma = pltpu.SemaphoreType.DMA
    shape = jax.ShapeDtypeStruct
    vmem = pl.BlockSpec(memory_space=pltpu.VMEM)
    return pl.pallas_call(
        functools.partial(attend_kernel, chips, blocks),
        out_shape=(
            shape((count, blocks * padded_rows), half),
            shape((H * count, DH), wide),
            shape((count, DH), wide),
            shape((H * count, DH), half),
            shape((total, 2 * DH), half),
            shape((count, H * DH), half),
            shape((H * count, 1), wide),
            shape((count, width), wide),
            shape((count, width), wide),
            shape((count, width), half),
        ),
        in_specs=[vmem] * 12,
        out_specs=(vmem,) * 10,
        scratch_shapes=[
            pltpu.VMEM((count, 2 * DH), half),
            pltpu.VMEM((count, blocks * padded_rows), wide),
            dma((2, chips)),
            dma((2, chips)),
        ],
        compiler_params=pltpu.CompilerParams(
            collective_id=3, has_side_effects=True, vmem_limit_bytes=56 * 2**20
        ),
        cost_estimate=pl.CostEstimate(
            flops=2 * count * width * (H + 2) * DH * 2,
            bytes_accessed=60 * 2**20,
            transcendentals=H * count * total,
        ),
        name="attend",
    )(inputs, *rest)


def back_kernel(
    seqs,
    chips,
    fed_back_ref,
    residual_ref,
    mixed_ref,
    cot_ref,
    inputs_ref,
    spread_ref,
    queries_ref,
    key_rows_ref,
    query_rot_ref,
    both_ref,
    attended_ref,
    logsum_ref,
    output_ref,
    joint_ref,
    grad_final_ref,
    gain_attention_ref,
    gain_query_ref,
    gain_key_ref,
    gain_post_ref,
    gain_feed_ref,
    cosine_ref,
    sinus_ref,
    place_ref,
    places_ref,
    input_grad_ref,
    grad_output_ref,
    grad_query_ref,
    grad_pair_ref,
    gains_ref,
    mixed_back,
    attended_back,
    upper_round,
    probs,
    score_back,
    query_up,
    pair_part,
    pair_to_sibling,
    pair_from_sibling,
    pair_to_chip,
    pair_from_chip,
    joint_back,
    gain_term,
    gain_near,
    gain_chip,
    gain_plane,
    gain_row,
    gain_line,
    *rest,
):
    seq, place, core = peers()
    ctx = place * 2 + core
    ctxs = 2 * chips
    sibling = (seq, place * 2 + 1 - core)
    count = cot_ref.shape[0]
    buffers = [rest[7 * b : 7 * b + 7] for b in range(3)]
    (
        pair_sibling_sems,
        pair_chip_sems,
        gain_near_sems,
        gain_plane_sems,
        gain_line_sems,
        near_sems,
        plane_sems,
        line_sems,
    ) = rest[21:]
    barrier = pltpu.get_barrier_semaphore()
    pl.semaphore_signal(barrier, inc=1, device_id=sibling, device_id_type=MESH)
    for k in range(1, chips):
        pl.semaphore_signal(
            barrier,
            inc=1,
            device_id=(seq, lax.rem(place + k, chips) * 2 + core),
            device_id_type=MESH,
        )
    for j in range(1, seqs):
        pl.semaphore_signal(
            barrier, inc=1, device_id=(lax.rem(seq + j, seqs), ctx), device_id_type=MESH
        )
    pl.semaphore_wait(barrier, chips + seqs - 1)

    def block_of(j, k, which):
        row = lax.rem(seq + j, seqs)
        chip = lax.rem(place + k, chips)
        return row * ctxs + chip * 2 + which

    def near_copy(b, j, k):
        term, near = buffers[b][:2]
        return send_to(
            term.at[block_of(j, k, 1 - core)],
            near.at[j, k],
            near_sems.at[0, b, j, k],
            near_sems.at[1, b, j, k],
            sibling,
        )

    def plane_copy(b, j, k):
        plane_to, plane_from = buffers[b][2:4]
        return send_to(
            plane_to.at[j, k],
            plane_from.at[j, k],
            plane_sems.at[0, b, j, k],
            plane_sems.at[1, b, j, k],
            (lax.rem(seq + j, seqs), ctx),
        )

    def line_copy(b, k):
        line_to, line_from = buffers[b][4:6]
        return send_to(
            line_to.at[k],
            line_from.at[k],
            line_sems.at[0, b, k],
            line_sems.at[1, b, k],
            (seq, lax.rem(place + k, chips) * 2 + core),
        )

    def start_near(b):
        def one(k, carry):
            for j in range(seqs):
                near_copy(b, j, lax.rem(k + 1, chips)).start()
            return carry

        lax.fori_loop(0, chips, one, 0)

    def run_plane(b):
        term, near, plane_to = buffers[b][:3]

        def one(i, carry):
            k = lax.rem(i + 1, chips)
            for j in list(range(1, seqs)) + [0]:
                near_copy(b, j, k).wait_recv()
                plane_to[j, k] = (
                    term[block_of(j, k, core)].astype(jnp.float32)
                    + near[j, k].astype(jnp.float32)
                ).astype(jnp.bfloat16)
                if j > 0:
                    plane_copy(b, j, k).start()
            return carry

        lax.fori_loop(0, chips, one, 0)

    def run_line(b):
        _, _, plane_to, plane_from, line_to, _, own = buffers[b]

        def one(i, carry):
            k = lax.rem(i + 1, chips)
            total = plane_to[0, k].astype(jnp.float32)
            for j in range(1, seqs):
                plane_copy(b, j, k).wait_recv()
                total = total + plane_from[j, k].astype(jnp.float32)

            @pl.when(k > 0)
            def _():
                line_to[k] = total.astype(jnp.bfloat16)
                line_copy(b, k).start()

            @pl.when(k == 0)
            def _():
                own[...] = total

            return carry

        lax.fori_loop(0, chips, one, 0)

    def finish(b, target):
        _, _, _, _, _, line_from, own = buffers[b]
        total = own[...]
        for k in range(1, chips):
            line_copy(b, k).wait_recv()
            total = total + line_from[k].astype(jnp.float32)
        target[...] = total

    def drain(b):
        def one(k, carry):
            for j in range(seqs):
                near_copy(b, j, k).wait_send()
                if j > 0:
                    plane_copy(b, j, k).wait_send()
            return carry

        lax.fori_loop(0, chips, one, 0)
        for k in range(1, chips):
            line_copy(b, k).wait_send()

    def pair_rows(chip, which):
        return pl.ds(pl.multiple_of((chip * 2 + which) * count, count), count)

    def pair_sibling_copy(k):
        return send_to(
            pair_to_sibling.at[k],
            pair_from_sibling.at[k],
            pair_sibling_sems.at[0, k],
            pair_sibling_sems.at[1, k],
            sibling,
        )

    def pair_chip_copy(k):
        return send_to(
            pair_to_chip.at[k],
            pair_from_chip.at[k],
            pair_chip_sems.at[0, k],
            pair_chip_sems.at[1, k],
            (seq, lax.rem(place + k, chips) * 2 + core),
        )

    scaling = 1.0 / math.sqrt(DH)
    cosine = cosine_ref[...]
    sinus = sinus_ref[...]
    residual = residual_ref[...]
    residual_factor = rms_factor(residual)
    fed_back = fed_back_ref[...]
    gain_term[...] = jnp.zeros_like(gain_term)
    gain_term[3:4, :] = grad_final_ref[...]
    gain_term[2:3, :] = jnp.sum(fed_back * residual * residual_factor, axis=0, keepdims=True)
    residual_back = cot_ref[...].astype(jnp.float32) + norm_back(
        residual, residual_factor, gain_feed_ref[...], fed_back
    )
    input_grad_ref[...] = residual_back
    mixed = mixed_ref[...]
    mixed_factor = rms_factor(mixed)
    gain_term[1:2, :] = jnp.sum(residual_back * mixed * mixed_factor, axis=0, keepdims=True)
    mixed_back[...] = norm_back(mixed, mixed_factor, gain_post_ref[...], residual_back).astype(
        jnp.bfloat16
    )
    output_term = buffers[0][0]
    output_rows = output_term.shape[1]
    for h in range(H):
        columns = slice(h * DH, (h + 1) * DH)
        part = transposed_times(attended_ref[:, columns], mixed_back[...])
        each = DH // output_rows
        for i in range(each):
            output_term[h * each + i] = part[i * output_rows : (i + 1) * output_rows].astype(
                jnp.bfloat16
            )
    start_near(0)
    attended_back[...] = times_transposed(mixed_back[...], output_ref[...])

    def head(h, carry):
        rows = pl.ds(pl.multiple_of(h * count, count), count)
        columns = pl.ds(pl.multiple_of(h * DH, DH), DH)
        upper = attended_back[:, columns]
        upper_round[rows, :] = upper.astype(jnp.bfloat16)
        row_delta = jnp.sum(
            upper * attended_ref[:, columns].astype(jnp.float32), axis=-1, keepdims=True
        )
        allowed = places_ref[...] <= place_ref[...]
        scores = times_transposed(query_rot_ref[rows, :], both_ref[:, :DH]) * scaling
        probability = jnp.where(allowed, jnp.exp(scores - logsum_ref[rows, :]), 0.0)
        probs[rows, :] = probability.astype(jnp.bfloat16)
        prob_back = times_transposed(upper_round[rows, :], both_ref[:, DH:])
        score_back[rows, :] = (probability * (prob_back - row_delta) * scaling).astype(
            jnp.bfloat16
        )
        return carry

    lax.fori_loop(0, H, head, 0)
    pair_part[:, :DH] = transposed_times(score_back[...], query_rot_ref[...])
    pair_part[:, DH:] = transposed_times(probs[...], upper_round[...])
    for i in range(chips):
        k = (i + 1) % chips
        chip = lax.rem(place + k, chips)
        pair_to_sibling[k] = pair_part[pair_rows(chip, 1 - core), :].astype(jnp.bfloat16)
        pair_sibling_copy(k).start()
    run_plane(0)
    for i in range(chips - 1):
        k = i + 1
        chip = lax.rem(place + k, chips)
        pair_sibling_copy(k).wait_recv()
        pair_to_chip[k] = (
            pair_part[pair_rows(chip, core), :] + pair_from_sibling[k].astype(jnp.float32)
        ).astype(jnp.bfloat16)
        pair_chip_copy(k).start()

    gain_query = gain_query_ref[...]
    grad_query_gain = jnp.zeros((1, DH), jnp.float32)
    for h in range(H):
        rows = slice(h * count, (h + 1) * count)
        upward = rotate_back(times_right(score_back[rows, :], both_ref[:, :DH]), cosine, sinus)
        queries = queries_ref[rows, :]
        factor = rms_factor(queries)
        grad_query_gain += jnp.sum(upward * queries * factor, axis=0, keepdims=True)
        joint_back[:, h * DH : (h + 1) * DH] = norm_back(
            queries, factor, gain_query, upward
        ).astype(jnp.bfloat16)
    gain_term[4:5, :DH] = grad_query_gain

    def joint_term(b, columns):
        term = buffers[b][0]
        blocks, rows, _ = term.shape
        group = 256 // rows if 256 % rows == 0 else 8
        while blocks % group:
            group -= 1
        wide = group * rows
        for g in range(blocks // group):
            part = transposed_times(
                spread_ref[:, g * wide : (g + 1) * wide], joint_back[:, columns]
            )
            for i in range(group):
                term[g * group + i] = part[i * rows : (i + 1) * rows].astype(jnp.bfloat16)

    joint_term(1, slice(0, H * DH))
    start_near(1)
    run_line(0)

    pair_sibling_copy(0).wait_recv()
    own_pair = pair_part[pair_rows(place, core), :] + pair_from_sibling[0].astype(jnp.float32)
    for k in range(1, chips):
        pair_chip_copy(k).wait_recv()
        own_pair = own_pair + pair_from_chip[k].astype(jnp.float32)
    key_up = rotate_back(own_pair[:, :DH], cosine, sinus)
    key_rows = key_rows_ref[...]
    key_factor = rms_factor(key_rows)
    gain_term[4:5, DH : 2 * DH] = jnp.sum(key_up * key_rows * key_factor, axis=0, keepdims=True)
    joint_back[:, H * DH : (H + 1) * DH] = norm_back(
        key_rows, key_factor, gain_key_ref[...], key_up
    ).astype(jnp.bfloat16)
    joint_back[:, (H + 1) * DH :] = own_pair[:, DH:].astype(jnp.bfloat16)
    joint_term(2, slice(H * DH, (H + 2) * DH))
    start_near(2)
    run_plane(1)

    query_up[...] = times_transposed(joint_back[...], joint_ref[...])
    normed_back = query_up[...]
    input_wide = inputs_ref[...].astype(jnp.float32)
    input_factor = rms_factor(input_wide)
    gain_term[0:1, :] = jnp.sum(normed_back * input_wide * input_factor, axis=0, keepdims=True)

    def gain_near_copy():
        return send_to(gain_term, gain_near, gain_near_sems.at[0], gain_near_sems.at[1], sibling)

    def gain_plane_copy(j):
        return send_to(
            gain_chip,
            gain_plane.at[j],
            gain_plane_sems.at[0, j],
            gain_plane_sems.at[1, j],
            (lax.rem(seq + j, seqs), ctx),
        )

    def gain_line_copy(k):
        return send_to(
            gain_row,
            gain_line.at[k],
            gain_line_sems.at[0, k],
            gain_line_sems.at[1, k],
            (seq, lax.rem(place + k, chips) * 2 + core),
        )

    gain_near_copy().start()
    run_plane(2)
    gain_near_copy().wait_recv()
    gain_chip[...] = gain_term[...] + gain_near[...]
    for j in range(1, seqs):
        gain_plane_copy(j).start()
    input_grad_ref[...] += norm_back(input_wide, input_factor, gain_attention_ref[...], normed_back)
    run_line(1)
    run_line(2)
    total = gain_chip[...]
    for j in range(1, seqs):
        gain_plane_copy(j).wait_recv()
        total = total + gain_plane[j]
    gain_row[...] = total
    for k in range(1, chips):
        gain_line_copy(k).start()
    finish(0, grad_output_ref)
    finish(1, grad_query_ref)
    finish(2, grad_pair_ref)
    total = gain_row[...]
    for k in range(1, chips):
        gain_line_copy(k).wait_recv()
        total = total + gain_line[k]
    gains_ref[...] = total
    for b in range(3):
        drain(b)
    for k in range(chips):
        pair_sibling_copy(k).wait_send()
    for k in range(1, chips):
        pair_chip_copy(k).wait_send()
        gain_line_copy(k).wait_send()
    gain_near_copy().wait_send()
    for j in range(1, seqs):
        gain_plane_copy(j).wait_send()


def back_call(seqs, chips, padded_rows, output_rows, *operands):
    fed_back = operands[0]
    count, width = fed_back.shape
    ctxs = 2 * chips
    total = ctxs * count
    blocks = seqs * ctxs
    wide = jnp.float32
    half = jnp.bfloat16
    dma = pltpu.SemaphoreType.DMA
    shape = jax.ShapeDtypeStruct
    vmem = pl.BlockSpec(memory_space=pltpu.VMEM)
    sizes = ((output_rows, width), (padded_rows, H * DH), (padded_rows, 2 * DH))
    scratch = [
        pltpu.VMEM((count, width), half),
        pltpu.VMEM((count, H * DH), wide),
        pltpu.VMEM((H * count, DH), half),
        pltpu.VMEM((H * count, total), half),
        pltpu.VMEM((H * count, total), half),
        pltpu.VMEM((count, width), wide),
        pltpu.VMEM((total, 2 * DH), wide),
        pltpu.VMEM((chips, count, 2 * DH), half),
        pltpu.VMEM((chips, count, 2 * DH), half),
        pltpu.VMEM((chips, count, 2 * DH), half),
        pltpu.VMEM((chips, count, 2 * DH), half),
        pltpu.VMEM((count, (H + 2) * DH), half),
        pltpu.VMEM((8, width), wide),
        pltpu.VMEM((8, width), wide),
        pltpu.VMEM((8, width), wide),
        pltpu.VMEM((seqs, 8, width), wide),
        pltpu.VMEM((8, width), wide),
        pltpu.VMEM((chips, 8, width), wide),
    ]
    for rows, columns in sizes:
        scratch += [
            pltpu.VMEM((blocks, rows, columns), half),
            pltpu.VMEM((seqs, chips, rows, columns), half),
            pltpu.VMEM((seqs, chips, rows, columns), half),
            pltpu.VMEM((seqs, chips, rows, columns), half),
            pltpu.VMEM((chips, rows, columns), half),
            pltpu.VMEM((chips, rows, columns), half),
            pltpu.VMEM((rows, columns), wide),
        ]
    scratch += [
        dma((2, chips)),
        dma((2, chips)),
        dma((2,)),
        dma((2, seqs)),
        dma((2, chips)),
        dma((2, 3, seqs, chips)),
        dma((2, 3, seqs, chips)),
        dma((2, 3, chips)),
    ]
    return pl.pallas_call(
        functools.partial(back_kernel, seqs, chips),
        out_shape=(
            shape((count, width), wide),
            shape(sizes[0], wide),
            shape(sizes[1], wide),
            shape(sizes[2], wide),
            shape((8, width), wide),
        ),
        in_specs=[vmem] * len(operands),
        out_specs=(vmem,) * 5,
        scratch_shapes=scratch,
        compiler_params=pltpu.CompilerParams(
            collective_id=4, has_side_effects=True, vmem_limit_bytes=58 * 2**20
        ),
        cost_estimate=pl.CostEstimate(
            flops=8 * count * width * (H + 2) * DH,
            bytes_accessed=200 * 2**20,
            transcendentals=H * count * total,
        ),
        name="back",
    )(*operands)


def swap_kernel(
    seqs, chips, pair_ref, gate_ref, up_ref, wide_pair, to_ctx, from_ctx, joined, swap_sems
):
    seq, place, core = peers()
    ctx = place * 2 + core
    ctxs = 2 * chips
    rows, width = gate_ref.shape
    units = width // (seqs * ctxs)
    barrier = pltpu.get_barrier_semaphore()
    for k in range(1, ctxs):
        pl.semaphore_signal(
            barrier, inc=1, device_id=(seq, lax.rem(ctx + k, ctxs)), device_id_type=MESH
        )

    def swap_copy(k):
        target = lax.rem(ctx + k, ctxs)
        return send_to(
            to_ctx.at[target],
            from_ctx.at[ctx],
            swap_sems.at[0, k],
            swap_sems.at[1, k],
            (seq, target),
        )

    wide_pair[...] = pair_ref[...].astype(jnp.float32)
    for c in range(ctxs):
        for b in range(2):
            joined[b * rows : (b + 1) * rows, :] = wide_pair[b, c * rows : (c + 1) * rows, :]
        to_ctx[c] = joined[...].astype(jnp.bfloat16)
    pl.semaphore_wait(barrier, ctxs - 1)
    for k in range(1, ctxs):
        swap_copy(k).start()
    from_ctx[ctx] = to_ctx[ctx]
    for k in range(1, ctxs):
        swap_copy(k).wait_recv()
    for c in range(ctxs):
        joined[...] = from_ctx[c].astype(jnp.float32)
        for b, target in ((0, gate_ref), (1, up_ref)):
            for s in range(seqs):
                first = (s * ctxs + c) * units
                target[:, first : first + units] = joined[
                    b * rows : (b + 1) * rows, s * units : (s + 1) * units
                ]
    for k in range(1, ctxs):
        swap_copy(k).wait_send()


def swap_call(seqs, chips, rows, width, pair):
    half = jnp.bfloat16
    shape = jax.ShapeDtypeStruct
    vmem = pl.BlockSpec(memory_space=pltpu.VMEM)
    ctxs = 2 * chips
    unit_count = pair.shape[-1]
    padded = -(-2 * rows // 16) * 16
    return pl.pallas_call(
        functools.partial(swap_kernel, seqs, chips),
        out_shape=(shape((rows, width), jnp.float32), shape((rows, width), jnp.float32)),
        in_specs=[vmem],
        out_specs=(vmem,) * 2,
        scratch_shapes=[
            pltpu.VMEM(pair.shape, jnp.float32),
            pltpu.VMEM((ctxs, padded, unit_count), half),
            pltpu.VMEM((ctxs, padded, unit_count), half),
            pltpu.VMEM((padded, unit_count), jnp.float32),
            pltpu.SemaphoreType.DMA((2, ctxs)),
        ],
        compiler_params=pltpu.CompilerParams(
            collective_id=5, has_side_effects=True, vmem_limit_bytes=40 * 2**20
        ),
        cost_estimate=pl.CostEstimate(flops=0, bytes_accessed=60 * 2**20, transcendentals=0),
        name="swap",
    )(pair)


def per_device(
    inputs,
    positions,
    attention_gain,
    query_weight,
    key_weight,
    value_weight,
    query_gain,
    key_gain,
    output_weight,
    attention_post,
    feedfwd_gain,
    gate_weight,
    up_weight,
    down_weight,
    feedfwd_post,
    cotangent,
):
    seq_total = lax.axis_size("seq")
    ctx_total = lax.axis_size("ctx")
    device_total = seq_total * ctx_total
    token_count = inputs.shape[0]
    width_rows = query_weight.shape[0]
    head_rows = query_gain.shape[0]
    unit_rows = down_weight.shape[0]

    block_number = (positions[:1] // token_count).astype(jnp.bfloat16)
    small = jnp.concatenate(
        [attention_gain, attention_post, feedfwd_gain, feedfwd_post, query_gain, key_gain]
        + [block_number]
    )
    chips = ctx_total // 2
    small_row = jnp.pad(small, (0, (H + 2) * DH - small.shape[0]))[None]
    packet = jnp.concatenate(
        [jnp.concatenate([query_weight, key_weight, value_weight], axis=1), small_row], axis=0
    )
    packet_rows = -(-packet.shape[0] // 16) * 16
    packet = jnp.pad(packet, ((0, packet_rows - packet.shape[0]), (0, 0)))
    packets, outputs, pair = start_call(
        packet, output_weight, gate_weight, up_weight, seq_total, chips
    )
    joint_weight = packets[:, :width_rows].reshape(D, (H + 2) * DH)
    output_all = outputs.reshape(H * DH, D)
    smalls = packets[:, width_rows]

    def gain_of(start, size):
        return smalls[:, start : start + size].reshape(-1).astype(jnp.float32)

    gain_attention = gain_of(0, width_rows)
    gain_post = gain_of(width_rows, width_rows)
    gain_feed = gain_of(2 * width_rows, width_rows)
    gain_final = gain_of(3 * width_rows, width_rows)
    gain_query = gain_of(4 * width_rows, head_rows)
    gain_key = gain_of(4 * width_rows + head_rows, head_rows)
    numbers = smalls[:, 4 * width_rows + 2 * head_rows].astype(jnp.int32)
    own_numbers = lax.dynamic_slice(numbers, (lax.axis_index("seq") * ctx_total,), (ctx_total,))
    place_all = (
        own_numbers[:, None] * token_count + jnp.arange(token_count, dtype=jnp.int32)[None, :]
    ).reshape(-1)

    unit_count = seq_total * unit_rows
    seq_rows = ctx_total * width_rows
    pair_all = lax.all_gather(pair, "seq", axis=0, tiled=False)
    gate_all = pair_all[:, 0].reshape(D, unit_count)
    up_all = pair_all[:, 1].reshape(D, unit_count)
    down_all = lax.all_gather(down_weight, "seq", axis=0, tiled=True)

    cosine, sinus = rotary(positions)
    padded_rows = -(-width_rows // 16) * 16
    (
        spread,
        queries,
        key_rows,
        query_rot,
        both_rows,
        attended,
        logsum,
        mixed_values,
        residual,
        fed_own,
    ) = attend_call(
        chips,
        device_total,
        padded_rows,
        inputs,
        joint_weight,
        output_all,
        gain_attention[None],
        gain_query[None],
        gain_key[None],
        gain_post[None],
        gain_feed[None],
        cosine,
        sinus,
        positions[:, None],
        place_all[None],
    )
    block_out, grad_final, fed_back, down_term, pair_term = feed_call(
        fed_own,
        residual,
        cotangent,
        gain_final[None],
        gate_all,
        up_all,
        down_all,
        seq_total,
        chips,
    )
    pair_sum = lax.psum_scatter(
        pair_term.reshape(seq_total * 2 * seq_rows, unit_count),
        "seq",
        scatter_dimension=0,
        tiled=True,
    )
    grad_down = lax.psum_scatter(
        down_term, "seq", scatter_dimension=0, tiled=True
    ).astype(jnp.float32)
    input_grad, grad_output, grad_query, grad_pair, gains = back_call(
        seq_total,
        chips,
        padded_rows,
        output_weight.shape[0],
        fed_back,
        residual,
        mixed_values,
        cotangent,
        inputs,
        spread,
        queries,
        key_rows,
        query_rot,
        both_rows,
        attended,
        logsum,
        output_all,
        joint_weight,
        grad_final,
        gain_attention[None],
        gain_query[None],
        gain_key[None],
        gain_post[None],
        gain_feed[None],
        cosine,
        sinus,
        positions[:, None],
        place_all[None],
    )
    grad_gate, grad_up = swap_call(
        seq_total, chips, width_rows, FF, pair_sum.reshape(2, seq_rows, unit_count)
    )
    device = lax.axis_index("seq") * ctx_total + lax.axis_index("ctx")

    def own_gain(row, start, size):
        return lax.dynamic_slice(gains, (row, start + device * size), (1, size))[0]

    return (
        block_out,
        input_grad,
        own_gain(0, 0, width_rows),
        grad_query[:width_rows],
        grad_pair[:width_rows, :DH],
        grad_pair[:width_rows, DH:],
        own_gain(4, 0, head_rows),
        own_gain(4, DH, head_rows),
        grad_output,
        own_gain(1, 0, width_rows),
        own_gain(2, 0, width_rows),
        grad_gate,
        grad_up,
        grad_down,
        own_gain(3, 0, width_rows),
    )


def solution(mesh):
    return jax.shard_map(
        per_device,
        mesh=mesh,
        in_specs=(
            P(("seq", "ctx"), None),
            P(("seq", "ctx")),
            P(("seq", "ctx")),
            P(("seq", "ctx"), None),
            P(("seq", "ctx"), None),
            P(("seq", "ctx"), None),
            P(("seq", "ctx")),
            P(("seq", "ctx")),
            P(("seq", "ctx"), None),
            P(("seq", "ctx")),
            P(("seq", "ctx")),
            P(("seq", "ctx"), None),
            P(("seq", "ctx"), None),
            P(("seq", "ctx"), None),
            P(("seq", "ctx")),
            P(("seq", "ctx"), None),
        ),
        out_specs=(
            P(("seq", "ctx"), None),
            P(("seq", "ctx"), None),
            P(("seq", "ctx")),
            P(("seq", "ctx"), None),
            P(("seq", "ctx"), None),
            P(("seq", "ctx"), None),
            P(("seq", "ctx")),
            P(("seq", "ctx")),
            P(("seq", "ctx"), None),
            P(("seq", "ctx")),
            P(("seq", "ctx")),
            P(("seq", "ctx"), None),
            P(("seq", "ctx"), None),
            P(("seq", "ctx"), None),
            P(("seq", "ctx")),
        ),
        check_vma=False,
    )
```

```python
import functools
import math

import jax
import jax.numpy as jnp
from jax import lax
from jax.experimental import pallas as pl
from jax.experimental.pallas import tpu as pltpu
from jax.sharding import PartitionSpec as P

D = 1152
H = 4
DH = 256
FF = 6912


EPSILON = 1e-06
THETA = 1000000.0
GELU_COEF = math.sqrt(2.0 / math.pi)


def rms_factor(values):
    return lax.rsqrt(jnp.mean(values * values, axis=-1, keepdims=True) + EPSILON)


def norm_back(values, factor, gain_vector, upstream):
    scaled = gain_vector * upstream
    cubed = factor * factor * factor
    return factor * scaled - values * cubed * jnp.mean(scaled * values, axis=-1, keepdims=True)


def rotary(places):
    half_width = DH // 2
    exponent = jnp.arange(half_width, dtype=jnp.float32) * (-2.0 / DH)
    frequency = jnp.power(jnp.float32(THETA), exponent)
    angles = places.astype(jnp.float32)[:, None] * frequency[None, :]
    return (jnp.cos(angles), jnp.sin(angles))


def rotate(values, cosine, sinus):
    half_width = values.shape[-1] // 2
    first = values[..., :half_width]
    second = values[..., half_width:]
    return jnp.concatenate(
        [first * cosine - second * sinus, second * cosine + first * sinus], axis=-1
    )


def rotate_back(upstream, cosine, sinus):
    half_width = upstream.shape[-1] // 2
    first = upstream[..., :half_width]
    second = upstream[..., half_width:]
    return jnp.concatenate(
        [first * cosine + second * sinus, second * cosine - first * sinus], axis=-1
    )


def gelu_tanh(values):
    inner = GELU_COEF * (values + 0.044715 * values * values * values)
    return 0.5 * values * (1.0 + jnp.tanh(inner))


def gelu_slope(values):
    inner = GELU_COEF * (values + 0.044715 * values * values * values)
    tangent = jnp.tanh(inner)
    return 0.5 * (1.0 + tangent) + 0.5 * values * (1.0 - tangent * tangent) * GELU_COEF * (
        1.0 + 3.0 * 0.044715 * values * values
    )


def times_right(left_side, right_side):
    return jnp.dot(left_side, right_side, preferred_element_type=jnp.float32)


def times_transposed(left_side, right_side):
    return lax.dot_general(
        left_side, right_side, (((1,), (1,)), ((), ())), preferred_element_type=jnp.float32
    )


def transposed_times(left_side, right_side):
    return lax.dot_general(
        left_side, right_side, (((0,), (0,)), ((), ())), preferred_element_type=jnp.float32
    )


BOTH = ("seq", "ctx")
MESH = pl.DeviceIdType.MESH


def peers():
    seq = lax.axis_index("seq")
    ctx = lax.axis_index("ctx")
    return seq, ctx // 2, lax.rem(ctx, 2)


def greet(seq, place, core, chips):
    barrier = pltpu.get_barrier_semaphore()
    pl.semaphore_signal(
        barrier, inc=1, device_id=(seq, place * 2 + 1 - core), device_id_type=MESH
    )
    for k in range(1, chips):
        other = lax.rem(place + k, chips) * 2 + core
        pl.semaphore_signal(barrier, inc=1, device_id=(seq, other), device_id_type=MESH)
    pl.semaphore_wait(barrier, chips)


def send_to(source, target, send_sem, recv_sem, device):
    return pltpu.make_async_remote_copy(
        src_ref=source,
        dst_ref=target,
        send_sem=send_sem,
        recv_sem=recv_sem,
        device_id=device,
        device_id_type=MESH,
    )


def feed_kernel(
    chips,
    fed_ref,
    residual_ref,
    cot_ref,
    gain_ref,
    gate_ref,
    up_ref,
    down_ref,
    block_ref,
    grad_final_ref,
    fed_back_ref,
    grad_down_ref,
    grad_pair_ref,
    hidden_ref,
    gate_back_ref,
    up_back_ref,
    fed_all,
    back_all,
    gate_values,
    up_values,
    part,
    hidden_back,
    own,
    back_own,
    grad_part,
    to_sibling,
    from_sibling,
    to_chip,
    from_chip,
    gather_sems,
    forward_sems,
    sibling_sems,
    chip_sems,
):
    seq, place, core = peers()
    sibling = (seq, place * 2 + 1 - core)
    count = fed_ref.shape[0]
    pair_count = 2 * count
    chunk = min(64, pair_count)
    greet(seq, place, core, chips)

    def rows_of(chip, which):
        return pl.ds(pl.multiple_of((chip * 2 + which) * count, count), count)

    def pair_of(chip):
        return pl.ds(pl.multiple_of(chip * pair_count, pair_count), pair_count)

    def phase(index, source, rows_all, work, later):
        mine = rows_of(place, core)
        rows_all[mine, :] = source[...]

        def gather_copy(k):
            chip = lax.rem(place + k, chips)
            return send_to(
                source,
                rows_all.at[mine],
                gather_sems.at[0, index, k],
                gather_sems.at[1, index, k],
                (seq, chip * 2 + core),
            )

        def forward_copy(k):
            chip = lax.rem(place - k + chips, chips)
            block = rows_all.at[rows_of(chip, core)]
            return send_to(
                block,
                block,
                forward_sems.at[0, index, k],
                forward_sems.at[1, index, k],
                sibling,
            )

        def sibling_copy(k):
            return send_to(
                to_sibling.at[k],
                from_sibling.at[index, k],
                sibling_sems.at[0, index, k],
                sibling_sems.at[1, index, k],
                sibling,
            )

        def chip_copy(k):
            chip = lax.rem(place - k + chips, chips)
            return send_to(
                to_chip.at[k],
                from_chip.at[index, k],
                chip_sems.at[0, index, k],
                chip_sems.at[1, index, k],
                (seq, chip * 2 + core),
            )

        forward_copy(0).start()
        for k in range(1, chips):
            gather_copy(k).start()

        def step(k, carry):
            chip = lax.rem(place - k + chips, chips)

            @pl.when(k > 0)
            def _():
                gather_copy(k).wait_recv()
                forward_copy(k).start()

            forward_copy(k).wait_recv()
            work(pair_of(chip))
            other_rows = pl.ds(pl.multiple_of((1 - core) * count, count), count)
            own_rows = pl.ds(pl.multiple_of(core * count, count), count)
            to_sibling[k] = part[other_rows, :].astype(jnp.bfloat16)
            sibling_copy(k).start()
            sibling_copy(k).wait_recv()
            total = part[own_rows, :] + from_sibling[index, k].astype(jnp.float32)

            @pl.when(k == 0)
            def _():
                own[...] = total

            @pl.when(k > 0)
            def _():
                to_chip[k] = total.astype(jnp.bfloat16)
                chip_copy(k).start()

            return carry

        lax.fori_loop(0, chips, step, 0)
        later()
        for k in range(1, chips):
            chip_copy(k).wait_recv()
            own[...] += from_chip[index, k].astype(jnp.float32)
        for k in range(chips):
            forward_copy(k).wait_send()
            sibling_copy(k).wait_send()
        for k in range(1, chips):
            gather_copy(k).wait_send()
            chip_copy(k).wait_send()

    def forward_work(rows):
        block = fed_all[rows, :]
        gate_values[rows, :] = times_right(block, gate_ref[...])
        up_values[rows, :] = times_right(block, up_ref[...])

        def gated(j, carry):
            here = pl.ds(pl.multiple_of(rows.start + j * chunk, chunk), chunk)
            hidden_ref[here, :] = (gelu_tanh(gate_values[here, :]) * up_values[here, :]).astype(
                jnp.bfloat16
            )
            return carry

        lax.fori_loop(0, pair_count // chunk, gated, 0)
        part[...] = times_right(hidden_ref[rows, :], down_ref[...])

    def backward_work(rows):
        hidden_back[...] = times_transposed(back_all[rows, :], down_ref[...])

        def gated(j, carry):
            here = pl.ds(pl.multiple_of(rows.start + j * chunk, chunk), chunk)
            local = pl.ds(pl.multiple_of(j * chunk, chunk), chunk)
            gate_now = gate_values[here, :]
            upper = hidden_back[local, :]
            gate_back_ref[here, :] = (upper * up_values[here, :] * gelu_slope(gate_now)).astype(
                jnp.bfloat16
            )
            up_back_ref[here, :] = (upper * gelu_tanh(gate_now)).astype(jnp.bfloat16)
            return carry

        lax.fori_loop(0, pair_count // chunk, gated, 0)
        part[...] = times_transposed(gate_back_ref[rows, :], gate_ref[...])
        part[...] += times_transposed(up_back_ref[rows, :], up_ref[...])

    def weight_terms():
        grad_down_ref[...] = transposed_times(hidden_ref[...], back_all[...]).astype(jnp.bfloat16)
        slabs = grad_pair_ref.shape[0]
        slab_rows = grad_pair_ref.shape[2]
        for b, source in ((0, gate_back_ref), (1, up_back_ref)):
            grad_part[...] = transposed_times(fed_all[...], source[...])
            for s in range(slabs):
                grad_pair_ref[s, b] = grad_part[s * slab_rows : (s + 1) * slab_rows, :].astype(
                    jnp.bfloat16
                )

    phase(0, fed_ref, fed_all, forward_work, lambda: None)
    down_values = own[...]
    down_factor = rms_factor(down_values)
    gain_final = gain_ref[3:4, :]
    block_ref[...] = (residual_ref[...] + down_values * down_factor * gain_final).astype(
        jnp.bfloat16
    )
    cot_wide = cot_ref[...].astype(jnp.float32)
    grad_final_ref[...] = jnp.sum(cot_wide * down_values * down_factor, axis=0, keepdims=True)
    back_own[...] = norm_back(down_values, down_factor, gain_final, cot_wide).astype(jnp.bfloat16)
    phase(1, back_own, back_all, backward_work, weight_terms)
    fed_back_ref[...] = own[...]


def feed_call(fed, residual, cot, gain, gate, up, down, seqs, chips):
    count, width = fed.shape
    total = 2 * chips * count
    units = down.shape[0]
    wide = jnp.float32
    half = jnp.bfloat16
    dma = pltpu.SemaphoreType.DMA
    shape = jax.ShapeDtypeStruct
    vmem = pl.BlockSpec(memory_space=pltpu.VMEM)
    flops = 18 * total * width * units
    return pl.pallas_call(
        functools.partial(feed_kernel, chips),
        out_shape=(
            shape((count, width), half),
            shape((1, width), wide),
            shape((count, width), wide),
            shape((units, width), half),
            shape((seqs, 2, width // seqs, units), half),
        ),
        in_specs=[vmem] * 7,
        out_specs=(vmem,) * 5,
        scratch_shapes=[
            pltpu.VMEM((total, units), half),
            pltpu.VMEM((total, units), half),
            pltpu.VMEM((total, units), half),
            pltpu.VMEM((total, width), half),
            pltpu.VMEM((total, width), half),
            pltpu.VMEM((total, units), wide),
            pltpu.VMEM((total, units), wide),
            pltpu.VMEM((2 * count, width), wide),
            pltpu.VMEM((2 * count, units), wide),
            pltpu.VMEM((count, width), wide),
            pltpu.VMEM((count, width), half),
            pltpu.VMEM((width, units), wide),
            pltpu.VMEM((chips, count, width), half),
            pltpu.VMEM((2, chips, count, width), half),
            pltpu.VMEM((chips, count, width), half),
            pltpu.VMEM((2, chips, count, width), half),
            dma((2, 2, chips)),
            dma((2, 2, chips)),
            dma((2, 2, chips)),
            dma((2, 2, chips)),
        ],
        compiler_params=pltpu.CompilerParams(
            collective_id=1, has_side_effects=True, vmem_limit_bytes=56 * 2**20
        ),
        cost_estimate=pl.CostEstimate(
            flops=flops, bytes_accessed=8 * total * width * 2, transcendentals=total * units
        ),
        name="feed",
    )(fed, residual, cot, gain, gate, up, down)


def front_kernel(
    seqs,
    chips,
    inputs_ref,
    query_ref,
    key_ref,
    value_ref,
    small_ref,
    output_ref,
    gate_ref,
    up_ref,
    down_ref,
    cosine_ref,
    sinus_ref,
    place_ref,
    packets,
    outputs,
    gate_all,
    up_all,
    down_all,
    gains,
    places,
    spread_ref,
    queries_ref,
    key_rows_ref,
    query_rot_ref,
    both_ref,
    attended_ref,
    logsum_ref,
    mixed_ref,
    residual_ref,
    fed_ref,
    wide_packet,
    own_packet,
    own_down,
    to_ctx,
    from_ctx,
    joined,
    packed,
    spread,
    spread_gain,
    own_pair,
    line_sems,
    plane_sems,
    core_sems,
    swap_sems,
    slab_sems,
    gather_sems,
    forward_sems,
):
    seq, place, core = peers()
    ctx = place * 2 + core
    sibling = (seq, place * 2 + 1 - core)
    ctxs = 2 * chips
    blocks = seqs * ctxs
    count, width = inputs_ref.shape
    rows = gate_ref.shape[0]
    head_rows = DH // blocks
    units = down_ref.shape[0]
    slab = own_down.shape[0]
    square = seqs == 4
    beside = seq + 1 - 2 * lax.rem(seq, 2)
    across = lax.rem(seq + 2, 4)
    direct = (1, 2) if square else range(1, seqs)
    barrier = pltpu.get_barrier_semaphore()
    for k in range(1, ctxs):
        pl.semaphore_signal(
            barrier, inc=1, device_id=(seq, lax.rem(ctx + k, ctxs)), device_id_type=MESH
        )
    for j in range(1, seqs):
        pl.semaphore_signal(
            barrier, inc=1, device_id=(lax.rem(seq + j, seqs), ctx), device_id_type=MESH
        )

    def index_of(row, chip, which):
        return row * ctxs + chip * 2 + which

    both = ((own_packet, packets), (output_ref, outputs))

    def line_copy(b, k):
        own, everything = both[b]
        chip = lax.rem(place + k, chips)
        return send_to(
            own,
            everything.at[index_of(seq, place, core)],
            line_sems.at[0, b, k],
            line_sems.at[1, b, k],
            (seq, chip * 2 + core),
        )

    def plane_copy(b, j, k):
        everything = both[b][1]
        chip = lax.rem(place - k + chips, chips)
        row, target = seq, lax.rem(seq + j, seqs)
        if square:
            even = lax.rem(jnp.int32(k), 2) == 0
            if j == 3:
                row = jnp.where(even, beside, across)
                target = jnp.where(even, across, beside)
            else:
                target = beside if j == 1 else across
        block = everything.at[index_of(row, chip, core)]
        return send_to(
            block,
            block,
            plane_sems.at[0, b, j, k],
            plane_sems.at[1, b, j, k],
            (target, ctx),
        )

    def core_copy(b, j, k):
        everything = both[b][1]
        row = (seq, beside, across, 3 - seq)[j] if square else lax.rem(seq - j + seqs, seqs)
        chip = lax.rem(place - k + chips, chips)
        block = everything.at[index_of(row, chip, core)]
        return send_to(
            block, block, core_sems.at[0, b, j, k], core_sems.at[1, b, j, k], sibling
        )

    def swap_copy(k):
        target = lax.rem(ctx + k, ctxs)
        return send_to(
            to_ctx.at[target],
            from_ctx.at[ctx],
            swap_sems.at[0, k],
            swap_sems.at[1, k],
            (seq, target),
        )

    def slab_copy(which, j):
        height = slab if which == 0 else ctxs * rows
        everything = (down_all, gate_all, up_all)[which]
        first, size, target = seq * height, height, lax.rem(seq + j, seqs)
        if square:
            half = height // 2
            if j == 0:
                target = beside
            elif j == 1:
                target = across
            elif j == 2:
                first, size, target = beside * height, half, across
            else:
                first, size, target = across * height + half, half, beside
            first = pl.multiple_of(first, half)
        else:
            first = pl.multiple_of(first, height)
        here = everything.at[pl.ds(first, size)]
        return send_to(
            here,
            here,
            slab_sems.at[0, which, j],
            slab_sems.at[1, which, j],
            (target, ctx),
        )

    def start_slab(which):
        for j in (0, 1) if square else range(1, seqs):
            slab_copy(which, j).start()

    def relay_slab(which):
        if square:
            slab_copy(which, 0).wait_recv()
            slab_copy(which, 2).start()
            slab_copy(which, 1).wait_recv()
            slab_copy(which, 3).start()

    def finish_slab(which):
        if square:
            slab_copy(which, 0).wait_send()
            slab_copy(which, 1).wait_send()
            slab_copy(which, 2).wait()
            slab_copy(which, 3).wait()
        else:
            for j in range(1, seqs):
                slab_copy(which, j).wait()

    def rows_of(chip):
        return pl.ds(pl.multiple_of((chip * 2 + core) * count, count), count)

    def gather_copy(k):
        chip = lax.rem(place + k, chips)
        return send_to(
            own_pair,
            both_ref.at[rows_of(place)],
            gather_sems.at[0, k],
            gather_sems.at[1, k],
            (seq, chip * 2 + core),
        )

    def forward_copy(k):
        chip = lax.rem(place - k + chips, chips)
        block = both_ref.at[rows_of(chip)]
        return send_to(block, block, forward_sems.at[0, k], forward_sems.at[1, k], sibling)

    def start_own(b):
        own, everything = both[b]
        for k in range(1, chips):
            line_copy(b, k).start()
        everything[index_of(seq, place, core)] = own[...]
        for j in direct:
            plane_copy(b, j, 0).start()
        core_copy(b, 0, 0).start()

    def line_step(b):
        def one(k, carry):
            line_copy(b, k).wait_recv()
            for j in direct:
                plane_copy(b, j, k).start()
            core_copy(b, 0, k).start()
            return carry

        lax.fori_loop(1, chips, one, 0)

    def plane_step(b):
        def one(k, carry):
            for j in direct:
                plane_copy(b, j, k).wait_recv()
            if square:
                plane_copy(b, 3, k).start()
            for j in direct:
                core_copy(b, j, k).start()
            return carry

        lax.fori_loop(0, chips, one, 0)

    def relay_step(b):
        def one(k, carry):
            plane_copy(b, 3, k).wait_recv()
            core_copy(b, 3, k).start()
            return carry

        if square:
            lax.fori_loop(0, chips, one, 0)

    def core_step(b):
        def one(k, carry):
            for j in range(seqs):
                core_copy(b, j, k).wait_recv()
            return carry

        lax.fori_loop(0, chips, one, 0)

    def drain(b):
        def one(k, carry):
            for j in range(seqs):
                core_copy(b, j, k).wait_send()
                if j > 0:
                    plane_copy(b, j, k).wait_send()
            return carry

        lax.fori_loop(0, chips, one, 0)
        for k in range(1, chips):
            line_copy(b, k).wait_send()

    wide_packet[...] = jnp.zeros_like(wide_packet)
    wide_packet[0:rows, 0 : H * DH] = query_ref[...].astype(jnp.float32)
    wide_packet[0:rows, H * DH : (H + 1) * DH] = key_ref[...].astype(jnp.float32)
    wide_packet[0:rows, (H + 1) * DH :] = value_ref[...].astype(jnp.float32)
    wide_packet[rows : rows + 1, :] = small_ref[...].astype(jnp.float32)
    own_packet[...] = wide_packet[...].astype(jnp.bfloat16)
    own_down[...] = jnp.zeros_like(own_down)
    own_down[0:units, :] = down_ref[...].astype(jnp.float32)
    down_all[pl.ds(pl.multiple_of(seq * slab, slab), slab), :] = own_down[...].astype(
        jnp.bfloat16
    )
    pl.semaphore_wait(barrier, ctxs + seqs - 2)
    start_own(0)
    start_slab(0)

    joined[...] = jnp.zeros_like(joined)
    for c in range(ctxs):
        for b, source in ((0, gate_ref), (1, up_ref)):
            for s in range(seqs):
                first = (s * ctxs + c) * units
                low = first // 128 * 128
                high = min(-(-(first + units) // 128) * 128, gate_ref.shape[1])
                wide = source[:, low:high].astype(jnp.float32)
                joined[b * rows : (b + 1) * rows, s * slab : s * slab + units] = wide[
                    :, first - low : first - low + units
                ]
        to_ctx[c] = joined[...].astype(jnp.bfloat16)
    line_step(0)
    for k in range(1, ctxs):
        swap_copy(k).start()
    start_own(1)
    from_ctx[ctx] = to_ctx[ctx]

    input_wide = inputs_ref[...].astype(jnp.float32)
    scaled = input_wide * rms_factor(input_wide)
    spread[...] = jnp.zeros_like(spread)
    step = packets.shape[1]
    for i in range(blocks):
        spread[:, i * step : i * step + rows] = scaled[:, i * rows : (i + 1) * rows]
    plane_step(0)
    line_step(1)
    relay_step(0)
    core_step(0)

    gains[...] = jnp.zeros_like(gains)
    spread_gain[...] = jnp.zeros_like(spread_gain)
    base = rows // 8 * 8
    for i in range(blocks):
        line = packets[i, base:, :256].astype(jnp.float32)[rows - base : rows - base + 1]
        for g in range(4):
            gains[g : g + 1, i * rows : (i + 1) * rows] = line[:, g * rows : (g + 1) * rows]
        spread_gain[0:1, i * step : i * step + rows] = line[:, 0:rows]
        for g in range(2):
            first = 4 * rows + g * head_rows
            here = g * DH + i * head_rows
            gains[4:5, here : here + head_rows] = line[:, first : first + head_rows]
    number_at = 4 * rows + 2 * head_rows
    offsets = lax.broadcasted_iota(jnp.int32, (1, count), 1).astype(jnp.float32)
    for c in range(ctxs):
        line = packets[seq * ctxs + c, base:, :256].astype(jnp.float32)
        number = line[rows - base : rows - base + 1, number_at : number_at + 1]
        places[:, c * count : (c + 1) * count] = number * count + offsets
    spread_ref[...] = (spread[...] * spread_gain[0:1, :]).astype(jnp.bfloat16)
    joint = packets.reshape(blocks * step, (H + 2) * DH)
    cosine = cosine_ref[...]
    sinus = sinus_ref[...]
    pair = times_right(spread_ref[...], joint[:, H * DH :])
    key_rows = pair[:, :DH]
    key_rows_ref[...] = key_rows
    key_rot = rotate(key_rows * rms_factor(key_rows) * gains[4:5, DH : 2 * DH], cosine, sinus)
    own_pair[:, :DH] = key_rot.astype(jnp.bfloat16)
    own_pair[:, DH:] = pair[:, DH:].astype(jnp.bfloat16)
    both_ref[rows_of(place), :] = own_pair[...]
    for k in range(1, chips):
        gather_copy(k).start()
    forward_copy(0).start()
    for h in range(H):
        mine = slice(h * count, (h + 1) * count)
        queries = times_right(spread_ref[...], joint[:, h * DH : (h + 1) * DH])
        queries_ref[mine, :] = queries
        query_rot_ref[mine, :] = rotate(
            queries * rms_factor(queries) * gains[4:5, 0:DH], cosine, sinus
        ).astype(jnp.bfloat16)

    for k in range(1, ctxs):
        swap_copy(k).wait_recv()
    for c in range(ctxs):
        joined[...] = from_ctx[c].astype(jnp.float32)
        for b in range(2):
            packed[b, c * rows : (c + 1) * rows, :] = joined[b * rows : (b + 1) * rows, :]
    height = ctxs * rows
    here = pl.ds(pl.multiple_of(seq * height, height), height)
    gate_all[here, :] = packed[0].astype(jnp.bfloat16)
    up_all[here, :] = packed[1].astype(jnp.bfloat16)
    start_slab(1)
    start_slab(2)
    relay_slab(0)
    plane_step(1)

    for k in range(1, chips):
        gather_copy(k).wait_recv()
        forward_copy(k).start()
    for k in range(chips):
        forward_copy(k).wait_recv()
    scaling = 1.0 / math.sqrt(DH)

    def head(h, carry):
        mine = pl.ds(pl.multiple_of(h * count, count), count)
        columns = pl.ds(pl.multiple_of(h * DH, DH), DH)
        allowed = places[...] <= place_ref[...]
        scores = times_transposed(query_rot_ref[mine, :], both_ref[:, :DH]) * scaling
        expscore = jnp.where(allowed, jnp.exp(scores), 0.0)
        weight_sum = jnp.sum(expscore, axis=-1, keepdims=True)
        summed = times_right(expscore.astype(jnp.bfloat16), both_ref[:, DH:])
        attended_ref[:, columns] = (summed / weight_sum).astype(jnp.bfloat16)
        logsum_ref[mine, :] = jnp.log(weight_sum)
        return carry

    lax.fori_loop(0, H, head, 0)
    relay_step(1)
    core_step(1)
    relay_slab(1)
    mixed_ref[...] = times_right(attended_ref[...], outputs.reshape(H * DH, width)[...])
    mixed = mixed_ref[...]
    residual = inputs_ref[...].astype(jnp.float32) + mixed * rms_factor(mixed) * gains[1:2, :]
    residual_ref[...] = residual
    fed_ref[...] = (residual * rms_factor(residual) * gains[2:3, :]).astype(jnp.bfloat16)
    for b in range(2):
        drain(b)
    for k in range(1, ctxs):
        swap_copy(k).wait_send()
    for k in range(chips):
        forward_copy(k).wait_send()
    for k in range(1, chips):
        gather_copy(k).wait_send()
    relay_slab(2)
    for which in range(3):
        finish_slab(which)


def front_call(seqs, chips, *operands):
    inputs, query_weight = operands[:2]
    output, gate, _, down = operands[5:9]
    count, width = inputs.shape
    wide = jnp.float32
    half = jnp.bfloat16
    dma = pltpu.SemaphoreType.DMA
    shape = jax.ShapeDtypeStruct
    vmem = pl.BlockSpec(memory_space=pltpu.VMEM)
    ctxs = 2 * chips
    total = ctxs * count
    blocks = seqs * ctxs
    rows = gate.shape[0]
    packet_rows = -(-(rows + 1) // 16) * 16
    joint_width = (H + 2) * DH
    slab = -(-down.shape[0] // 16) * 16
    unit_count = seqs * slab
    padded = -(-2 * rows // 16) * 16
    return pl.pallas_call(
        functools.partial(front_kernel, seqs, chips),
        out_shape=(
            shape((blocks, packet_rows, joint_width), half),
            shape((blocks,) + output.shape, half),
            shape((width, unit_count), half),
            shape((width, unit_count), half),
            shape((unit_count, width), half),
            shape((8, width), wide),
            shape((1, total), wide),
            shape((count, blocks * packet_rows), half),
            shape((H * count, DH), wide),
            shape((count, DH), wide),
            shape((H * count, DH), half),
            shape((total, 2 * DH), half),
            shape((count, H * DH), half),
            shape((H * count, 1), wide),
            shape((count, width), wide),
            shape((count, width), wide),
            shape((count, width), half),
        ),
        in_specs=[vmem] * len(operands),
        out_specs=(vmem,) * 17,
        scratch_shapes=[
            pltpu.VMEM((packet_rows, joint_width), wide),
            pltpu.VMEM((packet_rows, joint_width), half),
            pltpu.VMEM((slab, width), wide),
            pltpu.VMEM((ctxs, padded, unit_count), half),
            pltpu.VMEM((ctxs, padded, unit_count), half),
            pltpu.VMEM((padded, unit_count), wide),
            pltpu.VMEM((2, ctxs * rows, unit_count), wide),
            pltpu.VMEM((count, blocks * packet_rows), wide),
            pltpu.VMEM((8, blocks * packet_rows), wide),
            pltpu.VMEM((count, 2 * DH), half),
            dma((2, 2, chips)),
            dma((2, 2, seqs, chips)),
            dma((2, 2, seqs, chips)),
            dma((2, ctxs)),
            dma((2, 3, max(seqs, 4))),
            dma((2, chips)),
            dma((2, chips)),
        ],
        compiler_params=pltpu.CompilerParams(
            collective_id=2, has_side_effects=True, vmem_limit_bytes=58 * 2**20
        ),
        name="front",
    )(*operands)


def back_kernel(
    seqs,
    chips,
    fed_back_ref,
    residual_ref,
    mixed_ref,
    cot_ref,
    inputs_ref,
    spread_ref,
    queries_ref,
    key_rows_ref,
    query_rot_ref,
    both_ref,
    attended_ref,
    logsum_ref,
    output_ref,
    joint_ref,
    grad_final_ref,
    gain_all_ref,
    cosine_ref,
    sinus_ref,
    place_ref,
    places_ref,
    pair_term_ref,
    down_term_ref,
    input_grad_ref,
    grad_output_ref,
    grad_query_ref,
    grad_pair_ref,
    gains_ref,
    grad_gate_ref,
    grad_up_ref,
    grad_down_ref,
    mixed_back,
    attended_back,
    upper_round,
    probs,
    score_back,
    normed_wide,
    input_wide_back,
    pair_part,
    pair_to_sibling,
    pair_from_sibling,
    pair_to_chip,
    pair_from_chip,
    joint_back,
    gain_term,
    gain_near,
    gain_chip,
    gain_plane,
    gain_row,
    gain_line,
    gate_near,
    down_near,
    gate_middle,
    down_middle,
    gate_total,
    to_ctx,
    from_ctx,
    joined,
    *rest,
):
    seq, place, core = peers()
    ctx = place * 2 + core
    ctxs = 2 * chips
    sibling = (seq, place * 2 + 1 - core)
    count = cot_ref.shape[0]
    buffers = [rest[6 * b : 6 * b + 6] for b in range(3)]
    (
        pair_sibling_sems,
        pair_chip_sems,
        gain_near_sems,
        gain_plane_sems,
        gain_line_sems,
        near_sems,
        plane_sems,
        line_sems,
        slab_sems,
        own_sems,
        swap_sems,
    ) = rest[18:]
    barrier = pltpu.get_barrier_semaphore()
    for k in range(1, ctxs):
        pl.semaphore_signal(
            barrier, inc=1, device_id=(seq, lax.rem(ctx + k, ctxs)), device_id_type=MESH
        )
    for j in range(1, seqs):
        pl.semaphore_signal(
            barrier, inc=1, device_id=(lax.rem(seq + j, seqs), ctx), device_id_type=MESH
        )
    pl.semaphore_wait(barrier, ctxs + seqs - 2)
    rows_own, gate_width = grad_gate_ref.shape
    units = grad_down_ref.shape[0]
    slab = down_near.shape[1]

    square = seqs == 4
    beside = seq + 1 - 2 * lax.rem(seq, 2)
    across = lax.rem(seq + 2, 4)
    direct = (1, 2) if square else range(1, seqs)

    def part_of(which, half):
        if which == 0:
            return half
        return pl.ds(half * (slab // 2), slab // 2)

    terms = (pair_term_ref, down_term_ref)
    nears = (gate_near, down_near)
    middles = (gate_middle, down_middle)

    def slab_copy(which, j):
        source, near, middle = terms[which], nears[which], middles[which]
        low, high = part_of(which, 0), part_of(which, 1)
        if not square:
            row = lax.rem(seq + j, seqs)
            origin, goal, target = source.at[row], near.at[j], row
        elif j == 0:
            origin, goal, target = source.at[3 - seq, low], middle.at[0, low], beside
        elif j == 1:
            origin, goal, target = source.at[3 - seq, high], middle.at[0, high], across
        elif j == 2:
            origin, goal, target = source.at[across, high], near.at[2, high], across
        elif j == 3:
            origin, goal, target = source.at[beside, low], near.at[1, low], beside
        elif j == 4:
            origin, goal, target = middle.at[1, low], near.at[2, low], across
        else:
            origin, goal, target = middle.at[1, high], near.at[1, high], beside
        return send_to(
            origin, goal, slab_sems.at[0, which, j], slab_sems.at[1, which, j], (target, ctx)
        )

    def own_slab(which):
        return pltpu.make_async_copy(
            terms[which].at[seq], nears[which].at[0], own_sems.at[which, 0]
        )

    def middle_slab(which, half):
        part = part_of(which, half)
        row = across if half == 0 else beside
        return pltpu.make_async_copy(
            terms[which].at[row, part], middles[which].at[1, part], own_sems.at[which, 1 + half]
        )

    def start_slab(which):
        for j in range(4) if square else range(1, seqs):
            slab_copy(which, j).start()
        own_slab(which).start()
        if square:
            middle_slab(which, 0).start()
            middle_slab(which, 1).start()

    def relay_slab(which):
        if square:
            middle = middles[which]
            for half in range(2):
                part = part_of(which, half)
                middle_slab(which, half).wait()
                slab_copy(which, half).wait_recv()
                middle[1, part] = (
                    middle[1, part].astype(jnp.float32) + middle[0, part].astype(jnp.float32)
                ).astype(jnp.bfloat16)
                slab_copy(which, 4 + half).start()

    def finish_slab(which):
        own_slab(which).wait()
        for j in range(2, 6) if square else range(1, seqs):
            slab_copy(which, j).wait_recv()

    def swap_copy(k):
        target = lax.rem(ctx + k, ctxs)
        return send_to(
            to_ctx.at[target],
            from_ctx.at[ctx],
            swap_sems.at[0, k],
            swap_sems.at[1, k],
            (seq, target),
        )

    start_slab(0)
    start_slab(1)

    def block_of(j, k, which):
        row = (seq, beside, across, 3 - seq)[j] if square else lax.rem(seq + j, seqs)
        chip = lax.rem(place + k, chips)
        return row * ctxs + chip * 2 + which

    def near_copy(b, j, k):
        term, near = buffers[b][:2]
        return send_to(
            term.at[block_of(j, k, 1 - core)],
            near.at[j, k],
            near_sems.at[0, b, j, k],
            near_sems.at[1, b, j, k],
            sibling,
        )

    def plane_copy(b, j, k):
        near, plane_from = buffers[b][1:3]
        target = lax.rem(seq + j, seqs)
        if square:
            even = lax.rem(jnp.int32(k), 2) == 0
            target = (seq, beside, across, jnp.where(even, beside, across))[j]
        return send_to(
            near.at[j, k],
            plane_from.at[j, k],
            plane_sems.at[0, b, j, k],
            plane_sems.at[1, b, j, k],
            (target, ctx),
        )

    def line_copy(b, k):
        line_to, line_from = buffers[b][3:5]
        return send_to(
            line_to.at[k],
            line_from.at[k],
            line_sems.at[0, b, k],
            line_sems.at[1, b, k],
            (seq, lax.rem(place + k, chips) * 2 + core),
        )

    def start_near(b):
        def one(k, carry):
            for j in range(seqs):
                near_copy(b, j, lax.rem(k + 1, chips)).start()
            return carry

        lax.fori_loop(0, chips, one, 0)

    def run_plane(b):
        term, near = buffers[b][:2]

        def one(i, carry):
            k = lax.rem(i + 1, chips)
            for j in range(seqs - 1, -1, -1):
                near_copy(b, j, k).wait_recv()
                near[j, k] = (
                    term[block_of(j, k, core)].astype(jnp.float32)
                    + near[j, k].astype(jnp.float32)
                ).astype(jnp.bfloat16)
                if j == 3 or (j > 0 and not square):
                    plane_copy(b, j, k).start()
            if square:

                @pl.when(lax.rem(k, 2) == 0)
                def _():
                    plane_copy(b, 1, k).start()

                @pl.when(lax.rem(k, 2) == 1)
                def _():
                    plane_copy(b, 2, k).start()

            return carry

        lax.fori_loop(0, chips, one, 0)

    def relay_plane(b):
        _, near, plane_from = buffers[b][:3]

        def one(i, carry):
            k = lax.rem(i + 1, chips)
            plane_copy(b, 3, k).wait_recv()

            def add(j):
                near[j, k] = (
                    near[j, k].astype(jnp.float32) + plane_from[3, k].astype(jnp.float32)
                ).astype(jnp.bfloat16)
                plane_copy(b, j, k).start()

            @pl.when(lax.rem(k, 2) == 0)
            def _():
                add(2)

            @pl.when(lax.rem(k, 2) == 1)
            def _():
                add(1)

            return carry

        if square:
            lax.fori_loop(0, chips, one, 0)

    def run_line(b):
        _, near, plane_from, line_to, _, own = buffers[b]

        def one(i, carry):
            k = lax.rem(i + 1, chips)
            total = near[0, k].astype(jnp.float32)
            for j in direct:
                plane_copy(b, j, k).wait_recv()
                total = total + plane_from[j, k].astype(jnp.float32)

            @pl.when(k > 0)
            def _():
                line_to[k] = total.astype(jnp.bfloat16)
                line_copy(b, k).start()

            @pl.when(k == 0)
            def _():
                own[...] = total

            return carry

        lax.fori_loop(0, chips, one, 0)

    def finish(b, target):
        _, _, _, _, line_from, own = buffers[b]
        total = own[...]
        for k in range(1, chips):
            line_copy(b, k).wait_recv()
            total = total + line_from[k].astype(jnp.float32)
        target[...] = total

    def drain(b):
        def one(k, carry):
            for j in range(seqs):
                near_copy(b, j, k).wait_send()
                if j > 0:
                    plane_copy(b, j, k).wait_send()
            return carry

        lax.fori_loop(0, chips, one, 0)
        for k in range(1, chips):
            line_copy(b, k).wait_send()

    def pair_rows(chip, which):
        return pl.ds(pl.multiple_of((chip * 2 + which) * count, count), count)

    def pair_sibling_copy(k):
        return send_to(
            pair_to_sibling.at[k],
            pair_from_sibling.at[k],
            pair_sibling_sems.at[0, k],
            pair_sibling_sems.at[1, k],
            sibling,
        )

    def pair_chip_copy(k):
        return send_to(
            pair_to_chip.at[k],
            pair_from_chip.at[k],
            pair_chip_sems.at[0, k],
            pair_chip_sems.at[1, k],
            (seq, lax.rem(place + k, chips) * 2 + core),
        )

    scaling = 1.0 / math.sqrt(DH)
    cosine = cosine_ref[...]
    sinus = sinus_ref[...]
    residual = residual_ref[...]
    residual_factor = rms_factor(residual)
    fed_back = fed_back_ref[...]
    gain_term[...] = jnp.zeros_like(gain_term)
    gain_term[3:4, :] = grad_final_ref[...]
    gain_term[2:3, :] = jnp.sum(fed_back * residual * residual_factor, axis=0, keepdims=True)
    residual_back = cot_ref[...].astype(jnp.float32) + norm_back(
        residual, residual_factor, gain_all_ref[2:3, :], fed_back
    )
    input_grad_ref[...] = residual_back
    mixed = mixed_ref[...]
    mixed_factor = rms_factor(mixed)
    gain_term[1:2, :] = jnp.sum(residual_back * mixed * mixed_factor, axis=0, keepdims=True)
    mixed_back[...] = norm_back(mixed, mixed_factor, gain_all_ref[1:2, :], residual_back).astype(
        jnp.bfloat16
    )
    output_term = buffers[0][0]
    output_rows = output_term.shape[1]
    for h in range(H):
        columns = slice(h * DH, (h + 1) * DH)
        part = transposed_times(attended_ref[:, columns], mixed_back[...])
        each = DH // output_rows
        for i in range(each):
            output_term[h * each + i] = part[i * output_rows : (i + 1) * output_rows].astype(
                jnp.bfloat16
            )
    start_near(0)
    attended_back[...] = times_transposed(mixed_back[...], output_ref[...])

    def head(h, carry):
        rows = pl.ds(pl.multiple_of(h * count, count), count)
        columns = pl.ds(pl.multiple_of(h * DH, DH), DH)
        upper = attended_back[:, columns]
        upper_round[rows, :] = upper.astype(jnp.bfloat16)
        row_delta = jnp.sum(
            upper * attended_ref[:, columns].astype(jnp.float32), axis=-1, keepdims=True
        )
        allowed = places_ref[...] <= place_ref[...]
        scores = times_transposed(query_rot_ref[rows, :], both_ref[:, :DH]) * scaling
        probability = jnp.where(allowed, jnp.exp(scores - logsum_ref[rows, :]), 0.0)
        probs[rows, :] = probability.astype(jnp.bfloat16)
        prob_back = times_transposed(upper_round[rows, :], both_ref[:, DH:])
        score_back[rows, :] = (probability * (prob_back - row_delta) * scaling).astype(
            jnp.bfloat16
        )
        return carry

    lax.fori_loop(0, H, head, 0)
    relay_slab(0)
    pair_part[:, :DH] = transposed_times(score_back[...], query_rot_ref[...])
    pair_part[:, DH:] = transposed_times(probs[...], upper_round[...])
    for i in range(chips):
        k = (i + 1) % chips
        chip = lax.rem(place + k, chips)
        pair_to_sibling[k] = pair_part[pair_rows(chip, 1 - core), :].astype(jnp.bfloat16)
        pair_sibling_copy(k).start()
    run_plane(0)
    for i in range(chips - 1):
        k = i + 1
        chip = lax.rem(place + k, chips)
        pair_sibling_copy(k).wait_recv()
        pair_to_chip[k] = (
            pair_part[pair_rows(chip, core), :] + pair_from_sibling[k].astype(jnp.float32)
        ).astype(jnp.bfloat16)
        pair_chip_copy(k).start()

    relay_plane(0)
    gain_query = gain_all_ref[4:5, 0:DH]
    grad_query_gain = jnp.zeros((1, DH), jnp.float32)
    for h in range(H):
        rows = slice(h * count, (h + 1) * count)
        upward = rotate_back(times_right(score_back[rows, :], both_ref[:, :DH]), cosine, sinus)
        queries = queries_ref[rows, :]
        factor = rms_factor(queries)
        grad_query_gain += jnp.sum(upward * queries * factor, axis=0, keepdims=True)
        joint_back[:, h * DH : (h + 1) * DH] = norm_back(
            queries, factor, gain_query, upward
        ).astype(jnp.bfloat16)
    gain_term[4:5, :DH] = grad_query_gain

    def joint_term(b, columns):
        term = buffers[b][0]
        blocks, rows, _ = term.shape
        group = 256 // rows if 256 % rows == 0 else 8
        while blocks % group:
            group -= 1
        wide = group * rows
        for g in range(blocks // group):
            part = transposed_times(
                spread_ref[:, g * wide : (g + 1) * wide], joint_back[:, columns]
            )
            for i in range(group):
                term[g * group + i] = part[i * rows : (i + 1) * rows].astype(jnp.bfloat16)

    joint_term(1, slice(0, H * DH))
    start_near(1)
    relay_slab(1)
    run_line(0)
    finish_slab(0)
    for b in range(2):
        total = gate_near[0, b].astype(jnp.float32)
        for j in direct:
            total = total + gate_near[j, b].astype(jnp.float32)
        gate_total[b] = total
    for c in range(ctxs):
        for b in range(2):
            joined[b * rows_own : (b + 1) * rows_own, :] = gate_total[
                b, c * rows_own : (c + 1) * rows_own, :
            ]
        to_ctx[c] = joined[...].astype(jnp.bfloat16)
    for k in range(1, ctxs):
        swap_copy(k).start()
    from_ctx[ctx] = to_ctx[ctx]

    pair_sibling_copy(0).wait_recv()
    own_pair = pair_part[pair_rows(place, core), :] + pair_from_sibling[0].astype(jnp.float32)
    for k in range(1, chips):
        pair_chip_copy(k).wait_recv()
        own_pair = own_pair + pair_from_chip[k].astype(jnp.float32)
    key_up = rotate_back(own_pair[:, :DH], cosine, sinus)
    key_rows = key_rows_ref[...]
    key_factor = rms_factor(key_rows)
    gain_term[4:5, DH : 2 * DH] = jnp.sum(key_up * key_rows * key_factor, axis=0, keepdims=True)
    joint_back[:, H * DH : (H + 1) * DH] = norm_back(
        key_rows, key_factor, gain_all_ref[4:5, DH : 2 * DH], key_up
    ).astype(jnp.bfloat16)
    joint_back[:, (H + 1) * DH :] = own_pair[:, DH:].astype(jnp.bfloat16)
    joint_term(2, slice(H * DH, (H + 2) * DH))
    start_near(2)
    run_plane(1)

    normed_wide[...] = times_transposed(joint_back[...], joint_ref[...])
    spaced = spread_ref.shape[1] // (seqs * ctxs)
    for i in range(seqs * ctxs):
        input_wide_back[:, i * rows_own : (i + 1) * rows_own] = normed_wide[
            :, i * spaced : i * spaced + rows_own
        ]
    normed_back = input_wide_back[...]
    input_wide = inputs_ref[...].astype(jnp.float32)
    input_factor = rms_factor(input_wide)
    gain_term[0:1, :] = jnp.sum(normed_back * input_wide * input_factor, axis=0, keepdims=True)

    def gain_near_copy():
        return send_to(gain_term, gain_near, gain_near_sems.at[0], gain_near_sems.at[1], sibling)

    def gain_plane_copy(j):
        return send_to(
            gain_chip,
            gain_plane.at[j],
            gain_plane_sems.at[0, j],
            gain_plane_sems.at[1, j],
            (lax.rem(seq + j, seqs), ctx),
        )

    def gain_line_copy(k):
        return send_to(
            gain_row,
            gain_line.at[k],
            gain_line_sems.at[0, k],
            gain_line_sems.at[1, k],
            (seq, lax.rem(place + k, chips) * 2 + core),
        )

    gain_near_copy().start()
    run_plane(2)
    relay_plane(1)
    gain_near_copy().wait_recv()
    gain_chip[...] = gain_term[...] + gain_near[...]
    for j in range(1, seqs):
        gain_plane_copy(j).start()
    input_grad_ref[...] += norm_back(
        input_wide, input_factor, gain_all_ref[0:1, :], normed_back
    )
    relay_plane(2)
    run_line(1)
    run_line(2)
    total = gain_chip[...]
    for j in range(1, seqs):
        gain_plane_copy(j).wait_recv()
        total = total + gain_plane[j]
    gain_row[...] = total
    for k in range(1, chips):
        gain_line_copy(k).start()
    finish_slab(1)
    total = down_near[0].astype(jnp.float32)
    for j in direct:
        total = total + down_near[j].astype(jnp.float32)
    grad_down_ref[...] = total[0:units]
    for k in range(1, ctxs):
        swap_copy(k).wait_recv()
    for c in range(ctxs):
        joined[...] = from_ctx[c].astype(jnp.float32)
        for b, target in ((0, grad_gate_ref), (1, grad_up_ref)):
            for s in range(seqs):
                first = (s * ctxs + c) * units
                target[:, first : first + units] = joined[
                    b * rows_own : (b + 1) * rows_own, s * slab : s * slab + units
                ]
    finish(0, grad_output_ref)
    finish(1, grad_query_ref)
    finish(2, grad_pair_ref)
    total = gain_row[...]
    for k in range(1, chips):
        gain_line_copy(k).wait_recv()
        total = total + gain_line[k]
    gains_ref[...] = total
    for b in range(3):
        drain(b)
    for which in range(2):
        for j in range(6) if square else range(1, seqs):
            slab_copy(which, j).wait_send()
    for k in range(1, ctxs):
        swap_copy(k).wait_send()
    for k in range(chips):
        pair_sibling_copy(k).wait_send()
    for k in range(1, chips):
        pair_chip_copy(k).wait_send()
        gain_line_copy(k).wait_send()
    gain_near_copy().wait_send()
    for j in range(1, seqs):
        gain_plane_copy(j).wait_send()


def back_call(seqs, chips, padded_rows, output_rows, width_rows, units, *operands):
    fed_back = operands[0]
    count, width = fed_back.shape
    ctxs = 2 * chips
    total = ctxs * count
    blocks = seqs * ctxs
    wide = jnp.float32
    half = jnp.bfloat16
    dma = pltpu.SemaphoreType.DMA
    shape = jax.ShapeDtypeStruct
    vmem = pl.BlockSpec(memory_space=pltpu.VMEM)
    pair_term, down_term = operands[-2:]
    near_slabs, middle_slabs = (3, 2) if seqs == 4 else (seqs, 1)
    unit_count = pair_term.shape[-1]
    both_rows = -(-2 * width_rows // 16) * 16
    hbm = pl.BlockSpec(memory_space=pl.ANY)
    sizes = ((output_rows, width), (padded_rows, H * DH), (padded_rows, 2 * DH))
    scratch = [
        pltpu.VMEM((count, width), half),
        pltpu.VMEM((count, H * DH), wide),
        pltpu.VMEM((H * count, DH), half),
        pltpu.VMEM((H * count, total), half),
        pltpu.VMEM((H * count, total), half),
        pltpu.VMEM((count, blocks * padded_rows), wide),
        pltpu.VMEM((count, width), wide),
        pltpu.VMEM((total, 2 * DH), wide),
        pltpu.VMEM((chips, count, 2 * DH), half),
        pltpu.VMEM((chips, count, 2 * DH), half),
        pltpu.VMEM((chips, count, 2 * DH), half),
        pltpu.VMEM((chips, count, 2 * DH), half),
        pltpu.VMEM((count, (H + 2) * DH), half),
        pltpu.VMEM((8, width), wide),
        pltpu.VMEM((8, width), wide),
        pltpu.VMEM((8, width), wide),
        pltpu.VMEM((seqs, 8, width), wide),
        pltpu.VMEM((8, width), wide),
        pltpu.VMEM((chips, 8, width), wide),
        pltpu.VMEM((near_slabs,) + pair_term.shape[1:], half),
        pltpu.VMEM((near_slabs,) + down_term.shape[1:], half),
        pltpu.VMEM((middle_slabs,) + pair_term.shape[1:], half),
        pltpu.VMEM((middle_slabs,) + down_term.shape[1:], half),
        pltpu.VMEM(pair_term.shape[1:], wide),
        pltpu.VMEM((ctxs, both_rows, unit_count), half),
        pltpu.VMEM((ctxs, both_rows, unit_count), half),
        pltpu.VMEM((both_rows, unit_count), wide),
    ]
    for rows, columns in sizes:
        scratch += [
            pltpu.VMEM((blocks, rows, columns), half),
            pltpu.VMEM((seqs, chips, rows, columns), half),
            pltpu.VMEM((seqs, chips, rows, columns), half),
            pltpu.VMEM((chips, rows, columns), half),
            pltpu.VMEM((chips, rows, columns), half),
            pltpu.VMEM((rows, columns), wide),
        ]
    scratch += [
        dma((2, chips)),
        dma((2, chips)),
        dma((2,)),
        dma((2, seqs)),
        dma((2, chips)),
        dma((2, 3, seqs, chips)),
        dma((2, 3, seqs, chips)),
        dma((2, 3, chips)),
        dma((2, 2, max(seqs, 6))),
        dma((2, 3)),
        dma((2, ctxs)),
    ]
    return pl.pallas_call(
        functools.partial(back_kernel, seqs, chips),
        out_shape=(
            shape((count, width), wide),
            shape(sizes[0], wide),
            shape(sizes[1], wide),
            shape(sizes[2], wide),
            shape((8, width), wide),
            shape((width_rows, blocks * units), wide),
            shape((width_rows, blocks * units), wide),
            shape((units, width), wide),
        ),
        in_specs=[vmem] * (len(operands) - 2) + [hbm] * 2,
        out_specs=(vmem,) * 8,
        scratch_shapes=scratch,
        compiler_params=pltpu.CompilerParams(
            collective_id=4, has_side_effects=True, vmem_limit_bytes=58 * 2**20
        ),
        cost_estimate=pl.CostEstimate(
            flops=8 * count * width * (H + 2) * DH,
            bytes_accessed=200 * 2**20,
            transcendentals=H * count * total,
        ),
        name="back",
    )(*operands)


def per_device(
    inputs,
    positions,
    attention_gain,
    query_weight,
    key_weight,
    value_weight,
    query_gain,
    key_gain,
    output_weight,
    attention_post,
    feedfwd_gain,
    gate_weight,
    up_weight,
    down_weight,
    feedfwd_post,
    cotangent,
):
    seq_total = lax.axis_size("seq")
    ctx_total = lax.axis_size("ctx")
    device_total = seq_total * ctx_total
    token_count = inputs.shape[0]
    width_rows = query_weight.shape[0]
    head_rows = query_gain.shape[0]
    unit_rows = down_weight.shape[0]

    block_number = (positions[:1] // token_count).astype(jnp.bfloat16)
    small = jnp.concatenate(
        [attention_gain, attention_post, feedfwd_gain, feedfwd_post, query_gain, key_gain]
        + [block_number]
    )
    chips = ctx_total // 2
    padded_rows = -(-(width_rows + 1) // 16) * 16
    small_row = jnp.pad(small, (0, (H + 2) * DH - small.shape[0]))[None]
    cosine, sinus = rotary(positions)
    place_wide = positions.astype(jnp.float32)[:, None]
    (
        packets,
        outputs,
        gate_all,
        up_all,
        down_all,
        gain_all,
        places,
        spread,
        queries,
        key_rows,
        query_rot,
        both_rows,
        attended,
        logsum,
        mixed_values,
        residual,
        fed_own,
    ) = front_call(
        seq_total,
        chips,
        inputs,
        query_weight,
        key_weight,
        value_weight,
        small_row,
        output_weight,
        gate_weight,
        up_weight,
        down_weight,
        cosine,
        sinus,
        place_wide,
    )
    block_out, grad_final, fed_back, down_term, pair_term = feed_call(
        fed_own,
        residual,
        cotangent,
        gain_all,
        gate_all,
        up_all,
        down_all,
        seq_total,
        chips,
    )
    (
        input_grad,
        grad_output,
        grad_query,
        grad_pair,
        gains,
        grad_gate,
        grad_up,
        grad_down,
    ) = back_call(
        seq_total,
        chips,
        padded_rows,
        output_weight.shape[0],
        width_rows,
        unit_rows,
        fed_back,
        residual,
        mixed_values,
        cotangent,
        inputs,
        spread,
        queries,
        key_rows,
        query_rot,
        both_rows,
        attended,
        logsum,
        outputs.reshape(H * DH, D),
        packets.reshape(-1, (H + 2) * DH),
        grad_final,
        gain_all,
        cosine,
        sinus,
        place_wide,
        places,
        pair_term,
        down_term.reshape(seq_total, -1, D),
    )
    device = lax.axis_index("seq") * ctx_total + lax.axis_index("ctx")

    def own_gain(row, start, size):
        return lax.dynamic_slice(gains, (row, start + device * size), (1, size))[0]

    return (
        block_out,
        input_grad,
        own_gain(0, 0, width_rows),
        grad_query[:width_rows],
        grad_pair[:width_rows, :DH],
        grad_pair[:width_rows, DH:],
        own_gain(4, 0, head_rows),
        own_gain(4, DH, head_rows),
        grad_output,
        own_gain(1, 0, width_rows),
        own_gain(2, 0, width_rows),
        grad_gate,
        grad_up,
        grad_down,
        own_gain(3, 0, width_rows),
    )


def solution(mesh):
    return jax.shard_map(
        per_device,
        mesh=mesh,
        in_specs=(
            P(("seq", "ctx"), None),
            P(("seq", "ctx")),
            P(("seq", "ctx")),
            P(("seq", "ctx"), None),
            P(("seq", "ctx"), None),
            P(("seq", "ctx"), None),
            P(("seq", "ctx")),
            P(("seq", "ctx")),
            P(("seq", "ctx"), None),
            P(("seq", "ctx")),
            P(("seq", "ctx")),
            P(("seq", "ctx"), None),
            P(("seq", "ctx"), None),
            P(("seq", "ctx"), None),
            P(("seq", "ctx")),
            P(("seq", "ctx"), None),
        ),
        out_specs=(
            P(("seq", "ctx"), None),
            P(("seq", "ctx"), None),
            P(("seq", "ctx")),
            P(("seq", "ctx"), None),
            P(("seq", "ctx"), None),
            P(("seq", "ctx"), None),
            P(("seq", "ctx")),
            P(("seq", "ctx")),
            P(("seq", "ctx"), None),
            P(("seq", "ctx")),
            P(("seq", "ctx")),
            P(("seq", "ctx"), None),
            P(("seq", "ctx"), None),
            P(("seq", "ctx"), None),
            P(("seq", "ctx")),
        ),
        check_vma=False,
    )
```

```python
import functools
import math

import jax
import jax.numpy as jnp
from jax import lax
from jax.experimental import pallas as pl
from jax.experimental.pallas import tpu as pltpu
from jax.sharding import PartitionSpec as P

D = 1152
H = 4
DH = 256
FF = 6912


EPSILON = 1e-06
THETA = 1000000.0
GELU_COEF = math.sqrt(2.0 / math.pi)


def rms_factor(values):
    return lax.rsqrt(jnp.mean(values * values, axis=-1, keepdims=True) + EPSILON)


def norm_back(values, factor, gain_vector, upstream):
    scaled = gain_vector * upstream
    cubed = factor * factor * factor
    return factor * scaled - values * cubed * jnp.mean(scaled * values, axis=-1, keepdims=True)


def rotary(places):
    half_width = DH // 2
    exponent = jnp.arange(half_width, dtype=jnp.float32) * (-2.0 / DH)
    frequency = jnp.power(jnp.float32(THETA), exponent)
    angles = places.astype(jnp.float32)[:, None] * frequency[None, :]
    return (jnp.cos(angles), jnp.sin(angles))


def rotate(values, cosine, sinus):
    half_width = values.shape[-1] // 2
    first = values[..., :half_width]
    second = values[..., half_width:]
    return jnp.concatenate(
        [first * cosine - second * sinus, second * cosine + first * sinus], axis=-1
    )


def rotate_back(upstream, cosine, sinus):
    half_width = upstream.shape[-1] // 2
    first = upstream[..., :half_width]
    second = upstream[..., half_width:]
    return jnp.concatenate(
        [first * cosine + second * sinus, second * cosine - first * sinus], axis=-1
    )


def gelu_tanh(values):
    inner = GELU_COEF * (values + 0.044715 * values * values * values)
    return 0.5 * values * (1.0 + jnp.tanh(inner))


def gelu_slope(values):
    inner = GELU_COEF * (values + 0.044715 * values * values * values)
    tangent = jnp.tanh(inner)
    return 0.5 * (1.0 + tangent) + 0.5 * values * (1.0 - tangent * tangent) * GELU_COEF * (
        1.0 + 3.0 * 0.044715 * values * values
    )


def times_right(left_side, right_side):
    return jnp.dot(left_side, right_side, preferred_element_type=jnp.float32)


def times_transposed(left_side, right_side):
    return lax.dot_general(
        left_side, right_side, (((1,), (1,)), ((), ())), preferred_element_type=jnp.float32
    )


def transposed_times(left_side, right_side):
    return lax.dot_general(
        left_side, right_side, (((0,), (0,)), ((), ())), preferred_element_type=jnp.float32
    )


BOTH = ("seq", "ctx")
MESH = pl.DeviceIdType.MESH


def peers():
    seq = lax.axis_index("seq")
    ctx = lax.axis_index("ctx")
    return seq, ctx // 2, lax.rem(ctx, 2)


def greet(seq, place, core, chips):
    barrier = pltpu.get_barrier_semaphore()
    pl.semaphore_signal(
        barrier, inc=1, device_id=(seq, place * 2 + 1 - core), device_id_type=MESH
    )
    for k in range(1, chips):
        other = lax.rem(place + k, chips) * 2 + core
        pl.semaphore_signal(barrier, inc=1, device_id=(seq, other), device_id_type=MESH)
    pl.semaphore_wait(barrier, chips)


def send_to(source, target, send_sem, recv_sem, device):
    return pltpu.make_async_remote_copy(
        src_ref=source,
        dst_ref=target,
        send_sem=send_sem,
        recv_sem=recv_sem,
        device_id=device,
        device_id_type=MESH,
    )


def plane_of(seq):
    return seq + 1 - 2 * lax.rem(seq, 2), lax.rem(seq + 2, 4)


def slab_sum(seqs, ctx, seq, term, near, middle, part_of, slab_sems, own_sems):
    square = seqs == 4
    beside, across = plane_of(seq)
    low, high = part_of(0), part_of(1)

    def copy(j):
        if not square:
            row = lax.rem(seq + j, seqs)
            origin, goal, target = term.at[row], near.at[j], row
        elif j == 0:
            origin, goal, target = term.at[3 - seq, low], middle.at[0, low], beside
        elif j == 1:
            origin, goal, target = term.at[3 - seq, high], middle.at[0, high], across
        elif j == 2:
            origin, goal, target = term.at[across, high], near.at[2, high], across
        elif j == 3:
            origin, goal, target = term.at[beside, low], near.at[1, low], beside
        elif j == 4:
            origin, goal, target = middle.at[1, low], near.at[2, low], across
        else:
            origin, goal, target = middle.at[1, high], near.at[1, high], beside
        return send_to(origin, goal, slab_sems.at[0, j], slab_sems.at[1, j], (target, ctx))

    def own():
        return pltpu.make_async_copy(term.at[seq], near.at[0], own_sems.at[0])

    def between(half):
        part = part_of(half)
        row = across if half == 0 else beside
        return pltpu.make_async_copy(
            term.at[row, part], middle.at[1, part], own_sems.at[1 + half]
        )

    def start():
        for j in range(2) if square else range(1, seqs):
            copy(j).start()
        own().start()
        if square:
            between(0).start()
            between(1).start()

    def rest():
        if square:
            copy(2).start()
            copy(3).start()

    def relay():
        if square:
            for half in range(2):
                part = part_of(half)
                between(half).wait()
                copy(half).wait_recv()
                middle[1, part] = (
                    middle[1, part].astype(jnp.float32) + middle[0, part].astype(jnp.float32)
                ).astype(jnp.bfloat16)
                copy(4 + half).start()

    def finish():
        own().wait()
        for j in range(2, 6) if square else range(1, seqs):
            copy(j).wait_recv()

    def drain():
        for j in range(6) if square else range(1, seqs):
            copy(j).wait_send()

    return start, rest, relay, finish, drain


def feed_kernel(
    seqs,
    chips,
    fed_all,
    residual_ref,
    cot_ref,
    gain_ref,
    gate_ref,
    up_ref,
    down_ref,
    block_ref,
    grad_final_ref,
    fed_back_ref,
    grad_down_ref,
    grad_pair_ref,
    hidden_ref,
    gate_back_ref,
    up_back_ref,
    back_all,
    gate_values,
    up_values,
    part,
    hidden_back,
    own,
    grad_part,
    down_term,
    down_near,
    down_middle,
    to_sibling,
    from_sibling,
    to_chip,
    from_chip,
    gather_sems,
    forward_sems,
    sibling_sems,
    chip_sems,
    slab_sems,
    own_sems,
):
    seq, place, core = peers()
    ctx = place * 2 + core
    sibling = (seq, place * 2 + 1 - core)
    count = residual_ref.shape[0]
    pair_count = 2 * count
    chunk = min(64, pair_count)
    slab = down_near.shape[1]
    barrier = pltpu.get_barrier_semaphore()
    pl.semaphore_signal(barrier, inc=1, device_id=sibling, device_id_type=MESH)
    for k in range(1, chips):
        other = lax.rem(place + k, chips) * 2 + core
        pl.semaphore_signal(barrier, inc=1, device_id=(seq, other), device_id_type=MESH)
    for j in range(1, seqs):
        pl.semaphore_signal(
            barrier, inc=1, device_id=(lax.rem(seq + j, seqs), ctx), device_id_type=MESH
        )
    start_down, rest_down, relay_down, finish_down, drain_down = slab_sum(
        seqs,
        ctx,
        seq,
        down_term,
        down_near,
        down_middle,
        lambda half: pl.ds(half * (slab // 2), slab // 2),
        slab_sems,
        own_sems,
    )

    def rows_of(chip, which):
        return pl.ds(pl.multiple_of((chip * 2 + which) * count, count), count)

    def pair_of(chip):
        return pl.ds(pl.multiple_of(chip * pair_count, pair_count), pair_count)

    mine = rows_of(place, core)

    def gather_copy(k):
        chip = lax.rem(place + k, chips)
        return send_to(
            back_all.at[mine],
            back_all.at[mine],
            gather_sems.at[0, k],
            gather_sems.at[1, k],
            (seq, chip * 2 + core),
        )

    def forward_copy(k):
        chip = lax.rem(place - k + chips, chips)
        block = back_all.at[rows_of(chip, core)]
        return send_to(block, block, forward_sems.at[0, k], forward_sems.at[1, k], sibling)

    def sibling_copy(index, k):
        return send_to(
            to_sibling.at[k],
            from_sibling.at[index, k],
            sibling_sems.at[0, index, k],
            sibling_sems.at[1, index, k],
            sibling,
        )

    def chip_copy(index, k):
        chip = lax.rem(place - k + chips, chips)
        return send_to(
            to_chip.at[k],
            from_chip.at[index, k],
            chip_sems.at[0, index, k],
            chip_sems.at[1, index, k],
            (seq, chip * 2 + core),
        )

    def pass_part(index, k):
        other_rows = pl.ds(pl.multiple_of((1 - core) * count, count), count)
        own_rows = pl.ds(pl.multiple_of(core * count, count), count)
        to_sibling[k] = part[other_rows, :].astype(jnp.bfloat16)
        sibling_copy(index, k).start()
        sibling_copy(index, k).wait_recv()
        total = part[own_rows, :] + from_sibling[index, k].astype(jnp.float32)

        @pl.when(k == 0)
        def _():
            own[...] = total

        @pl.when(k > 0)
        def _():
            to_chip[k] = total.astype(jnp.bfloat16)
            chip_copy(index, k).start()

    def collect(index):
        for k in range(1, chips):
            chip_copy(index, k).wait_recv()
            own[...] += from_chip[index, k].astype(jnp.float32)
        for k in range(chips):
            sibling_copy(index, k).wait_send()
        for k in range(1, chips):
            chip_copy(index, k).wait_send()

    def forward_step(i, carry):
        k = lax.rem(i + 1, chips)
        rows = pair_of(lax.rem(place - k + chips, chips))
        block = fed_all[rows, :]
        gate_values[rows, :] = times_right(block, gate_ref[...])
        up_values[rows, :] = times_right(block, up_ref[...])

        def gated(j, carry):
            here = pl.ds(pl.multiple_of(rows.start + j * chunk, chunk), chunk)
            hidden_ref[here, :] = (gelu_tanh(gate_values[here, :]) * up_values[here, :]).astype(
                jnp.bfloat16
            )
            return carry

        lax.fori_loop(0, pair_count // chunk, gated, 0)
        part[...] = times_right(hidden_ref[rows, :], down_ref[...])

        @pl.when(i == 0)
        def _():
            pl.semaphore_wait(barrier, chips + seqs - 1)

        pass_part(0, k)
        return carry

    def backward_step(k, carry):
        @pl.when(k < 2)
        def _():
            forward_copy(k).wait_recv()

        rows = pair_of(lax.rem(place - k + chips, chips))
        hidden_back[...] = times_transposed(back_all[rows, :], down_ref[...])

        def gated(j, carry):
            here = pl.ds(pl.multiple_of(rows.start + j * chunk, chunk), chunk)
            local = pl.ds(pl.multiple_of(j * chunk, chunk), chunk)
            gate_now = gate_values[here, :]
            upper = hidden_back[local, :]
            gate_back_ref[here, :] = (upper * up_values[here, :] * gelu_slope(gate_now)).astype(
                jnp.bfloat16
            )
            up_back_ref[here, :] = (upper * gelu_tanh(gate_now)).astype(jnp.bfloat16)
            return carry

        lax.fori_loop(0, pair_count // chunk, gated, 0)
        part[...] = times_transposed(gate_back_ref[rows, :], gate_ref[...])
        part[...] += times_transposed(up_back_ref[rows, :], up_ref[...])
        pass_part(1, k)

        @pl.when(k == 0)
        def _():
            for k in range(1, chips):
                gather_copy(k).wait_recv()
                forward_copy(k).start()

        @pl.when(k == 1)
        def _():
            for k in range(2, chips):
                forward_copy(k).wait_recv()
            for s in range(seqs):
                down_term[s] = transposed_times(
                    hidden_ref[:, s * slab : (s + 1) * slab], back_all[...]
                ).astype(jnp.bfloat16)
            start_down()
            rest_down()

        return carry

    lax.fori_loop(0, chips, forward_step, 0)
    collect(0)
    down_values = own[...]
    down_factor = rms_factor(down_values)
    gain_final = gain_ref[3:4, :]
    cot_wide = cot_ref[...].astype(jnp.float32)
    back_all[mine, :] = norm_back(down_values, down_factor, gain_final, cot_wide).astype(
        jnp.bfloat16
    )
    for k in range(1, chips):
        gather_copy(k).start()
    forward_copy(0).start()
    block_ref[...] = (residual_ref[...] + down_values * down_factor * gain_final).astype(
        jnp.bfloat16
    )
    grad_final_ref[...] = jnp.sum(cot_wide * down_values * down_factor, axis=0, keepdims=True)
    lax.fori_loop(0, chips, backward_step, 0)
    relay_down()
    slabs, _, slab_rows, _ = grad_pair_ref.shape
    tall = grad_part.shape[0]
    for b, source in ((0, gate_back_ref), (1, up_back_ref)):
        for c in range(slabs * slab_rows // tall):
            grad_part[...] = transposed_times(
                fed_all[:, c * tall : (c + 1) * tall], source[...]
            )
            for s in range(slabs):
                low = max(s * slab_rows, c * tall)
                high = min((s + 1) * slab_rows, (c + 1) * tall)
                if low < high:
                    grad_pair_ref[s, b, low - s * slab_rows : high - s * slab_rows] = grad_part[
                        low - c * tall : high - c * tall, :
                    ].astype(jnp.bfloat16)
    collect(1)
    fed_back_ref[...] = own[...]
    finish_down()
    total = down_near[0].astype(jnp.float32)
    for j in (1, 2) if seqs == 4 else range(1, seqs):
        total = total + down_near[j].astype(jnp.float32)
    grad_down_ref[...] = total[0 : grad_down_ref.shape[0]]
    drain_down()
    for k in range(chips):
        forward_copy(k).wait_send()
    for k in range(1, chips):
        gather_copy(k).wait_send()


def feed_call(fed, residual, cot, gain, gate, up, down, down_rows, seqs, chips):
    count, width = residual.shape
    total = 2 * chips * count
    units = down.shape[0]
    slab = units // seqs
    wide = jnp.float32
    half = jnp.bfloat16
    dma = pltpu.SemaphoreType.DMA
    shape = jax.ShapeDtypeStruct
    vmem = pl.BlockSpec(memory_space=pltpu.VMEM)
    near_slabs, middle_slabs = (3, 2) if seqs == 4 else (seqs, 1)
    return pl.pallas_call(
        functools.partial(feed_kernel, seqs, chips),
        out_shape=(
            shape((count, width), half),
            shape((1, width), wide),
            shape((count, width), wide),
            shape((down_rows, width), wide),
            shape((seqs, 2, width // seqs, units), half),
        ),
        in_specs=[vmem] * 7,
        out_specs=(vmem,) * 5,
        scratch_shapes=[
            pltpu.VMEM((total, units), half),
            pltpu.VMEM((total, units), half),
            pltpu.VMEM((total, units), half),
            pltpu.VMEM((total, width), half),
            pltpu.VMEM((total, units), wide),
            pltpu.VMEM((total, units), wide),
            pltpu.VMEM((2 * count, width), wide),
            pltpu.VMEM((2 * count, units), wide),
            pltpu.VMEM((count, width), wide),
            pltpu.VMEM((width // 3, units), wide),
            pltpu.VMEM((seqs, slab, width), half),
            pltpu.VMEM((near_slabs, slab, width), half),
            pltpu.VMEM((middle_slabs, slab, width), half),
            pltpu.VMEM((chips, count, width), half),
            pltpu.VMEM((2, chips, count, width), half),
            pltpu.VMEM((chips, count, width), half),
            pltpu.VMEM((2, chips, count, width), half),
            dma((2, chips)),
            dma((2, chips)),
            dma((2, 2, chips)),
            dma((2, 2, chips)),
            dma((2, max(seqs, 6))),
            dma((3,)),
        ],
        compiler_params=pltpu.CompilerParams(
            collective_id=1, has_side_effects=True, vmem_limit_bytes=58 * 2**20
        ),
        name="feed",
    )(fed, residual, cot, gain, gate, up, down)


def front_kernel(
    seqs,
    chips,
    inputs_ref,
    query_ref,
    key_ref,
    value_ref,
    small_ref,
    output_ref,
    gate_ref,
    up_ref,
    down_ref,
    cosine_ref,
    sinus_ref,
    place_ref,
    packets,
    outputs,
    gate_all,
    up_all,
    down_all,
    gains,
    places,
    spread_ref,
    queries_ref,
    key_rows_ref,
    query_rot_ref,
    both_ref,
    attended_ref,
    logsum_ref,
    mixed_ref,
    residual_ref,
    fed_all,
    wide_packet,
    own_packet,
    own_down,
    to_ctx,
    from_ctx,
    joined,
    packed,
    spread,
    spread_gain,
    own_pair,
    line_sems,
    plane_sems,
    core_sems,
    swap_sems,
    slab_sems,
    gather_sems,
    forward_sems,
    fed_sems,
    pass_sems,
):
    seq, place, core = peers()
    ctx = place * 2 + core
    sibling = (seq, place * 2 + 1 - core)
    ctxs = 2 * chips
    blocks = seqs * ctxs
    count, width = inputs_ref.shape
    rows = gate_ref.shape[0]
    head_rows = DH // blocks
    units = down_ref.shape[0]
    slab = own_down.shape[0]
    square = seqs == 4
    beside = seq + 1 - 2 * lax.rem(seq, 2)
    across = lax.rem(seq + 2, 4)
    direct = (1, 2) if square else range(1, seqs)
    barrier = pltpu.get_barrier_semaphore()
    for k in range(1, ctxs):
        pl.semaphore_signal(
            barrier, inc=1, device_id=(seq, lax.rem(ctx + k, ctxs)), device_id_type=MESH
        )
    for j in range(1, seqs):
        pl.semaphore_signal(
            barrier, inc=1, device_id=(lax.rem(seq + j, seqs), ctx), device_id_type=MESH
        )

    def index_of(row, chip, which):
        return row * ctxs + chip * 2 + which

    both = ((own_packet, packets), (output_ref, outputs))

    def line_copy(b, k):
        own, everything = both[b]
        chip = lax.rem(place + k, chips)
        return send_to(
            own,
            everything.at[index_of(seq, place, core)],
            line_sems.at[0, b, k],
            line_sems.at[1, b, k],
            (seq, chip * 2 + core),
        )

    def plane_copy(b, j, k):
        everything = both[b][1]
        chip = lax.rem(place - k + chips, chips)
        row, target = seq, lax.rem(seq + j, seqs)
        if square:
            even = lax.rem(jnp.int32(k), 2) == 0
            if j == 3:
                row = jnp.where(even, beside, across)
                target = jnp.where(even, across, beside)
            else:
                target = beside if j == 1 else across
        block = everything.at[index_of(row, chip, core)]
        return send_to(
            block,
            block,
            plane_sems.at[0, b, j, k],
            plane_sems.at[1, b, j, k],
            (target, ctx),
        )

    def core_copy(b, j, k):
        everything = both[b][1]
        row = (seq, beside, across, 3 - seq)[j] if square else lax.rem(seq - j + seqs, seqs)
        chip = lax.rem(place - k + chips, chips)
        block = everything.at[index_of(row, chip, core)]
        return send_to(
            block, block, core_sems.at[0, b, j, k], core_sems.at[1, b, j, k], sibling
        )

    def swap_copy(k):
        target = lax.rem(ctx + k, ctxs)
        return send_to(
            to_ctx.at[target],
            from_ctx.at[ctx],
            swap_sems.at[0, k],
            swap_sems.at[1, k],
            (seq, target),
        )

    def slab_copy(which, j):
        height = slab if which == 0 else ctxs * rows
        everything = (down_all, gate_all, up_all)[which]
        first, size, target = seq * height, height, lax.rem(seq + j, seqs)
        if square:
            half = height // 2
            if j == 0:
                target = beside
            elif j == 1:
                target = across
            elif j == 2:
                first, size, target = beside * height, half, across
            else:
                first, size, target = across * height + half, half, beside
            first = pl.multiple_of(first, half)
        else:
            first = pl.multiple_of(first, height)
        here = everything.at[pl.ds(first, size)]
        return send_to(
            here,
            here,
            slab_sems.at[0, which, j],
            slab_sems.at[1, which, j],
            (target, ctx),
        )

    def start_slab(which):
        for j in (0, 1) if square else range(1, seqs):
            slab_copy(which, j).start()

    def relay_slab(which):
        if square:
            slab_copy(which, 0).wait_recv()
            slab_copy(which, 2).start()
            slab_copy(which, 1).wait_recv()
            slab_copy(which, 3).start()

    def finish_slab(which):
        if square:
            slab_copy(which, 0).wait_send()
            slab_copy(which, 1).wait_send()
            slab_copy(which, 2).wait()
            slab_copy(which, 3).wait()
        else:
            for j in range(1, seqs):
                slab_copy(which, j).wait()

    def rows_of(chip):
        return pl.ds(pl.multiple_of((chip * 2 + core) * count, count), count)

    def gather_copy(k):
        chip = lax.rem(place + k, chips)
        return send_to(
            own_pair,
            both_ref.at[rows_of(place)],
            gather_sems.at[0, k],
            gather_sems.at[1, k],
            (seq, chip * 2 + core),
        )

    def forward_copy(k):
        chip = lax.rem(place - k + chips, chips)
        block = both_ref.at[rows_of(chip)]
        return send_to(block, block, forward_sems.at[0, k], forward_sems.at[1, k], sibling)

    def fed_copy(k):
        chip = lax.rem(place + k, chips)
        block = fed_all.at[rows_of(place)]
        return send_to(
            block, block, fed_sems.at[0, k], fed_sems.at[1, k], (seq, chip * 2 + core)
        )

    def pass_copy(k):
        chip = lax.rem(place - k + chips, chips)
        block = fed_all.at[rows_of(chip)]
        return send_to(block, block, pass_sems.at[0, k], pass_sems.at[1, k], sibling)

    def start_own(b):
        own, everything = both[b]
        for k in range(1, chips):
            line_copy(b, k).start()
        everything[index_of(seq, place, core)] = own[...]
        for j in direct:
            plane_copy(b, j, 0).start()
        core_copy(b, 0, 0).start()

    def line_step(b):
        def one(k, carry):
            line_copy(b, k).wait_recv()
            for j in direct:
                plane_copy(b, j, k).start()
            core_copy(b, 0, k).start()
            return carry

        lax.fori_loop(1, chips, one, 0)

    def plane_step(b):
        def one(k, carry):
            for j in direct:
                plane_copy(b, j, k).wait_recv()
            if square:
                plane_copy(b, 3, k).start()
            for j in direct:
                core_copy(b, j, k).start()
            return carry

        lax.fori_loop(0, chips, one, 0)

    def relay_step(b):
        def one(k, carry):
            plane_copy(b, 3, k).wait_recv()
            core_copy(b, 3, k).start()
            return carry

        if square:
            lax.fori_loop(0, chips, one, 0)

    def core_step(b):
        def one(k, carry):
            for j in range(seqs):
                core_copy(b, j, k).wait_recv()
            return carry

        lax.fori_loop(0, chips, one, 0)

    def drain(b):
        def one(k, carry):
            for j in range(seqs):
                core_copy(b, j, k).wait_send()
                if j > 0:
                    plane_copy(b, j, k).wait_send()
            return carry

        lax.fori_loop(0, chips, one, 0)
        for k in range(1, chips):
            line_copy(b, k).wait_send()

    wide_packet[...] = jnp.zeros_like(wide_packet)
    wide_packet[0:rows, 0 : H * DH] = query_ref[...].astype(jnp.float32)
    wide_packet[0:rows, H * DH : (H + 1) * DH] = key_ref[...].astype(jnp.float32)
    wide_packet[0:rows, (H + 1) * DH :] = value_ref[...].astype(jnp.float32)
    wide_packet[rows : rows + 1, :] = small_ref[...].astype(jnp.float32)
    own_packet[...] = wide_packet[...].astype(jnp.bfloat16)
    own_down[...] = jnp.zeros_like(own_down)
    own_down[0:units, :] = down_ref[...].astype(jnp.float32)
    down_all[pl.ds(pl.multiple_of(seq * slab, slab), slab), :] = own_down[...].astype(
        jnp.bfloat16
    )
    pl.semaphore_wait(barrier, ctxs + seqs - 2)
    start_own(0)
    start_slab(0)

    joined[...] = jnp.zeros_like(joined)
    for c in range(ctxs):
        for b, source in ((0, gate_ref), (1, up_ref)):
            for s in range(seqs):
                first = (s * ctxs + c) * units
                low = first // 128 * 128
                high = min(-(-(first + units) // 128) * 128, gate_ref.shape[1])
                wide = source[:, low:high].astype(jnp.float32)
                joined[b * rows : (b + 1) * rows, s * slab : s * slab + units] = wide[
                    :, first - low : first - low + units
                ]
        to_ctx[c] = joined[...].astype(jnp.bfloat16)
    line_step(0)
    for k in range(1, ctxs):
        swap_copy(k).start()
    start_own(1)
    from_ctx[ctx] = to_ctx[ctx]

    input_wide = inputs_ref[...].astype(jnp.float32)
    scaled = input_wide * rms_factor(input_wide)
    spread[...] = jnp.zeros_like(spread)
    step = packets.shape[1]
    for i in range(blocks):
        spread[:, i * step : i * step + rows] = scaled[:, i * rows : (i + 1) * rows]
    plane_step(0)
    line_step(1)
    relay_step(0)
    core_step(0)

    gains[...] = jnp.zeros_like(gains)
    spread_gain[...] = jnp.zeros_like(spread_gain)
    base = rows // 8 * 8
    for i in range(blocks):
        line = packets[i, base:, :256].astype(jnp.float32)[rows - base : rows - base + 1]
        for g in range(4):
            gains[g : g + 1, i * rows : (i + 1) * rows] = line[:, g * rows : (g + 1) * rows]
        spread_gain[0:1, i * step : i * step + rows] = line[:, 0:rows]
        for g in range(2):
            first = 4 * rows + g * head_rows
            here = g * DH + i * head_rows
            gains[4:5, here : here + head_rows] = line[:, first : first + head_rows]
    number_at = 4 * rows + 2 * head_rows
    offsets = lax.broadcasted_iota(jnp.int32, (1, count), 1).astype(jnp.float32)
    for c in range(ctxs):
        line = packets[seq * ctxs + c, base:, :256].astype(jnp.float32)
        number = line[rows - base : rows - base + 1, number_at : number_at + 1]
        places[:, c * count : (c + 1) * count] = number * count + offsets
    spread_ref[...] = (spread[...] * spread_gain[0:1, :]).astype(jnp.bfloat16)
    joint = packets.reshape(blocks * step, (H + 2) * DH)
    cosine = cosine_ref[...]
    sinus = sinus_ref[...]
    pair = times_right(spread_ref[...], joint[:, H * DH :])
    key_rows = pair[:, :DH]
    key_rows_ref[...] = key_rows
    key_rot = rotate(key_rows * rms_factor(key_rows) * gains[4:5, DH : 2 * DH], cosine, sinus)
    own_pair[:, :DH] = key_rot.astype(jnp.bfloat16)
    own_pair[:, DH:] = pair[:, DH:].astype(jnp.bfloat16)
    both_ref[rows_of(place), :] = own_pair[...]
    for k in range(1, chips):
        gather_copy(k).start()
    forward_copy(0).start()
    for h in range(H):
        mine = slice(h * count, (h + 1) * count)
        queries = times_right(spread_ref[...], joint[:, h * DH : (h + 1) * DH])
        queries_ref[mine, :] = queries
        query_rot_ref[mine, :] = rotate(
            queries * rms_factor(queries) * gains[4:5, 0:DH], cosine, sinus
        ).astype(jnp.bfloat16)

    for k in range(1, ctxs):
        swap_copy(k).wait_recv()
    for c in range(ctxs):
        joined[...] = from_ctx[c].astype(jnp.float32)
        for b in range(2):
            packed[b, c * rows : (c + 1) * rows, :] = joined[b * rows : (b + 1) * rows, :]
    height = ctxs * rows
    here = pl.ds(pl.multiple_of(seq * height, height), height)
    gate_all[here, :] = packed[0].astype(jnp.bfloat16)
    up_all[here, :] = packed[1].astype(jnp.bfloat16)
    start_slab(1)
    start_slab(2)
    relay_slab(0)
    plane_step(1)

    for k in range(1, chips):
        gather_copy(k).wait_recv()
        forward_copy(k).start()
    for k in range(chips):
        forward_copy(k).wait_recv()
    scaling = 1.0 / math.sqrt(DH)

    def head(h, carry):
        mine = pl.ds(pl.multiple_of(h * count, count), count)
        columns = pl.ds(pl.multiple_of(h * DH, DH), DH)
        allowed = places[...] <= place_ref[...]
        scores = times_transposed(query_rot_ref[mine, :], both_ref[:, :DH]) * scaling
        expscore = jnp.where(allowed, jnp.exp(scores), 0.0)
        weight_sum = jnp.sum(expscore, axis=-1, keepdims=True)
        summed = times_right(expscore.astype(jnp.bfloat16), both_ref[:, DH:])
        attended_ref[:, columns] = (summed / weight_sum).astype(jnp.bfloat16)
        logsum_ref[mine, :] = jnp.log(weight_sum)
        return carry

    lax.fori_loop(0, H, head, 0)
    relay_step(1)
    core_step(1)
    mixed_ref[...] = times_right(attended_ref[...], outputs.reshape(H * DH, width)[...])
    mixed = mixed_ref[...]
    residual = inputs_ref[...].astype(jnp.float32) + mixed * rms_factor(mixed) * gains[1:2, :]
    residual_ref[...] = residual
    fed_all[rows_of(place), :] = (residual * rms_factor(residual) * gains[2:3, :]).astype(
        jnp.bfloat16
    )
    for k in range(1, chips):
        fed_copy(k).start()
    pass_copy(0).start()
    relay_slab(1)
    for b in range(2):
        drain(b)
    for k in range(1, ctxs):
        swap_copy(k).wait_send()
    for k in range(chips):
        forward_copy(k).wait_send()
    for k in range(1, chips):
        gather_copy(k).wait_send()
    relay_slab(2)
    for k in range(1, chips):
        fed_copy(k).wait_recv()
        pass_copy(k).start()
    for which in range(3):
        finish_slab(which)
    for k in range(chips):
        pass_copy(k).wait()
    for k in range(1, chips):
        fed_copy(k).wait_send()


def front_call(seqs, chips, *operands):
    inputs, query_weight = operands[:2]
    output, gate, _, down = operands[5:9]
    count, width = inputs.shape
    wide = jnp.float32
    half = jnp.bfloat16
    dma = pltpu.SemaphoreType.DMA
    shape = jax.ShapeDtypeStruct
    vmem = pl.BlockSpec(memory_space=pltpu.VMEM)
    ctxs = 2 * chips
    total = ctxs * count
    blocks = seqs * ctxs
    rows = gate.shape[0]
    packet_rows = -(-(rows + 1) // 16) * 16
    joint_width = (H + 2) * DH
    slab = -(-down.shape[0] // 16) * 16
    unit_count = seqs * slab
    padded = -(-2 * rows // 16) * 16
    return pl.pallas_call(
        functools.partial(front_kernel, seqs, chips),
        out_shape=(
            shape((blocks, packet_rows, joint_width), half),
            shape((blocks,) + output.shape, half),
            shape((width, unit_count), half),
            shape((width, unit_count), half),
            shape((unit_count, width), half),
            shape((8, width), wide),
            shape((1, total), wide),
            shape((count, blocks * packet_rows), half),
            shape((H * count, DH), wide),
            shape((count, DH), wide),
            shape((H * count, DH), half),
            shape((total, 2 * DH), half),
            shape((count, H * DH), half),
            shape((H * count, 1), wide),
            shape((count, width), wide),
            shape((count, width), wide),
            shape((total, width), half),
        ),
        in_specs=[vmem] * len(operands),
        out_specs=(vmem,) * 17,
        scratch_shapes=[
            pltpu.VMEM((packet_rows, joint_width), wide),
            pltpu.VMEM((packet_rows, joint_width), half),
            pltpu.VMEM((slab, width), wide),
            pltpu.VMEM((ctxs, padded, unit_count), half),
            pltpu.VMEM((ctxs, padded, unit_count), half),
            pltpu.VMEM((padded, unit_count), wide),
            pltpu.VMEM((2, ctxs * rows, unit_count), wide),
            pltpu.VMEM((count, blocks * packet_rows), wide),
            pltpu.VMEM((8, blocks * packet_rows), wide),
            pltpu.VMEM((count, 2 * DH), half),
            dma((2, 2, chips)),
            dma((2, 2, seqs, chips)),
            dma((2, 2, seqs, chips)),
            dma((2, ctxs)),
            dma((2, 3, max(seqs, 4))),
            dma((2, chips)),
            dma((2, chips)),
            dma((2, chips)),
            dma((2, chips)),
        ],
        compiler_params=pltpu.CompilerParams(
            collective_id=2, has_side_effects=True, vmem_limit_bytes=58 * 2**20
        ),
        name="front",
    )(*operands)


def back_kernel(
    seqs,
    chips,
    fed_back_ref,
    residual_ref,
    mixed_ref,
    cot_ref,
    inputs_ref,
    spread_ref,
    queries_ref,
    key_rows_ref,
    query_rot_ref,
    both_ref,
    attended_ref,
    logsum_ref,
    output_ref,
    joint_ref,
    grad_final_ref,
    gain_all_ref,
    cosine_ref,
    sinus_ref,
    place_ref,
    places_ref,
    pair_term_ref,
    input_grad_ref,
    grad_output_ref,
    grad_query_ref,
    grad_key_ref,
    grad_value_ref,
    gains_ref,
    grad_gate_ref,
    grad_up_ref,
    mixed_back,
    attended_back,
    upper_round,
    probs,
    score_back,
    normed_wide,
    input_wide_back,
    pair_part,
    pair_to_sibling,
    pair_from_sibling,
    pair_to_chip,
    pair_from_chip,
    joint_back,
    gain_term,
    gain_near,
    gain_chip,
    gain_plane,
    gain_row,
    gain_line,
    gate_near,
    gate_middle,
    gate_total,
    to_ctx,
    from_ctx,
    joined,
    *rest,
):
    seq, place, core = peers()
    ctx = place * 2 + core
    ctxs = 2 * chips
    sibling = (seq, place * 2 + 1 - core)
    count = cot_ref.shape[0]
    buffers = [rest[6 * b : 6 * b + 6] for b in range(3)]
    (
        pair_sibling_sems,
        pair_chip_sems,
        gain_near_sems,
        gain_plane_sems,
        gain_line_sems,
        near_sems,
        plane_sems,
        line_sems,
        slab_sems,
        own_sems,
        swap_sems,
    ) = rest[18:]
    barrier = pltpu.get_barrier_semaphore()
    for k in range(1, ctxs):
        pl.semaphore_signal(
            barrier, inc=1, device_id=(seq, lax.rem(ctx + k, ctxs)), device_id_type=MESH
        )
    for j in range(1, seqs):
        pl.semaphore_signal(
            barrier, inc=1, device_id=(lax.rem(seq + j, seqs), ctx), device_id_type=MESH
        )
    pl.semaphore_wait(barrier, ctxs + seqs - 2)
    rows_own, gate_width = grad_gate_ref.shape
    units = gate_width // (seqs * ctxs)
    slab = gate_near.shape[-1] // seqs

    square = seqs == 4
    beside = seq + 1 - 2 * lax.rem(seq, 2)
    across = lax.rem(seq + 2, 4)
    direct = (1, 2) if square else range(1, seqs)

    start_slab, rest_slab, relay_slab, finish_slab, drain_slab = slab_sum(
        seqs,
        ctx,
        seq,
        pair_term_ref,
        gate_near,
        gate_middle,
        lambda half: half,
        slab_sems,
        own_sems,
    )

    def swap_copy(k):
        target = lax.rem(ctx + k, ctxs)
        return send_to(
            to_ctx.at[target],
            from_ctx.at[ctx],
            swap_sems.at[0, k],
            swap_sems.at[1, k],
            (seq, target),
        )

    start_slab()

    def block_of(j, k, which):
        row = (seq, beside, across, 3 - seq)[j] if square else lax.rem(seq + j, seqs)
        chip = lax.rem(place + k, chips)
        return row * ctxs + chip * 2 + which

    def near_copy(b, j, k):
        term, near = buffers[b][:2]
        return send_to(
            term.at[block_of(j, k, 1 - core)],
            near.at[j, k],
            near_sems.at[0, b, j, k],
            near_sems.at[1, b, j, k],
            sibling,
        )

    def plane_copy(b, j, k):
        near, plane_from = buffers[b][1:3]
        target = lax.rem(seq + j, seqs)
        if square:
            even = lax.rem(jnp.int32(k), 2) == 0
            target = (seq, beside, across, jnp.where(even, beside, across))[j]
        return send_to(
            near.at[j, k],
            plane_from.at[j, k],
            plane_sems.at[0, b, j, k],
            plane_sems.at[1, b, j, k],
            (target, ctx),
        )

    def line_copy(b, k):
        line_to, line_from = buffers[b][3:5]
        return send_to(
            line_to.at[k],
            line_from.at[k],
            line_sems.at[0, b, k],
            line_sems.at[1, b, k],
            (seq, lax.rem(place + k, chips) * 2 + core),
        )

    def start_near(b):
        def one(k, carry):
            for j in range(seqs):
                near_copy(b, j, lax.rem(k + 1, chips)).start()
            return carry

        lax.fori_loop(0, chips, one, 0)

    def run_plane(b):
        term, near = buffers[b][:2]

        def one(i, carry):
            k = lax.rem(i + 1, chips)
            for j in range(seqs - 1, -1, -1):
                near_copy(b, j, k).wait_recv()
                near[j, k] = (
                    term[block_of(j, k, core)].astype(jnp.float32)
                    + near[j, k].astype(jnp.float32)
                ).astype(jnp.bfloat16)
                if j == 3 or (j > 0 and not square):
                    plane_copy(b, j, k).start()
            if square:

                @pl.when(lax.rem(k, 2) == 0)
                def _():
                    plane_copy(b, 1, k).start()

                @pl.when(lax.rem(k, 2) == 1)
                def _():
                    plane_copy(b, 2, k).start()

            return carry

        lax.fori_loop(0, chips, one, 0)

    def relay_plane(b):
        _, near, plane_from = buffers[b][:3]

        def one(i, carry):
            k = lax.rem(i + 1, chips)
            plane_copy(b, 3, k).wait_recv()

            def add(j):
                near[j, k] = (
                    near[j, k].astype(jnp.float32) + plane_from[3, k].astype(jnp.float32)
                ).astype(jnp.bfloat16)
                plane_copy(b, j, k).start()

            @pl.when(lax.rem(k, 2) == 0)
            def _():
                add(2)

            @pl.when(lax.rem(k, 2) == 1)
            def _():
                add(1)

            return carry

        if square:
            lax.fori_loop(0, chips, one, 0)

    def run_line(b):
        _, near, plane_from, line_to, _, own = buffers[b]

        def one(i, carry):
            k = lax.rem(i + 1, chips)
            total = near[0, k].astype(jnp.float32)
            for j in direct:
                plane_copy(b, j, k).wait_recv()
                total = total + plane_from[j, k].astype(jnp.float32)

            @pl.when(k > 0)
            def _():
                line_to[k] = total.astype(jnp.bfloat16)
                line_copy(b, k).start()

            @pl.when(k == 0)
            def _():
                own[...] = total

            return carry

        lax.fori_loop(0, chips, one, 0)

    def finish(b):
        _, _, _, _, line_from, own = buffers[b]
        total = own[...]
        for k in range(1, chips):
            line_copy(b, k).wait_recv()
            total = total + line_from[k].astype(jnp.float32)
        return total

    def drain(b):
        def one(k, carry):
            for j in range(seqs):
                near_copy(b, j, k).wait_send()
                if j > 0:
                    plane_copy(b, j, k).wait_send()
            return carry

        lax.fori_loop(0, chips, one, 0)
        for k in range(1, chips):
            line_copy(b, k).wait_send()

    def pair_rows(chip, which):
        return pl.ds(pl.multiple_of((chip * 2 + which) * count, count), count)

    def pair_sibling_copy(k):
        return send_to(
            pair_to_sibling.at[k],
            pair_from_sibling.at[k],
            pair_sibling_sems.at[0, k],
            pair_sibling_sems.at[1, k],
            sibling,
        )

    def pair_chip_copy(k):
        return send_to(
            pair_to_chip.at[k],
            pair_from_chip.at[k],
            pair_chip_sems.at[0, k],
            pair_chip_sems.at[1, k],
            (seq, lax.rem(place + k, chips) * 2 + core),
        )

    scaling = 1.0 / math.sqrt(DH)
    cosine = cosine_ref[...]
    sinus = sinus_ref[...]
    residual = residual_ref[...]
    residual_factor = rms_factor(residual)
    fed_back = fed_back_ref[...]
    gain_term[...] = jnp.zeros_like(gain_term)
    gain_term[3:4, :] = grad_final_ref[...]
    gain_term[2:3, :] = jnp.sum(fed_back * residual * residual_factor, axis=0, keepdims=True)
    residual_back = cot_ref[...].astype(jnp.float32) + norm_back(
        residual, residual_factor, gain_all_ref[2:3, :], fed_back
    )
    input_grad_ref[...] = residual_back
    mixed = mixed_ref[...]
    mixed_factor = rms_factor(mixed)
    gain_term[1:2, :] = jnp.sum(residual_back * mixed * mixed_factor, axis=0, keepdims=True)
    mixed_back[...] = norm_back(mixed, mixed_factor, gain_all_ref[1:2, :], residual_back).astype(
        jnp.bfloat16
    )
    output_term = buffers[0][0]
    output_rows = output_term.shape[1]
    for h in range(H):
        columns = slice(h * DH, (h + 1) * DH)
        part = transposed_times(attended_ref[:, columns], mixed_back[...])
        each = DH // output_rows
        for i in range(each):
            output_term[h * each + i] = part[i * output_rows : (i + 1) * output_rows].astype(
                jnp.bfloat16
            )
    start_near(0)
    attended_back[...] = times_transposed(mixed_back[...], output_ref[...])

    def head(h, carry):
        rows = pl.ds(pl.multiple_of(h * count, count), count)
        columns = pl.ds(pl.multiple_of(h * DH, DH), DH)
        upper = attended_back[:, columns]
        upper_round[rows, :] = upper.astype(jnp.bfloat16)
        row_delta = jnp.sum(
            upper * attended_ref[:, columns].astype(jnp.float32), axis=-1, keepdims=True
        )
        allowed = places_ref[...] <= place_ref[...]
        scores = times_transposed(query_rot_ref[rows, :], both_ref[:, :DH]) * scaling
        probability = jnp.where(allowed, jnp.exp(scores - logsum_ref[rows, :]), 0.0)
        probs[rows, :] = probability.astype(jnp.bfloat16)
        prob_back = times_transposed(upper_round[rows, :], both_ref[:, DH:])
        score_back[rows, :] = (probability * (prob_back - row_delta) * scaling).astype(
            jnp.bfloat16
        )
        return carry

    lax.fori_loop(0, H, head, 0)
    relay_slab()
    rest_slab()
    pair_part[:, :DH] = transposed_times(score_back[...], query_rot_ref[...])
    pair_part[:, DH:] = transposed_times(probs[...], upper_round[...])
    for i in range(chips):
        k = (i + 1) % chips
        chip = lax.rem(place + k, chips)
        pair_to_sibling[k] = pair_part[pair_rows(chip, 1 - core), :].astype(jnp.bfloat16)
        pair_sibling_copy(k).start()
    run_plane(0)
    for i in range(chips - 1):
        k = i + 1
        chip = lax.rem(place + k, chips)
        pair_sibling_copy(k).wait_recv()
        pair_to_chip[k] = (
            pair_part[pair_rows(chip, core), :] + pair_from_sibling[k].astype(jnp.float32)
        ).astype(jnp.bfloat16)
        pair_chip_copy(k).start()

    relay_plane(0)
    gain_query = gain_all_ref[4:5, 0:DH]
    grad_query_gain = jnp.zeros((1, DH), jnp.float32)
    for h in range(H):
        rows = slice(h * count, (h + 1) * count)
        upward = rotate_back(times_right(score_back[rows, :], both_ref[:, :DH]), cosine, sinus)
        queries = queries_ref[rows, :]
        factor = rms_factor(queries)
        grad_query_gain += jnp.sum(upward * queries * factor, axis=0, keepdims=True)
        joint_back[:, h * DH : (h + 1) * DH] = norm_back(
            queries, factor, gain_query, upward
        ).astype(jnp.bfloat16)
    gain_term[4:5, :DH] = grad_query_gain

    def joint_term(b, columns):
        term = buffers[b][0]
        blocks, rows, _ = term.shape
        group = 256 // rows if 256 % rows == 0 else 8
        while blocks % group:
            group -= 1
        wide = group * rows
        for g in range(blocks // group):
            part = transposed_times(
                spread_ref[:, g * wide : (g + 1) * wide], joint_back[:, columns]
            )
            for i in range(group):
                term[g * group + i] = part[i * rows : (i + 1) * rows].astype(jnp.bfloat16)

    joint_term(1, slice(0, H * DH))
    start_near(1)
    run_line(0)
    finish_slab()
    for b in range(2):
        total = gate_near[0, b].astype(jnp.float32)
        for j in direct:
            total = total + gate_near[j, b].astype(jnp.float32)
        gate_total[b] = total
    for c in range(ctxs):
        for b in range(2):
            joined[b * rows_own : (b + 1) * rows_own, :] = gate_total[
                b, c * rows_own : (c + 1) * rows_own, :
            ]
        to_ctx[c] = joined[...].astype(jnp.bfloat16)
    for k in range(1, ctxs):
        swap_copy(k).start()
    from_ctx[ctx] = to_ctx[ctx]

    pair_sibling_copy(0).wait_recv()
    own_pair = pair_part[pair_rows(place, core), :] + pair_from_sibling[0].astype(jnp.float32)
    for k in range(1, chips):
        pair_chip_copy(k).wait_recv()
        own_pair = own_pair + pair_from_chip[k].astype(jnp.float32)
    key_up = rotate_back(own_pair[:, :DH], cosine, sinus)
    key_rows = key_rows_ref[...]
    key_factor = rms_factor(key_rows)
    gain_term[4:5, DH : 2 * DH] = jnp.sum(key_up * key_rows * key_factor, axis=0, keepdims=True)
    joint_back[:, H * DH : (H + 1) * DH] = norm_back(
        key_rows, key_factor, gain_all_ref[4:5, DH : 2 * DH], key_up
    ).astype(jnp.bfloat16)
    joint_back[:, (H + 1) * DH :] = own_pair[:, DH:].astype(jnp.bfloat16)
    joint_term(2, slice(H * DH, (H + 2) * DH))
    start_near(2)
    run_plane(1)

    normed_wide[...] = times_transposed(joint_back[...], joint_ref[...])
    spaced = spread_ref.shape[1] // (seqs * ctxs)
    for i in range(seqs * ctxs):
        input_wide_back[:, i * rows_own : (i + 1) * rows_own] = normed_wide[
            :, i * spaced : i * spaced + rows_own
        ]
    normed_back = input_wide_back[...]
    input_wide = inputs_ref[...].astype(jnp.float32)
    input_factor = rms_factor(input_wide)
    gain_term[0:1, :] = jnp.sum(normed_back * input_wide * input_factor, axis=0, keepdims=True)

    def gain_near_copy():
        return send_to(gain_term, gain_near, gain_near_sems.at[0], gain_near_sems.at[1], sibling)

    def gain_plane_copy(j):
        return send_to(
            gain_chip,
            gain_plane.at[j],
            gain_plane_sems.at[0, j],
            gain_plane_sems.at[1, j],
            (lax.rem(seq + j, seqs), ctx),
        )

    def gain_line_copy(k):
        return send_to(
            gain_row,
            gain_line.at[k],
            gain_line_sems.at[0, k],
            gain_line_sems.at[1, k],
            (seq, lax.rem(place + k, chips) * 2 + core),
        )

    gain_near_copy().start()
    run_plane(2)
    relay_plane(1)
    gain_near_copy().wait_recv()
    gain_chip[...] = gain_term[...] + gain_near[...]
    for j in range(1, seqs):
        gain_plane_copy(j).start()
    input_grad_ref[...] += norm_back(
        input_wide, input_factor, gain_all_ref[0:1, :], normed_back
    )
    relay_plane(2)
    run_line(1)
    run_line(2)
    total = gain_chip[...]
    for j in range(1, seqs):
        gain_plane_copy(j).wait_recv()
        total = total + gain_plane[j]
    gain_row[...] = total
    for k in range(1, chips):
        gain_line_copy(k).start()
    for k in range(1, ctxs):
        swap_copy(k).wait_recv()
    for c in range(ctxs):
        joined[...] = from_ctx[c].astype(jnp.float32)
        for b, target in ((0, grad_gate_ref), (1, grad_up_ref)):
            for s in range(seqs):
                first = (s * ctxs + c) * units
                target[:, first : first + units] = joined[
                    b * rows_own : (b + 1) * rows_own, s * slab : s * slab + units
                ]
    grad_output_ref[...] = finish(0)
    grad_query_ref[...] = finish(1)[0:rows_own]
    total = finish(2)[0:rows_own]
    grad_key_ref[...] = total[:, :DH]
    grad_value_ref[...] = total[:, DH:]
    total = gain_row[...]
    for k in range(1, chips):
        gain_line_copy(k).wait_recv()
        total = total + gain_line[k]
    gains_ref[...] = total
    for b in range(3):
        drain(b)
    drain_slab()
    for k in range(1, ctxs):
        swap_copy(k).wait_send()
    for k in range(chips):
        pair_sibling_copy(k).wait_send()
    for k in range(1, chips):
        pair_chip_copy(k).wait_send()
        gain_line_copy(k).wait_send()
    gain_near_copy().wait_send()
    for j in range(1, seqs):
        gain_plane_copy(j).wait_send()


def back_call(seqs, chips, padded_rows, output_rows, width_rows, units, *operands):
    fed_back = operands[0]
    count, width = fed_back.shape
    ctxs = 2 * chips
    total = ctxs * count
    blocks = seqs * ctxs
    wide = jnp.float32
    half = jnp.bfloat16
    dma = pltpu.SemaphoreType.DMA
    shape = jax.ShapeDtypeStruct
    vmem = pl.BlockSpec(memory_space=pltpu.VMEM)
    pair_term = operands[-1]
    near_slabs, middle_slabs = (3, 2) if seqs == 4 else (seqs, 1)
    unit_count = pair_term.shape[-1]
    both_rows = -(-2 * width_rows // 16) * 16
    hbm = pl.BlockSpec(memory_space=pl.ANY)
    sizes = ((output_rows, width), (padded_rows, H * DH), (padded_rows, 2 * DH))
    scratch = [
        pltpu.VMEM((count, width), half),
        pltpu.VMEM((count, H * DH), wide),
        pltpu.VMEM((H * count, DH), half),
        pltpu.VMEM((H * count, total), half),
        pltpu.VMEM((H * count, total), half),
        pltpu.VMEM((count, blocks * padded_rows), wide),
        pltpu.VMEM((count, width), wide),
        pltpu.VMEM((total, 2 * DH), wide),
        pltpu.VMEM((chips, count, 2 * DH), half),
        pltpu.VMEM((chips, count, 2 * DH), half),
        pltpu.VMEM((chips, count, 2 * DH), half),
        pltpu.VMEM((chips, count, 2 * DH), half),
        pltpu.VMEM((count, (H + 2) * DH), half),
        pltpu.VMEM((8, width), wide),
        pltpu.VMEM((8, width), wide),
        pltpu.VMEM((8, width), wide),
        pltpu.VMEM((seqs, 8, width), wide),
        pltpu.VMEM((8, width), wide),
        pltpu.VMEM((chips, 8, width), wide),
        pltpu.VMEM((near_slabs,) + pair_term.shape[1:], half),
        pltpu.VMEM((middle_slabs,) + pair_term.shape[1:], half),
        pltpu.VMEM(pair_term.shape[1:], wide),
        pltpu.VMEM((ctxs, both_rows, unit_count), half),
        pltpu.VMEM((ctxs, both_rows, unit_count), half),
        pltpu.VMEM((both_rows, unit_count), wide),
    ]
    for rows, columns in sizes:
        scratch += [
            pltpu.VMEM((blocks, rows, columns), half),
            pltpu.VMEM((seqs, chips, rows, columns), half),
            pltpu.VMEM((seqs, chips, rows, columns), half),
            pltpu.VMEM((chips, rows, columns), half),
            pltpu.VMEM((chips, rows, columns), half),
            pltpu.VMEM((rows, columns), wide),
        ]
    scratch += [
        dma((2, chips)),
        dma((2, chips)),
        dma((2,)),
        dma((2, seqs)),
        dma((2, chips)),
        dma((2, 3, seqs, chips)),
        dma((2, 3, seqs, chips)),
        dma((2, 3, chips)),
        dma((2, max(seqs, 6))),
        dma((3,)),
        dma((2, ctxs)),
    ]
    return pl.pallas_call(
        functools.partial(back_kernel, seqs, chips),
        out_shape=(
            shape((count, width), wide),
            shape(sizes[0], wide),
            shape((width_rows, H * DH), wide),
            shape((width_rows, DH), wide),
            shape((width_rows, DH), wide),
            shape((8, width), wide),
            shape((width_rows, blocks * units), wide),
            shape((width_rows, blocks * units), wide),
        ),
        in_specs=[vmem] * (len(operands) - 1) + [hbm],
        out_specs=(vmem,) * 8,
        scratch_shapes=scratch,
        compiler_params=pltpu.CompilerParams(
            collective_id=4, has_side_effects=True, vmem_limit_bytes=58 * 2**20
        ),
        cost_estimate=pl.CostEstimate(
            flops=8 * count * width * (H + 2) * DH,
            bytes_accessed=200 * 2**20,
            transcendentals=H * count * total,
        ),
        name="back",
    )(*operands)


def per_device(
    inputs,
    positions,
    attention_gain,
    query_weight,
    key_weight,
    value_weight,
    query_gain,
    key_gain,
    output_weight,
    attention_post,
    feedfwd_gain,
    gate_weight,
    up_weight,
    down_weight,
    feedfwd_post,
    cotangent,
):
    seq_total = lax.axis_size("seq")
    ctx_total = lax.axis_size("ctx")
    device_total = seq_total * ctx_total
    token_count = inputs.shape[0]
    width_rows = query_weight.shape[0]
    head_rows = query_gain.shape[0]
    unit_rows = down_weight.shape[0]

    block_number = (positions[:1] // token_count).astype(jnp.bfloat16)
    small = jnp.concatenate(
        [attention_gain, attention_post, feedfwd_gain, feedfwd_post, query_gain, key_gain]
        + [block_number]
    )
    chips = ctx_total // 2
    padded_rows = -(-(width_rows + 1) // 16) * 16
    small_row = jnp.pad(small, (0, (H + 2) * DH - small.shape[0]))[None]
    cosine, sinus = rotary(positions)
    place_wide = positions.astype(jnp.float32)[:, None]
    (
        packets,
        outputs,
        gate_all,
        up_all,
        down_all,
        gain_all,
        places,
        spread,
        queries,
        key_rows,
        query_rot,
        both_rows,
        attended,
        logsum,
        mixed_values,
        residual,
        fed_all,
    ) = front_call(
        seq_total,
        chips,
        inputs,
        query_weight,
        key_weight,
        value_weight,
        small_row,
        output_weight,
        gate_weight,
        up_weight,
        down_weight,
        cosine,
        sinus,
        place_wide,
    )
    block_out, grad_final, fed_back, grad_down, pair_term = feed_call(
        fed_all,
        residual,
        cotangent,
        gain_all,
        gate_all,
        up_all,
        down_all,
        unit_rows,
        seq_total,
        chips,
    )
    (
        input_grad,
        grad_output,
        grad_query,
        grad_key,
        grad_value,
        gains,
        grad_gate,
        grad_up,
    ) = back_call(
        seq_total,
        chips,
        padded_rows,
        output_weight.shape[0],
        width_rows,
        unit_rows,
        fed_back,
        residual,
        mixed_values,
        cotangent,
        inputs,
        spread,
        queries,
        key_rows,
        query_rot,
        both_rows,
        attended,
        logsum,
        outputs.reshape(H * DH, D),
        packets.reshape(-1, (H + 2) * DH),
        grad_final,
        gain_all,
        cosine,
        sinus,
        place_wide,
        places,
        pair_term,
    )
    device = lax.axis_index("seq") * ctx_total + lax.axis_index("ctx")

    def own_gain(row, start, size):
        return lax.dynamic_slice(gains, (row, start + device * size), (1, size))[0]

    return (
        block_out,
        input_grad,
        own_gain(0, 0, width_rows),
        grad_query,
        grad_key,
        grad_value,
        own_gain(4, 0, head_rows),
        own_gain(4, DH, head_rows),
        grad_output,
        own_gain(1, 0, width_rows),
        own_gain(2, 0, width_rows),
        grad_gate,
        grad_up,
        grad_down,
        own_gain(3, 0, width_rows),
    )


def solution(mesh):
    return jax.shard_map(
        per_device,
        mesh=mesh,
        in_specs=(
            P(("seq", "ctx"), None),
            P(("seq", "ctx")),
            P(("seq", "ctx")),
            P(("seq", "ctx"), None),
            P(("seq", "ctx"), None),
            P(("seq", "ctx"), None),
            P(("seq", "ctx")),
            P(("seq", "ctx")),
            P(("seq", "ctx"), None),
            P(("seq", "ctx")),
            P(("seq", "ctx")),
            P(("seq", "ctx"), None),
            P(("seq", "ctx"), None),
            P(("seq", "ctx"), None),
            P(("seq", "ctx")),
            P(("seq", "ctx"), None),
        ),
        out_specs=(
            P(("seq", "ctx"), None),
            P(("seq", "ctx"), None),
            P(("seq", "ctx")),
            P(("seq", "ctx"), None),
            P(("seq", "ctx"), None),
            P(("seq", "ctx"), None),
            P(("seq", "ctx")),
            P(("seq", "ctx")),
            P(("seq", "ctx"), None),
            P(("seq", "ctx")),
            P(("seq", "ctx")),
            P(("seq", "ctx"), None),
            P(("seq", "ctx"), None),
            P(("seq", "ctx"), None),
            P(("seq", "ctx")),
        ),
        check_vma=False,
    )
```

```python
import functools
import math

import jax
import jax.numpy as jnp
from jax import lax
from jax.experimental import pallas as pl
from jax.experimental.pallas import tpu as pltpu
from jax.sharding import PartitionSpec as P

D = 1152
H = 4
DH = 256
FF = 6912


EPSILON = 1e-06
THETA = 1000000.0
GELU_COEF = math.sqrt(2.0 / math.pi)


def rms_factor(values):
    return lax.rsqrt(jnp.mean(values * values, axis=-1, keepdims=True) + EPSILON)


def norm_back(values, factor, gain_vector, upstream):
    scaled = gain_vector * upstream
    cubed = factor * factor * factor
    return factor * scaled - values * cubed * jnp.mean(scaled * values, axis=-1, keepdims=True)


def rotary(places):
    half_width = DH // 2
    exponent = jnp.arange(half_width, dtype=jnp.float32) * (-2.0 / DH)
    frequency = jnp.power(jnp.float32(THETA), exponent)
    angles = places.astype(jnp.float32)[:, None] * frequency[None, :]
    return (jnp.cos(angles), jnp.sin(angles))


def rotate(values, cosine, sinus):
    half_width = values.shape[-1] // 2
    first = values[..., :half_width]
    second = values[..., half_width:]
    return jnp.concatenate(
        [first * cosine - second * sinus, second * cosine + first * sinus], axis=-1
    )


def rotate_back(upstream, cosine, sinus):
    half_width = upstream.shape[-1] // 2
    first = upstream[..., :half_width]
    second = upstream[..., half_width:]
    return jnp.concatenate(
        [first * cosine + second * sinus, second * cosine - first * sinus], axis=-1
    )


def gelu_tanh(values):
    inner = GELU_COEF * (values + 0.044715 * values * values * values)
    return 0.5 * values * (1.0 + jnp.tanh(inner))


def gelu_slope(values):
    inner = GELU_COEF * (values + 0.044715 * values * values * values)
    tangent = jnp.tanh(inner)
    return 0.5 * (1.0 + tangent) + 0.5 * values * (1.0 - tangent * tangent) * GELU_COEF * (
        1.0 + 3.0 * 0.044715 * values * values
    )


def times_right(left_side, right_side):
    return jnp.dot(left_side, right_side, preferred_element_type=jnp.float32)


def times_transposed(left_side, right_side):
    return lax.dot_general(
        left_side, right_side, (((1,), (1,)), ((), ())), preferred_element_type=jnp.float32
    )


def transposed_times(left_side, right_side):
    return lax.dot_general(
        left_side, right_side, (((0,), (0,)), ((), ())), preferred_element_type=jnp.float32
    )


BOTH = ("seq", "ctx")
MESH = pl.DeviceIdType.MESH


def peers():
    seq = lax.axis_index("seq")
    ctx = lax.axis_index("ctx")
    return seq, ctx // 2, lax.rem(ctx, 2)


def greet(seq, place, core, chips):
    barrier = pltpu.get_barrier_semaphore()
    pl.semaphore_signal(
        barrier, inc=1, device_id=(seq, place * 2 + 1 - core), device_id_type=MESH
    )
    for k in range(1, chips):
        other = lax.rem(place + k, chips) * 2 + core
        pl.semaphore_signal(barrier, inc=1, device_id=(seq, other), device_id_type=MESH)
    pl.semaphore_wait(barrier, chips)


def send_to(source, target, send_sem, recv_sem, device):
    return pltpu.make_async_remote_copy(
        src_ref=source,
        dst_ref=target,
        send_sem=send_sem,
        recv_sem=recv_sem,
        device_id=device,
        device_id_type=MESH,
    )


def plane_of(seq):
    return seq + 1 - 2 * lax.rem(seq, 2), lax.rem(seq + 2, 4)


def slab_sum(seqs, ctx, seq, term, near, middle, part_of, slab_sems, own_sems):
    square = seqs == 4
    beside, across = plane_of(seq)
    low, high = part_of(0), part_of(1)

    def copy(j):
        if not square:
            row = lax.rem(seq + j, seqs)
            origin, goal, target = term.at[row], near.at[j], row
        elif j == 0:
            origin, goal, target = term.at[3 - seq, low], middle.at[0, low], beside
        elif j == 1:
            origin, goal, target = term.at[3 - seq, high], middle.at[0, high], across
        elif j == 2:
            origin, goal, target = term.at[across, high], near.at[2, high], across
        elif j == 3:
            origin, goal, target = term.at[beside, low], near.at[1, low], beside
        elif j == 4:
            origin, goal, target = middle.at[1, low], near.at[2, low], across
        else:
            origin, goal, target = middle.at[1, high], near.at[1, high], beside
        return send_to(origin, goal, slab_sems.at[0, j], slab_sems.at[1, j], (target, ctx))

    def own():
        return pltpu.make_async_copy(term.at[seq], near.at[0], own_sems.at[0])

    def between(half):
        part = part_of(half)
        row = across if half == 0 else beside
        return pltpu.make_async_copy(
            term.at[row, part], middle.at[1, part], own_sems.at[1 + half]
        )

    def start():
        for j in range(2) if square else range(1, seqs):
            copy(j).start()
        own().start()
        if square:
            between(0).start()
            between(1).start()

    def rest():
        if square:
            copy(2).start()
            copy(3).start()

    def relay():
        if square:
            for half in range(2):
                part = part_of(half)
                between(half).wait()
                copy(half).wait_recv()
                middle[1, part] = (
                    middle[1, part].astype(jnp.float32) + middle[0, part].astype(jnp.float32)
                ).astype(jnp.bfloat16)
                copy(4 + half).start()

    def finish():
        own().wait()
        for j in range(2, 6) if square else range(1, seqs):
            copy(j).wait_recv()

    def drain():
        for j in range(6) if square else range(1, seqs):
            copy(j).wait_send()

    return start, rest, relay, finish, drain


def feed_kernel(
    seqs,
    chips,
    fed_all,
    residual_ref,
    cot_ref,
    gain_ref,
    gate_ref,
    up_ref,
    down_ref,
    block_ref,
    grad_final_ref,
    fed_back_ref,
    grad_down_ref,
    grad_pair_ref,
    hidden_ref,
    gate_back_ref,
    up_back_ref,
    back_all,
    gate_values,
    up_values,
    part,
    hidden_back,
    own,
    grad_part,
    down_term,
    down_near,
    down_middle,
    to_sibling,
    from_sibling,
    to_chip,
    from_chip,
    gather_sems,
    forward_sems,
    sibling_sems,
    chip_sems,
    slab_sems,
    own_sems,
):
    seq, place, core = peers()
    ctx = place * 2 + core
    sibling = (seq, place * 2 + 1 - core)
    count = residual_ref.shape[0]
    pair_count = 2 * count
    chunk = min(64, pair_count)
    slab = down_near.shape[1]
    barrier = pltpu.get_barrier_semaphore()
    pl.semaphore_signal(barrier, inc=1, device_id=sibling, device_id_type=MESH)
    for k in range(1, chips):
        other = lax.rem(place + k, chips) * 2 + core
        pl.semaphore_signal(barrier, inc=1, device_id=(seq, other), device_id_type=MESH)
    for j in range(1, seqs):
        pl.semaphore_signal(
            barrier, inc=1, device_id=(lax.rem(seq + j, seqs), ctx), device_id_type=MESH
        )
    start_down, rest_down, relay_down, finish_down, drain_down = slab_sum(
        seqs,
        ctx,
        seq,
        down_term,
        down_near,
        down_middle,
        lambda half: pl.ds(half * (slab // 2), slab // 2),
        slab_sems,
        own_sems,
    )

    def rows_of(chip, which):
        return pl.ds(pl.multiple_of((chip * 2 + which) * count, count), count)

    def pair_of(chip):
        return pl.ds(pl.multiple_of(chip * pair_count, pair_count), pair_count)

    mine = rows_of(place, core)

    def line_copy(side, d):
        sign = 1 - 2 * side
        block = back_all.at[rows_of(place - sign * (d - 1), core)]
        return send_to(
            block,
            block,
            gather_sems.at[0, side, d],
            gather_sems.at[1, side, d],
            (seq, (place + sign) * 2 + core),
        )

    def pass_copy(side, d):
        sign = 1 - 2 * side
        block = back_all.at[rows_of(place - sign * d, core)]
        return send_to(
            block, block, forward_sems.at[0, side, d], forward_sems.at[1, side, d], sibling
        )

    def comes(side, d):
        return place - d >= 0 if side == 0 else place + d < chips

    def goes(side, d):
        if side == 0:
            return jnp.logical_and(place + 1 < chips, place - (d - 1) >= 0)
        return jnp.logical_and(place - 1 >= 0, place + (d - 1) < chips)

    def relay_line(d):
        for side in range(2):

            @pl.when(comes(side, d))
            def _():
                line_copy(side, d).wait_recv()
                pass_copy(side, d).start()

            @pl.when(jnp.logical_and(comes(side, d), goes(side, d + 1)))
            def _():
                line_copy(side, d + 1).start()

    def sibling_copy(index, k):
        return send_to(
            to_sibling.at[k],
            from_sibling.at[index, k],
            sibling_sems.at[0, index, k],
            sibling_sems.at[1, index, k],
            sibling,
        )

    def chip_copy(index, k):
        chip = lax.rem(place - k + chips, chips)
        return send_to(
            to_chip.at[k],
            from_chip.at[index, k],
            chip_sems.at[0, index, k],
            chip_sems.at[1, index, k],
            (seq, chip * 2 + core),
        )

    def pass_part(index, k):
        other_rows = pl.ds(pl.multiple_of((1 - core) * count, count), count)
        own_rows = pl.ds(pl.multiple_of(core * count, count), count)
        to_sibling[k] = part[other_rows, :].astype(jnp.bfloat16)
        sibling_copy(index, k).start()
        sibling_copy(index, k).wait_recv()
        total = part[own_rows, :] + from_sibling[index, k].astype(jnp.float32)

        @pl.when(k == 0)
        def _():
            own[...] = total

        @pl.when(k > 0)
        def _():
            to_chip[k] = total.astype(jnp.bfloat16)
            chip_copy(index, k).start()

    def collect(index):
        for k in range(1, chips):
            chip_copy(index, k).wait_recv()
            own[...] += from_chip[index, k].astype(jnp.float32)
        for k in range(chips):
            sibling_copy(index, k).wait_send()
        for k in range(1, chips):
            chip_copy(index, k).wait_send()

    def forward_step(i, carry):
        k = lax.rem(i + 1, chips)
        rows = pair_of(lax.rem(place - k + chips, chips))
        block = fed_all[rows, :]
        gate_values[rows, :] = times_right(block, gate_ref[...])
        up_values[rows, :] = times_right(block, up_ref[...])

        def gated(j, carry):
            here = pl.ds(pl.multiple_of(rows.start + j * chunk, chunk), chunk)
            hidden_ref[here, :] = (gelu_tanh(gate_values[here, :]) * up_values[here, :]).astype(
                jnp.bfloat16
            )
            return carry

        lax.fori_loop(0, pair_count // chunk, gated, 0)
        part[...] = times_right(hidden_ref[rows, :], down_ref[...])

        @pl.when(i == 0)
        def _():
            pl.semaphore_wait(barrier, chips + seqs - 1)

        pass_part(0, k)
        return carry

    def backward_work(k):
        rows = pair_of(lax.rem(place - k + chips, chips))
        hidden_back[...] = times_transposed(back_all[rows, :], down_ref[...])

        def gated(j, carry):
            here = pl.ds(pl.multiple_of(rows.start + j * chunk, chunk), chunk)
            local = pl.ds(pl.multiple_of(j * chunk, chunk), chunk)
            gate_now = gate_values[here, :]
            upper = hidden_back[local, :]
            gate_back_ref[here, :] = (upper * up_values[here, :] * gelu_slope(gate_now)).astype(
                jnp.bfloat16
            )
            up_back_ref[here, :] = (upper * gelu_tanh(gate_now)).astype(jnp.bfloat16)
            return carry

        lax.fori_loop(0, pair_count // chunk, gated, 0)
        part[...] = times_transposed(gate_back_ref[rows, :], gate_ref[...])
        part[...] += times_transposed(up_back_ref[rows, :], up_ref[...])
        pass_part(1, k)

    def backward_step(d, carry):
        @pl.when(jnp.logical_or(d == 1, place - (d - 1) < 0))
        def _():
            relay_line(d)

        @pl.when(d == chips - 1)
        def _():
            for side in range(2):

                @pl.when(comes(side, d))
                def _():
                    pass_copy(side, d).wait_recv()

            for s in range(seqs):
                down_term[s] = transposed_times(
                    hidden_ref[:, s * slab : (s + 1) * slab], back_all[...]
                ).astype(jnp.bfloat16)
            start_down()
            rest_down()

        @pl.when(comes(0, d))
        def _():
            @pl.when(d < chips - 1)
            def _():
                pass_copy(0, d).wait_recv()

            backward_work(d)

        @pl.when(jnp.logical_and(comes(0, d), d < chips - 1))
        def _():
            relay_line(d + 1)

        @pl.when(comes(1, d))
        def _():
            @pl.when(d < chips - 1)
            def _():
                pass_copy(1, d).wait_recv()

            backward_work(chips - d)

        return carry

    lax.fori_loop(0, chips, forward_step, 0)
    collect(0)
    down_values = own[...]
    down_factor = rms_factor(down_values)
    gain_final = gain_ref[3:4, :]
    cot_wide = cot_ref[...].astype(jnp.float32)
    back_all[mine, :] = norm_back(down_values, down_factor, gain_final, cot_wide).astype(
        jnp.bfloat16
    )
    for side in range(2):

        @pl.when(goes(side, 1))
        def _():
            line_copy(side, 1).start()

    pass_copy(0, 0).start()
    block_ref[...] = (residual_ref[...] + down_values * down_factor * gain_final).astype(
        jnp.bfloat16
    )
    grad_final_ref[...] = jnp.sum(cot_wide * down_values * down_factor, axis=0, keepdims=True)
    pass_copy(0, 0).wait_recv()
    backward_work(0)
    lax.fori_loop(1, chips, backward_step, 0)
    relay_down()
    slabs, _, slab_rows, _ = grad_pair_ref.shape
    tall = grad_part.shape[0]
    for b, source in ((0, gate_back_ref), (1, up_back_ref)):
        for c in range(slabs * slab_rows // tall):
            grad_part[...] = transposed_times(
                fed_all[:, c * tall : (c + 1) * tall], source[...]
            )
            for s in range(slabs):
                low = max(s * slab_rows, c * tall)
                high = min((s + 1) * slab_rows, (c + 1) * tall)
                if low < high:
                    grad_pair_ref[s, b, low - s * slab_rows : high - s * slab_rows] = grad_part[
                        low - c * tall : high - c * tall, :
                    ].astype(jnp.bfloat16)
    collect(1)
    fed_back_ref[...] = own[...]
    finish_down()
    total = down_near[0].astype(jnp.float32)
    for j in (1, 2) if seqs == 4 else range(1, seqs):
        total = total + down_near[j].astype(jnp.float32)
    grad_down_ref[...] = total[0 : grad_down_ref.shape[0]]
    drain_down()
    pass_copy(0, 0).wait_send()
    for d in range(1, chips):
        for side in range(2):

            @pl.when(comes(side, d))
            def _():
                pass_copy(side, d).wait_send()

            @pl.when(goes(side, d))
            def _():
                line_copy(side, d).wait_send()


def feed_call(fed, residual, cot, gain, gate, up, down, down_rows, seqs, chips):
    count, width = residual.shape
    total = 2 * chips * count
    units = down.shape[0]
    slab = units // seqs
    wide = jnp.float32
    half = jnp.bfloat16
    dma = pltpu.SemaphoreType.DMA
    shape = jax.ShapeDtypeStruct
    vmem = pl.BlockSpec(memory_space=pltpu.VMEM)
    near_slabs, middle_slabs = (3, 2) if seqs == 4 else (seqs, 1)
    return pl.pallas_call(
        functools.partial(feed_kernel, seqs, chips),
        out_shape=(
            shape((count, width), half),
            shape((1, width), wide),
            shape((count, width), wide),
            shape((down_rows, width), wide),
            shape((seqs, 2, width // seqs, units), half),
        ),
        in_specs=[vmem] * 7,
        out_specs=(vmem,) * 5,
        scratch_shapes=[
            pltpu.VMEM((total, units), half),
            pltpu.VMEM((total, units), half),
            pltpu.VMEM((total, units), half),
            pltpu.VMEM((total, width), half),
            pltpu.VMEM((total, units), wide),
            pltpu.VMEM((total, units), wide),
            pltpu.VMEM((2 * count, width), wide),
            pltpu.VMEM((2 * count, units), wide),
            pltpu.VMEM((count, width), wide),
            pltpu.VMEM((width // 3, units), wide),
            pltpu.VMEM((seqs, slab, width), half),
            pltpu.VMEM((near_slabs, slab, width), half),
            pltpu.VMEM((middle_slabs, slab, width), half),
            pltpu.VMEM((chips, count, width), half),
            pltpu.VMEM((2, chips, count, width), half),
            pltpu.VMEM((chips, count, width), half),
            pltpu.VMEM((2, chips, count, width), half),
            dma((2, 2, chips + 1)),
            dma((2, 2, chips + 1)),
            dma((2, 2, chips)),
            dma((2, 2, chips)),
            dma((2, max(seqs, 6))),
            dma((3,)),
        ],
        compiler_params=pltpu.CompilerParams(
            collective_id=1, has_side_effects=True, vmem_limit_bytes=58 * 2**20
        ),
        name="feed",
    )(fed, residual, cot, gain, gate, up, down)


def front_kernel(
    seqs,
    chips,
    inputs_ref,
    query_ref,
    key_ref,
    value_ref,
    small_ref,
    output_ref,
    gate_ref,
    up_ref,
    down_ref,
    cosine_ref,
    sinus_ref,
    place_ref,
    packets,
    outputs,
    gate_all,
    up_all,
    down_all,
    gains,
    places,
    spread_ref,
    queries_ref,
    key_rows_ref,
    query_rot_ref,
    both_ref,
    attended_ref,
    logsum_ref,
    mixed_ref,
    residual_ref,
    fed_all,
    wide_packet,
    own_packet,
    own_down,
    to_ctx,
    from_ctx,
    joined,
    packed,
    spread,
    spread_gain,
    own_pair,
    line_sems,
    plane_sems,
    core_sems,
    swap_sems,
    slab_sems,
    gather_sems,
    forward_sems,
    fed_sems,
    pass_sems,
):
    seq, place, core = peers()
    ctx = place * 2 + core
    sibling = (seq, place * 2 + 1 - core)
    ctxs = 2 * chips
    blocks = seqs * ctxs
    count, width = inputs_ref.shape
    rows = gate_ref.shape[0]
    head_rows = DH // blocks
    units = down_ref.shape[0]
    slab = own_down.shape[0]
    square = seqs == 4
    beside = seq + 1 - 2 * lax.rem(seq, 2)
    across = lax.rem(seq + 2, 4)
    direct = (1, 2) if square else range(1, seqs)
    barrier = pltpu.get_barrier_semaphore()
    for k in range(1, ctxs):
        pl.semaphore_signal(
            barrier, inc=1, device_id=(seq, lax.rem(ctx + k, ctxs)), device_id_type=MESH
        )
    for j in range(1, seqs):
        pl.semaphore_signal(
            barrier, inc=1, device_id=(lax.rem(seq + j, seqs), ctx), device_id_type=MESH
        )

    def index_of(row, chip, which):
        return row * ctxs + chip * 2 + which

    both = ((own_packet, packets), (output_ref, outputs))

    def line_copy(b, k):
        own, everything = both[b]
        chip = lax.rem(place + k, chips)
        return send_to(
            own,
            everything.at[index_of(seq, place, core)],
            line_sems.at[0, b, k],
            line_sems.at[1, b, k],
            (seq, chip * 2 + core),
        )

    def plane_copy(b, j, k):
        everything = both[b][1]
        chip = lax.rem(place - k + chips, chips)
        row, target = seq, lax.rem(seq + j, seqs)
        if square:
            even = lax.rem(jnp.int32(k), 2) == 0
            if j == 3:
                row = jnp.where(even, beside, across)
                target = jnp.where(even, across, beside)
            else:
                target = beside if j == 1 else across
        block = everything.at[index_of(row, chip, core)]
        return send_to(
            block,
            block,
            plane_sems.at[0, b, j, k],
            plane_sems.at[1, b, j, k],
            (target, ctx),
        )

    def core_copy(b, j, k):
        everything = both[b][1]
        row = (seq, beside, across, 3 - seq)[j] if square else lax.rem(seq - j + seqs, seqs)
        chip = lax.rem(place - k + chips, chips)
        block = everything.at[index_of(row, chip, core)]
        return send_to(
            block, block, core_sems.at[0, b, j, k], core_sems.at[1, b, j, k], sibling
        )

    def swap_copy(k):
        target = lax.rem(ctx + k, ctxs)
        return send_to(
            to_ctx.at[target],
            from_ctx.at[ctx],
            swap_sems.at[0, k],
            swap_sems.at[1, k],
            (seq, target),
        )

    def slab_copy(which, j):
        height = slab if which == 0 else ctxs * rows
        everything = (down_all, gate_all, up_all)[which]
        first, size, target = seq * height, height, lax.rem(seq + j, seqs)
        if square:
            half = height // 2
            if j == 0:
                target = beside
            elif j == 1:
                target = across
            elif j == 2:
                first, size, target = beside * height, half, across
            else:
                first, size, target = across * height + half, half, beside
            first = pl.multiple_of(first, half)
        else:
            first = pl.multiple_of(first, height)
        here = everything.at[pl.ds(first, size)]
        return send_to(
            here,
            here,
            slab_sems.at[0, which, j],
            slab_sems.at[1, which, j],
            (target, ctx),
        )

    def start_slab(which):
        for j in (0, 1) if square else range(1, seqs):
            slab_copy(which, j).start()

    def relay_slab(which):
        if square:
            slab_copy(which, 0).wait_recv()
            slab_copy(which, 2).start()
            slab_copy(which, 1).wait_recv()
            slab_copy(which, 3).start()

    def finish_slab(which):
        if square:
            slab_copy(which, 0).wait_send()
            slab_copy(which, 1).wait_send()
            slab_copy(which, 2).wait()
            slab_copy(which, 3).wait()
        else:
            for j in range(1, seqs):
                slab_copy(which, j).wait()

    def rows_of(chip):
        return pl.ds(pl.multiple_of((chip * 2 + core) * count, count), count)

    def gather_copy(k):
        chip = lax.rem(place + k, chips)
        return send_to(
            own_pair,
            both_ref.at[rows_of(place)],
            gather_sems.at[0, k],
            gather_sems.at[1, k],
            (seq, chip * 2 + core),
        )

    def forward_copy(k):
        chip = lax.rem(place - k + chips, chips)
        block = both_ref.at[rows_of(chip)]
        return send_to(block, block, forward_sems.at[0, k], forward_sems.at[1, k], sibling)

    def fed_copy(k):
        chip = lax.rem(place + k, chips)
        block = fed_all.at[rows_of(place)]
        return send_to(
            block, block, fed_sems.at[0, k], fed_sems.at[1, k], (seq, chip * 2 + core)
        )

    def pass_copy(k):
        chip = lax.rem(place - k + chips, chips)
        block = fed_all.at[rows_of(chip)]
        return send_to(block, block, pass_sems.at[0, k], pass_sems.at[1, k], sibling)

    def start_own(b):
        own, everything = both[b]
        for k in range(1, chips):
            line_copy(b, k).start()
        everything[index_of(seq, place, core)] = own[...]
        core_copy(b, 0, 0).start()

    def start_plane(b):
        for j in direct:
            plane_copy(b, j, 0).start()

    def line_step(b):
        def one(k, carry):
            line_copy(b, k).wait_recv()
            for j in direct:
                plane_copy(b, j, k).start()
            core_copy(b, 0, k).start()
            return carry

        lax.fori_loop(1, chips, one, 0)

    def plane_step(b):
        def one(k, carry):
            for j in direct:
                plane_copy(b, j, k).wait_recv()
            if square:
                plane_copy(b, 3, k).start()
            for j in direct:
                core_copy(b, j, k).start()
            return carry

        lax.fori_loop(0, chips, one, 0)

    def relay_step(b):
        def one(k, carry):
            plane_copy(b, 3, k).wait_recv()
            core_copy(b, 3, k).start()
            return carry

        if square:
            lax.fori_loop(0, chips, one, 0)

    def core_step(b):
        def one(k, carry):
            for j in range(seqs):
                core_copy(b, j, k).wait_recv()
            return carry

        lax.fori_loop(0, chips, one, 0)

    def drain(b):
        def one(k, carry):
            for j in range(seqs):
                core_copy(b, j, k).wait_send()
                if j > 0:
                    plane_copy(b, j, k).wait_send()
            return carry

        lax.fori_loop(0, chips, one, 0)
        for k in range(1, chips):
            line_copy(b, k).wait_send()

    wide_packet[...] = jnp.zeros_like(wide_packet)
    wide_packet[0:rows, 0 : H * DH] = query_ref[...].astype(jnp.float32)
    wide_packet[0:rows, H * DH : (H + 1) * DH] = key_ref[...].astype(jnp.float32)
    wide_packet[0:rows, (H + 1) * DH :] = value_ref[...].astype(jnp.float32)
    for g in range(4):
        wide_packet[rows : rows + 1, g * rows : (g + 1) * rows] = small_ref[g : g + 1, :rows]
    for g in range(2):
        first = 4 * rows + g * head_rows
        wide_packet[rows : rows + 1, first : first + head_rows] = small_ref[
            4 + g : 5 + g, :head_rows
        ]
    first = 4 * rows + 2 * head_rows
    wide_packet[rows : rows + 1, first : first + 1] = small_ref[6:7, 0:1]
    own_packet[...] = wide_packet[...].astype(jnp.bfloat16)
    own_down[...] = jnp.zeros_like(own_down)
    own_down[0:units, :] = down_ref[...].astype(jnp.float32)
    down_all[pl.ds(pl.multiple_of(seq * slab, slab), slab), :] = own_down[...].astype(
        jnp.bfloat16
    )
    pl.semaphore_wait(barrier, ctxs + seqs - 2)
    start_own(0)
    start_plane(0)
    start_slab(0)

    joined[...] = jnp.zeros_like(joined)
    for c in range(ctxs):
        for b, source in ((0, gate_ref), (1, up_ref)):
            for s in range(seqs):
                first = (s * ctxs + c) * units
                low = first // 128 * 128
                high = min(-(-(first + units) // 128) * 128, gate_ref.shape[1])
                wide = source[:, low:high].astype(jnp.float32)
                joined[b * rows : (b + 1) * rows, s * slab : s * slab + units] = wide[
                    :, first - low : first - low + units
                ]
        to_ctx[c] = joined[...].astype(jnp.bfloat16)
    line_step(0)
    for k in range(1, ctxs):
        swap_copy(k).start()
    from_ctx[ctx] = to_ctx[ctx]

    input_wide = inputs_ref[...].astype(jnp.float32)
    scaled = input_wide * rms_factor(input_wide)
    spread[...] = jnp.zeros_like(spread)
    step = packets.shape[1]
    for i in range(blocks):
        spread[:, i * step : i * step + rows] = scaled[:, i * rows : (i + 1) * rows]
    plane_step(0)
    relay_step(0)
    start_own(1)
    start_plane(1)
    core_step(0)

    gains[...] = jnp.zeros_like(gains)
    spread_gain[...] = jnp.zeros_like(spread_gain)
    base = rows // 8 * 8
    for i in range(blocks):
        line = packets[i, base:, :256].astype(jnp.float32)[rows - base : rows - base + 1]
        for g in range(4):
            gains[g : g + 1, i * rows : (i + 1) * rows] = line[:, g * rows : (g + 1) * rows]
        spread_gain[0:1, i * step : i * step + rows] = line[:, 0:rows]
        for g in range(2):
            first = 4 * rows + g * head_rows
            here = g * DH + i * head_rows
            gains[4:5, here : here + head_rows] = line[:, first : first + head_rows]
    number_at = 4 * rows + 2 * head_rows
    offsets = lax.broadcasted_iota(jnp.int32, (1, count), 1).astype(jnp.float32)
    for c in range(ctxs):
        line = packets[seq * ctxs + c, base:, :256].astype(jnp.float32)
        number = line[rows - base : rows - base + 1, number_at : number_at + 1]
        places[:, c * count : (c + 1) * count] = number * count + offsets
    spread_ref[...] = (spread[...] * spread_gain[0:1, :]).astype(jnp.bfloat16)
    joint = packets.reshape(blocks * step, (H + 2) * DH)
    cosine = cosine_ref[...]
    sinus = sinus_ref[...]
    pair = times_right(spread_ref[...], joint[:, H * DH :])
    key_rows = pair[:, :DH]
    key_rows_ref[...] = key_rows
    key_rot = rotate(key_rows * rms_factor(key_rows) * gains[4:5, DH : 2 * DH], cosine, sinus)
    own_pair[:, :DH] = key_rot.astype(jnp.bfloat16)
    own_pair[:, DH:] = pair[:, DH:].astype(jnp.bfloat16)
    both_ref[rows_of(place), :] = own_pair[...]
    for k in range(1, chips):
        gather_copy(k).start()
    forward_copy(0).start()
    for k in range(1, ctxs):
        swap_copy(k).wait_recv()
    for c in range(ctxs):
        joined[...] = from_ctx[c].astype(jnp.float32)
        for b in range(2):
            packed[b, c * rows : (c + 1) * rows, :] = joined[b * rows : (b + 1) * rows, :]
    height = ctxs * rows
    here = pl.ds(pl.multiple_of(seq * height, height), height)
    gate_all[here, :] = packed[0].astype(jnp.bfloat16)
    up_all[here, :] = packed[1].astype(jnp.bfloat16)
    start_slab(1)
    start_slab(2)
    relay_slab(0)
    line_step(1)
    for h in range(H):
        mine = slice(h * count, (h + 1) * count)
        queries = times_right(spread_ref[...], joint[:, h * DH : (h + 1) * DH])
        queries_ref[mine, :] = queries
        query_rot_ref[mine, :] = rotate(
            queries * rms_factor(queries) * gains[4:5, 0:DH], cosine, sinus
        ).astype(jnp.bfloat16)
    plane_step(1)
    for k in range(1, chips):
        gather_copy(k).wait_recv()
        forward_copy(k).start()
    for k in range(chips):
        forward_copy(k).wait_recv()
    scaling = 1.0 / math.sqrt(DH)

    def head(h, carry):
        mine = pl.ds(pl.multiple_of(h * count, count), count)
        columns = pl.ds(pl.multiple_of(h * DH, DH), DH)
        allowed = places[...] <= place_ref[...]
        scores = times_transposed(query_rot_ref[mine, :], both_ref[:, :DH]) * scaling
        expscore = jnp.where(allowed, jnp.exp(scores), 0.0)
        weight_sum = jnp.sum(expscore, axis=-1, keepdims=True)
        summed = times_right(expscore.astype(jnp.bfloat16), both_ref[:, DH:])
        attended_ref[:, columns] = (summed / weight_sum).astype(jnp.bfloat16)
        logsum_ref[mine, :] = jnp.log(weight_sum)
        return carry

    lax.fori_loop(0, H, head, 0)
    relay_slab(1)
    relay_step(1)
    core_step(1)
    mixed_ref[...] = times_right(attended_ref[...], outputs.reshape(H * DH, width)[...])
    mixed = mixed_ref[...]
    residual = inputs_ref[...].astype(jnp.float32) + mixed * rms_factor(mixed) * gains[1:2, :]
    residual_ref[...] = residual
    fed_all[rows_of(place), :] = (residual * rms_factor(residual) * gains[2:3, :]).astype(
        jnp.bfloat16
    )
    for k in range(1, chips):
        fed_copy(k).start()
    pass_copy(0).start()
    for b in range(2):
        drain(b)
    for k in range(1, ctxs):
        swap_copy(k).wait_send()
    for k in range(chips):
        forward_copy(k).wait_send()
    for k in range(1, chips):
        gather_copy(k).wait_send()
    relay_slab(2)
    for k in range(1, chips):
        fed_copy(k).wait_recv()
        pass_copy(k).start()
    for which in range(3):
        finish_slab(which)
    for k in range(chips):
        pass_copy(k).wait()
    for k in range(1, chips):
        fed_copy(k).wait_send()


def front_call(seqs, chips, *operands):
    inputs, query_weight = operands[:2]
    output, gate, _, down = operands[5:9]
    count, width = inputs.shape
    wide = jnp.float32
    half = jnp.bfloat16
    dma = pltpu.SemaphoreType.DMA
    shape = jax.ShapeDtypeStruct
    vmem = pl.BlockSpec(memory_space=pltpu.VMEM)
    ctxs = 2 * chips
    total = ctxs * count
    blocks = seqs * ctxs
    rows = gate.shape[0]
    packet_rows = -(-(rows + 1) // 16) * 16
    joint_width = (H + 2) * DH
    slab = -(-down.shape[0] // 16) * 16
    unit_count = seqs * slab
    padded = -(-2 * rows // 16) * 16
    return pl.pallas_call(
        functools.partial(front_kernel, seqs, chips),
        out_shape=(
            shape((blocks, packet_rows, joint_width), half),
            shape((blocks,) + output.shape, half),
            shape((width, unit_count), half),
            shape((width, unit_count), half),
            shape((unit_count, width), half),
            shape((8, width), wide),
            shape((1, total), wide),
            shape((count, blocks * packet_rows), half),
            shape((H * count, DH), wide),
            shape((count, DH), wide),
            shape((H * count, DH), half),
            shape((total, 2 * DH), half),
            shape((count, H * DH), half),
            shape((H * count, 1), wide),
            shape((count, width), wide),
            shape((count, width), wide),
            shape((total, width), half),
        ),
        in_specs=[vmem] * len(operands),
        out_specs=(vmem,) * 17,
        scratch_shapes=[
            pltpu.VMEM((packet_rows, joint_width), wide),
            pltpu.VMEM((packet_rows, joint_width), half),
            pltpu.VMEM((slab, width), wide),
            pltpu.VMEM((ctxs, padded, unit_count), half),
            pltpu.VMEM((ctxs, padded, unit_count), half),
            pltpu.VMEM((padded, unit_count), wide),
            pltpu.VMEM((2, ctxs * rows, unit_count), wide),
            pltpu.VMEM((count, blocks * packet_rows), wide),
            pltpu.VMEM((8, blocks * packet_rows), wide),
            pltpu.VMEM((count, 2 * DH), half),
            dma((2, 2, chips)),
            dma((2, 2, seqs, chips)),
            dma((2, 2, seqs, chips)),
            dma((2, ctxs)),
            dma((2, 3, max(seqs, 4))),
            dma((2, chips)),
            dma((2, chips)),
            dma((2, chips)),
            dma((2, chips)),
        ],
        compiler_params=pltpu.CompilerParams(
            collective_id=2, has_side_effects=True, vmem_limit_bytes=58 * 2**20
        ),
        name="front",
    )(*operands)


def back_kernel(
    seqs,
    chips,
    fed_back_ref,
    residual_ref,
    mixed_ref,
    cot_ref,
    inputs_ref,
    spread_ref,
    queries_ref,
    key_rows_ref,
    query_rot_ref,
    both_ref,
    attended_ref,
    logsum_ref,
    output_ref,
    joint_ref,
    grad_final_ref,
    gain_all_ref,
    cosine_ref,
    sinus_ref,
    place_ref,
    places_ref,
    pair_term_ref,
    input_grad_ref,
    grad_output_ref,
    grad_query_ref,
    grad_key_ref,
    grad_value_ref,
    gains_ref,
    grad_gate_ref,
    grad_up_ref,
    mixed_back,
    attended_back,
    upper_round,
    probs,
    score_back,
    normed_wide,
    input_wide_back,
    pair_part,
    pair_to_sibling,
    pair_from_sibling,
    pair_to_chip,
    pair_from_chip,
    joint_back,
    gain_term,
    gain_near,
    gain_chip,
    gain_plane,
    gain_row,
    gain_line,
    gate_near,
    gate_middle,
    gate_total,
    to_ctx,
    from_ctx,
    joined,
    *rest,
):
    seq, place, core = peers()
    ctx = place * 2 + core
    ctxs = 2 * chips
    sibling = (seq, place * 2 + 1 - core)
    count = cot_ref.shape[0]
    buffers = [rest[6 * b : 6 * b + 6] for b in range(3)]
    (
        pair_sibling_sems,
        pair_chip_sems,
        gain_near_sems,
        gain_plane_sems,
        gain_line_sems,
        near_sems,
        plane_sems,
        line_sems,
        slab_sems,
        own_sems,
        swap_sems,
    ) = rest[18:]
    barrier = pltpu.get_barrier_semaphore()
    for k in range(1, ctxs):
        pl.semaphore_signal(
            barrier, inc=1, device_id=(seq, lax.rem(ctx + k, ctxs)), device_id_type=MESH
        )
    for j in range(1, seqs):
        pl.semaphore_signal(
            barrier, inc=1, device_id=(lax.rem(seq + j, seqs), ctx), device_id_type=MESH
        )
    pl.semaphore_wait(barrier, ctxs + seqs - 2)
    rows_own, gate_width = grad_gate_ref.shape
    units = gate_width // (seqs * ctxs)
    slab = gate_near.shape[-1] // seqs

    square = seqs == 4
    beside = seq + 1 - 2 * lax.rem(seq, 2)
    across = lax.rem(seq + 2, 4)
    direct = (1, 2) if square else range(1, seqs)

    start_slab, rest_slab, relay_slab, finish_slab, drain_slab = slab_sum(
        seqs,
        ctx,
        seq,
        pair_term_ref,
        gate_near,
        gate_middle,
        lambda half: half,
        slab_sems,
        own_sems,
    )

    def swap_copy(k):
        target = lax.rem(ctx + k, ctxs)
        return send_to(
            to_ctx.at[target],
            from_ctx.at[ctx],
            swap_sems.at[0, k],
            swap_sems.at[1, k],
            (seq, target),
        )

    start_slab()

    def block_of(j, k, which):
        row = (seq, beside, across, 3 - seq)[j] if square else lax.rem(seq + j, seqs)
        chip = lax.rem(place + k, chips)
        return row * ctxs + chip * 2 + which

    def near_copy(b, j, k):
        term, near = buffers[b][:2]
        return send_to(
            term.at[block_of(j, k, 1 - core)],
            near.at[j, k],
            near_sems.at[0, b, j, k],
            near_sems.at[1, b, j, k],
            sibling,
        )

    def plane_copy(b, j, k):
        near, plane_from = buffers[b][1:3]
        target = lax.rem(seq + j, seqs)
        if square:
            even = lax.rem(jnp.int32(k), 2) == 0
            target = (seq, beside, across, jnp.where(even, beside, across))[j]
        return send_to(
            near.at[j, k],
            plane_from.at[j, k],
            plane_sems.at[0, b, j, k],
            plane_sems.at[1, b, j, k],
            (target, ctx),
        )

    def line_copy(b, k):
        line_to, line_from = buffers[b][3:5]
        return send_to(
            line_to.at[k],
            line_from.at[k],
            line_sems.at[0, b, k],
            line_sems.at[1, b, k],
            (seq, lax.rem(place + k, chips) * 2 + core),
        )

    def start_near(b):
        def one(k, carry):
            for j in range(seqs):
                near_copy(b, j, lax.rem(k + 1, chips)).start()
            return carry

        lax.fori_loop(0, chips, one, 0)

    def run_plane(b):
        term, near = buffers[b][:2]

        def one(i, carry):
            k = lax.rem(i + 1, chips)
            for j in range(seqs - 1, -1, -1):
                near_copy(b, j, k).wait_recv()
                near[j, k] = (
                    term[block_of(j, k, core)].astype(jnp.float32)
                    + near[j, k].astype(jnp.float32)
                ).astype(jnp.bfloat16)
                if j == 3 or (j > 0 and not square):
                    plane_copy(b, j, k).start()
            if square:

                @pl.when(lax.rem(k, 2) == 0)
                def _():
                    plane_copy(b, 1, k).start()

                @pl.when(lax.rem(k, 2) == 1)
                def _():
                    plane_copy(b, 2, k).start()

            return carry

        lax.fori_loop(0, chips, one, 0)

    def relay_plane(b):
        _, near, plane_from = buffers[b][:3]

        def one(i, carry):
            k = lax.rem(i + 1, chips)
            plane_copy(b, 3, k).wait_recv()

            def add(j):
                near[j, k] = (
                    near[j, k].astype(jnp.float32) + plane_from[3, k].astype(jnp.float32)
                ).astype(jnp.bfloat16)
                plane_copy(b, j, k).start()

            @pl.when(lax.rem(k, 2) == 0)
            def _():
                add(2)

            @pl.when(lax.rem(k, 2) == 1)
            def _():
                add(1)

            return carry

        if square:
            lax.fori_loop(0, chips, one, 0)

    def run_line(b):
        _, near, plane_from, line_to, _, own = buffers[b]

        def one(i, carry):
            k = lax.rem(i + 1, chips)
            total = near[0, k].astype(jnp.float32)
            for j in direct:
                plane_copy(b, j, k).wait_recv()
                total = total + plane_from[j, k].astype(jnp.float32)

            @pl.when(k > 0)
            def _():
                line_to[k] = total.astype(jnp.bfloat16)
                line_copy(b, k).start()

            @pl.when(k == 0)
            def _():
                own[...] = total

            return carry

        lax.fori_loop(0, chips, one, 0)

    def finish(b):
        _, _, _, _, line_from, own = buffers[b]
        total = own[...]
        for k in range(1, chips):
            line_copy(b, k).wait_recv()
            total = total + line_from[k].astype(jnp.float32)
        return total

    def drain(b):
        def one(k, carry):
            for j in range(seqs):
                near_copy(b, j, k).wait_send()
                if j > 0:
                    plane_copy(b, j, k).wait_send()
            return carry

        lax.fori_loop(0, chips, one, 0)
        for k in range(1, chips):
            line_copy(b, k).wait_send()

    def pair_rows(chip, which):
        return pl.ds(pl.multiple_of((chip * 2 + which) * count, count), count)

    def pair_sibling_copy(k):
        return send_to(
            pair_to_sibling.at[k],
            pair_from_sibling.at[k],
            pair_sibling_sems.at[0, k],
            pair_sibling_sems.at[1, k],
            sibling,
        )

    def pair_chip_copy(k):
        return send_to(
            pair_to_chip.at[k],
            pair_from_chip.at[k],
            pair_chip_sems.at[0, k],
            pair_chip_sems.at[1, k],
            (seq, lax.rem(place + k, chips) * 2 + core),
        )

    scaling = 1.0 / math.sqrt(DH)
    cosine = cosine_ref[...]
    sinus = sinus_ref[...]
    residual = residual_ref[...]
    residual_factor = rms_factor(residual)
    fed_back = fed_back_ref[...]
    gain_term[...] = jnp.zeros_like(gain_term)
    gain_term[3:4, :] = grad_final_ref[...]
    gain_term[2:3, :] = jnp.sum(fed_back * residual * residual_factor, axis=0, keepdims=True)
    residual_back = cot_ref[...].astype(jnp.float32) + norm_back(
        residual, residual_factor, gain_all_ref[2:3, :], fed_back
    )
    input_grad_ref[...] = residual_back
    mixed = mixed_ref[...]
    mixed_factor = rms_factor(mixed)
    gain_term[1:2, :] = jnp.sum(residual_back * mixed * mixed_factor, axis=0, keepdims=True)
    mixed_back[...] = norm_back(mixed, mixed_factor, gain_all_ref[1:2, :], residual_back).astype(
        jnp.bfloat16
    )
    output_term = buffers[0][0]
    output_rows = output_term.shape[1]
    for h in range(H):
        columns = slice(h * DH, (h + 1) * DH)
        part = transposed_times(attended_ref[:, columns], mixed_back[...])
        each = DH // output_rows
        for i in range(each):
            output_term[h * each + i] = part[i * output_rows : (i + 1) * output_rows].astype(
                jnp.bfloat16
            )
    start_near(0)
    attended_back[...] = times_transposed(mixed_back[...], output_ref[...])

    def head(h, carry):
        rows = pl.ds(pl.multiple_of(h * count, count), count)
        columns = pl.ds(pl.multiple_of(h * DH, DH), DH)
        upper = attended_back[:, columns]
        upper_round[rows, :] = upper.astype(jnp.bfloat16)
        row_delta = jnp.sum(
            upper * attended_ref[:, columns].astype(jnp.float32), axis=-1, keepdims=True
        )
        allowed = places_ref[...] <= place_ref[...]
        scores = times_transposed(query_rot_ref[rows, :], both_ref[:, :DH]) * scaling
        probability = jnp.where(allowed, jnp.exp(scores - logsum_ref[rows, :]), 0.0)
        probs[rows, :] = probability.astype(jnp.bfloat16)
        prob_back = times_transposed(upper_round[rows, :], both_ref[:, DH:])
        score_back[rows, :] = (probability * (prob_back - row_delta) * scaling).astype(
            jnp.bfloat16
        )
        return carry

    rest_slab()
    lax.fori_loop(0, H, head, 0)
    relay_slab()
    pair_part[:, :DH] = transposed_times(score_back[...], query_rot_ref[...])
    pair_part[:, DH:] = transposed_times(probs[...], upper_round[...])
    for i in range(chips):
        k = (i + 1) % chips
        chip = lax.rem(place + k, chips)
        pair_to_sibling[k] = pair_part[pair_rows(chip, 1 - core), :].astype(jnp.bfloat16)
        pair_sibling_copy(k).start()
    run_plane(0)
    for i in range(chips - 1):
        k = i + 1
        chip = lax.rem(place + k, chips)
        pair_sibling_copy(k).wait_recv()
        pair_to_chip[k] = (
            pair_part[pair_rows(chip, core), :] + pair_from_sibling[k].astype(jnp.float32)
        ).astype(jnp.bfloat16)
        pair_chip_copy(k).start()

    gain_query = gain_all_ref[4:5, 0:DH]
    grad_query_gain = jnp.zeros((1, DH), jnp.float32)
    for h in range(H):
        rows = slice(h * count, (h + 1) * count)
        upward = rotate_back(times_right(score_back[rows, :], both_ref[:, :DH]), cosine, sinus)
        queries = queries_ref[rows, :]
        factor = rms_factor(queries)
        grad_query_gain += jnp.sum(upward * queries * factor, axis=0, keepdims=True)
        joint_back[:, h * DH : (h + 1) * DH] = norm_back(
            queries, factor, gain_query, upward
        ).astype(jnp.bfloat16)
    gain_term[4:5, :DH] = grad_query_gain

    def joint_term(b, columns):
        term = buffers[b][0]
        blocks, rows, _ = term.shape
        group = 256 // rows if 256 % rows == 0 else 8
        while blocks % group:
            group -= 1
        wide = group * rows
        for g in range(blocks // group):
            part = transposed_times(
                spread_ref[:, g * wide : (g + 1) * wide], joint_back[:, columns]
            )
            for i in range(group):
                term[g * group + i] = part[i * rows : (i + 1) * rows].astype(jnp.bfloat16)

    joint_term(1, slice(0, H * DH))
    start_near(1)
    relay_plane(0)

    pair_sibling_copy(0).wait_recv()
    own_pair = pair_part[pair_rows(place, core), :] + pair_from_sibling[0].astype(jnp.float32)
    for k in range(1, chips):
        pair_chip_copy(k).wait_recv()
        own_pair = own_pair + pair_from_chip[k].astype(jnp.float32)
    key_up = rotate_back(own_pair[:, :DH], cosine, sinus)
    key_rows = key_rows_ref[...]
    key_factor = rms_factor(key_rows)
    gain_term[4:5, DH : 2 * DH] = jnp.sum(key_up * key_rows * key_factor, axis=0, keepdims=True)
    joint_back[:, H * DH : (H + 1) * DH] = norm_back(
        key_rows, key_factor, gain_all_ref[4:5, DH : 2 * DH], key_up
    ).astype(jnp.bfloat16)
    joint_back[:, (H + 1) * DH :] = own_pair[:, DH:].astype(jnp.bfloat16)
    joint_term(2, slice(H * DH, (H + 2) * DH))
    start_near(2)
    run_plane(1)
    run_line(0)
    run_plane(2)
    finish_slab()
    for b in range(2):
        total = gate_near[0, b].astype(jnp.float32)
        for j in direct:
            total = total + gate_near[j, b].astype(jnp.float32)
        gate_total[b] = total
    for c in range(ctxs):
        for b in range(2):
            joined[b * rows_own : (b + 1) * rows_own, :] = gate_total[
                b, c * rows_own : (c + 1) * rows_own, :
            ]
        to_ctx[c] = joined[...].astype(jnp.bfloat16)
    for k in range(1, ctxs):
        swap_copy(k).start()
    from_ctx[ctx] = to_ctx[ctx]


    normed_wide[...] = times_transposed(joint_back[...], joint_ref[...])
    spaced = spread_ref.shape[1] // (seqs * ctxs)
    for i in range(seqs * ctxs):
        input_wide_back[:, i * rows_own : (i + 1) * rows_own] = normed_wide[
            :, i * spaced : i * spaced + rows_own
        ]
    normed_back = input_wide_back[...]
    input_wide = inputs_ref[...].astype(jnp.float32)
    input_factor = rms_factor(input_wide)
    gain_term[0:1, :] = jnp.sum(normed_back * input_wide * input_factor, axis=0, keepdims=True)

    def gain_near_copy():
        return send_to(gain_term, gain_near, gain_near_sems.at[0], gain_near_sems.at[1], sibling)

    def gain_plane_copy(j):
        return send_to(
            gain_chip,
            gain_plane.at[j],
            gain_plane_sems.at[0, j],
            gain_plane_sems.at[1, j],
            (lax.rem(seq + j, seqs), ctx),
        )

    def gain_line_copy(k):
        return send_to(
            gain_row,
            gain_line.at[k],
            gain_line_sems.at[0, k],
            gain_line_sems.at[1, k],
            (seq, lax.rem(place + k, chips) * 2 + core),
        )

    gain_near_copy().start()
    relay_plane(1)
    gain_near_copy().wait_recv()
    gain_chip[...] = gain_term[...] + gain_near[...]
    for j in range(1, seqs):
        gain_plane_copy(j).start()
    input_grad_ref[...] += norm_back(
        input_wide, input_factor, gain_all_ref[0:1, :], normed_back
    )
    relay_plane(2)
    run_line(1)
    run_line(2)
    total = gain_chip[...]
    for j in range(1, seqs):
        gain_plane_copy(j).wait_recv()
        total = total + gain_plane[j]
    gain_row[...] = total
    for k in range(1, chips):
        gain_line_copy(k).start()
    for k in range(1, ctxs):
        swap_copy(k).wait_recv()
    for c in range(ctxs):
        joined[...] = from_ctx[c].astype(jnp.float32)
        for b, target in ((0, grad_gate_ref), (1, grad_up_ref)):
            for s in range(seqs):
                first = (s * ctxs + c) * units
                target[:, first : first + units] = joined[
                    b * rows_own : (b + 1) * rows_own, s * slab : s * slab + units
                ]
    grad_output_ref[...] = finish(0)
    grad_query_ref[...] = finish(1)[0:rows_own]
    total = finish(2)[0:rows_own]
    grad_key_ref[...] = total[:, :DH]
    grad_value_ref[...] = total[:, DH:]
    total = gain_row[...]
    for k in range(1, chips):
        gain_line_copy(k).wait_recv()
        total = total + gain_line[k]
    gains_ref[...] = total
    for b in range(3):
        drain(b)
    drain_slab()
    for k in range(1, ctxs):
        swap_copy(k).wait_send()
    for k in range(chips):
        pair_sibling_copy(k).wait_send()
    for k in range(1, chips):
        pair_chip_copy(k).wait_send()
        gain_line_copy(k).wait_send()
    gain_near_copy().wait_send()
    for j in range(1, seqs):
        gain_plane_copy(j).wait_send()


def back_call(seqs, chips, padded_rows, output_rows, width_rows, units, *operands):
    fed_back = operands[0]
    count, width = fed_back.shape
    ctxs = 2 * chips
    total = ctxs * count
    blocks = seqs * ctxs
    wide = jnp.float32
    half = jnp.bfloat16
    dma = pltpu.SemaphoreType.DMA
    shape = jax.ShapeDtypeStruct
    vmem = pl.BlockSpec(memory_space=pltpu.VMEM)
    pair_term = operands[-1]
    near_slabs, middle_slabs = (3, 2) if seqs == 4 else (seqs, 1)
    unit_count = pair_term.shape[-1]
    both_rows = -(-2 * width_rows // 16) * 16
    hbm = pl.BlockSpec(memory_space=pl.ANY)
    sizes = ((output_rows, width), (padded_rows, H * DH), (padded_rows, 2 * DH))
    scratch = [
        pltpu.VMEM((count, width), half),
        pltpu.VMEM((count, H * DH), wide),
        pltpu.VMEM((H * count, DH), half),
        pltpu.VMEM((H * count, total), half),
        pltpu.VMEM((H * count, total), half),
        pltpu.VMEM((count, blocks * padded_rows), wide),
        pltpu.VMEM((count, width), wide),
        pltpu.VMEM((total, 2 * DH), wide),
        pltpu.VMEM((chips, count, 2 * DH), half),
        pltpu.VMEM((chips, count, 2 * DH), half),
        pltpu.VMEM((chips, count, 2 * DH), half),
        pltpu.VMEM((chips, count, 2 * DH), half),
        pltpu.VMEM((count, (H + 2) * DH), half),
        pltpu.VMEM((8, width), wide),
        pltpu.VMEM((8, width), wide),
        pltpu.VMEM((8, width), wide),
        pltpu.VMEM((seqs, 8, width), wide),
        pltpu.VMEM((8, width), wide),
        pltpu.VMEM((chips, 8, width), wide),
        pltpu.VMEM((near_slabs,) + pair_term.shape[1:], half),
        pltpu.VMEM((middle_slabs,) + pair_term.shape[1:], half),
        pltpu.VMEM(pair_term.shape[1:], wide),
        pltpu.VMEM((ctxs, both_rows, unit_count), half),
        pltpu.VMEM((ctxs, both_rows, unit_count), half),
        pltpu.VMEM((both_rows, unit_count), wide),
    ]
    for rows, columns in sizes:
        scratch += [
            pltpu.VMEM((blocks, rows, columns), half),
            pltpu.VMEM((seqs, chips, rows, columns), half),
            pltpu.VMEM((seqs, chips, rows, columns), half),
            pltpu.VMEM((chips, rows, columns), half),
            pltpu.VMEM((chips, rows, columns), half),
            pltpu.VMEM((rows, columns), wide),
        ]
    scratch += [
        dma((2, chips)),
        dma((2, chips)),
        dma((2,)),
        dma((2, seqs)),
        dma((2, chips)),
        dma((2, 3, seqs, chips)),
        dma((2, 3, seqs, chips)),
        dma((2, 3, chips)),
        dma((2, max(seqs, 6))),
        dma((3,)),
        dma((2, ctxs)),
    ]
    return pl.pallas_call(
        functools.partial(back_kernel, seqs, chips),
        out_shape=(
            shape((count, width), wide),
            shape(sizes[0], wide),
            shape((width_rows, H * DH), wide),
            shape((width_rows, DH), wide),
            shape((width_rows, DH), wide),
            shape((8, width), wide),
            shape((width_rows, blocks * units), wide),
            shape((width_rows, blocks * units), wide),
        ),
        in_specs=[vmem] * (len(operands) - 1) + [hbm],
        out_specs=(vmem,) * 8,
        scratch_shapes=scratch,
        compiler_params=pltpu.CompilerParams(
            collective_id=4, has_side_effects=True, vmem_limit_bytes=58 * 2**20
        ),
        cost_estimate=pl.CostEstimate(
            flops=8 * count * width * (H + 2) * DH,
            bytes_accessed=200 * 2**20,
            transcendentals=H * count * total,
        ),
        name="back",
    )(*operands)


def per_device(
    inputs,
    positions,
    attention_gain,
    query_weight,
    key_weight,
    value_weight,
    query_gain,
    key_gain,
    output_weight,
    attention_post,
    feedfwd_gain,
    gate_weight,
    up_weight,
    down_weight,
    feedfwd_post,
    cotangent,
):
    seq_total = lax.axis_size("seq")
    ctx_total = lax.axis_size("ctx")
    device_total = seq_total * ctx_total
    token_count = inputs.shape[0]
    width_rows = query_weight.shape[0]
    head_rows = query_gain.shape[0]
    unit_rows = down_weight.shape[0]

    block_number = (positions[:1] // token_count).astype(jnp.float32)
    small_rows = jnp.stack(
        [
            jnp.pad(vector.astype(jnp.float32), (0, 128 - vector.shape[0]))
            for vector in (
                attention_gain,
                attention_post,
                feedfwd_gain,
                feedfwd_post,
                query_gain,
                key_gain,
                block_number,
            )
        ]
    )
    chips = ctx_total // 2
    padded_rows = -(-(width_rows + 1) // 16) * 16
    cosine, sinus = rotary(positions)
    place_wide = positions.astype(jnp.float32)[:, None]
    (
        packets,
        outputs,
        gate_all,
        up_all,
        down_all,
        gain_all,
        places,
        spread,
        queries,
        key_rows,
        query_rot,
        both_rows,
        attended,
        logsum,
        mixed_values,
        residual,
        fed_all,
    ) = front_call(
        seq_total,
        chips,
        inputs,
        query_weight,
        key_weight,
        value_weight,
        small_rows,
        output_weight,
        gate_weight,
        up_weight,
        down_weight,
        cosine,
        sinus,
        place_wide,
    )
    block_out, grad_final, fed_back, grad_down, pair_term = feed_call(
        fed_all,
        residual,
        cotangent,
        gain_all,
        gate_all,
        up_all,
        down_all,
        unit_rows,
        seq_total,
        chips,
    )
    (
        input_grad,
        grad_output,
        grad_query,
        grad_key,
        grad_value,
        gains,
        grad_gate,
        grad_up,
    ) = back_call(
        seq_total,
        chips,
        padded_rows,
        output_weight.shape[0],
        width_rows,
        unit_rows,
        fed_back,
        residual,
        mixed_values,
        cotangent,
        inputs,
        spread,
        queries,
        key_rows,
        query_rot,
        both_rows,
        attended,
        logsum,
        outputs.reshape(H * DH, D),
        packets.reshape(-1, (H + 2) * DH),
        grad_final,
        gain_all,
        cosine,
        sinus,
        place_wide,
        places,
        pair_term,
    )
    device = lax.axis_index("seq") * ctx_total + lax.axis_index("ctx")

    def own_gain(row, start, size):
        return lax.dynamic_slice(gains, (row, start + device * size), (1, size))[0]

    return (
        block_out,
        input_grad,
        own_gain(0, 0, width_rows),
        grad_query,
        grad_key,
        grad_value,
        own_gain(4, 0, head_rows),
        own_gain(4, DH, head_rows),
        grad_output,
        own_gain(1, 0, width_rows),
        own_gain(2, 0, width_rows),
        grad_gate,
        grad_up,
        grad_down,
        own_gain(3, 0, width_rows),
    )


def solution(mesh):
    return jax.shard_map(
        per_device,
        mesh=mesh,
        in_specs=(
            P(("seq", "ctx"), None),
            P(("seq", "ctx")),
            P(("seq", "ctx")),
            P(("seq", "ctx"), None),
            P(("seq", "ctx"), None),
            P(("seq", "ctx"), None),
            P(("seq", "ctx")),
            P(("seq", "ctx")),
            P(("seq", "ctx"), None),
            P(("seq", "ctx")),
            P(("seq", "ctx")),
            P(("seq", "ctx"), None),
            P(("seq", "ctx"), None),
            P(("seq", "ctx"), None),
            P(("seq", "ctx")),
            P(("seq", "ctx"), None),
        ),
        out_specs=(
            P(("seq", "ctx"), None),
            P(("seq", "ctx"), None),
            P(("seq", "ctx")),
            P(("seq", "ctx"), None),
            P(("seq", "ctx"), None),
            P(("seq", "ctx"), None),
            P(("seq", "ctx")),
            P(("seq", "ctx")),
            P(("seq", "ctx"), None),
            P(("seq", "ctx")),
            P(("seq", "ctx")),
            P(("seq", "ctx"), None),
            P(("seq", "ctx"), None),
            P(("seq", "ctx"), None),
            P(("seq", "ctx")),
        ),
        check_vma=False,
    )
```

```python
import functools
import math

import jax
import jax.numpy as jnp
from jax import lax
from jax.experimental import pallas as pl
from jax.experimental.pallas import tpu as pltpu
from jax.sharding import PartitionSpec as P

D = 1152
H = 4
DH = 256
FF = 6912


EPSILON = 1e-06
THETA = 1000000.0
GELU_COEF = math.sqrt(2.0 / math.pi)


def rms_factor(values):
    return lax.rsqrt(jnp.mean(values * values, axis=-1, keepdims=True) + EPSILON)


def norm_back(values, factor, gain_vector, upstream):
    scaled = gain_vector * upstream
    cubed = factor * factor * factor
    return factor * scaled - values * cubed * jnp.mean(scaled * values, axis=-1, keepdims=True)


def rotary(places):
    half_width = DH // 2
    exponent = jnp.arange(half_width, dtype=jnp.float32) * (-2.0 / DH)
    frequency = jnp.power(jnp.float32(THETA), exponent)
    angles = places.astype(jnp.float32)[:, None] * frequency[None, :]
    return (jnp.cos(angles), jnp.sin(angles))


def rotate(values, cosine, sinus):
    half_width = values.shape[-1] // 2
    first = values[..., :half_width]
    second = values[..., half_width:]
    return jnp.concatenate(
        [first * cosine - second * sinus, second * cosine + first * sinus], axis=-1
    )


def rotate_back(upstream, cosine, sinus):
    half_width = upstream.shape[-1] // 2
    first = upstream[..., :half_width]
    second = upstream[..., half_width:]
    return jnp.concatenate(
        [first * cosine + second * sinus, second * cosine - first * sinus], axis=-1
    )


def gelu_tanh(values):
    inner = GELU_COEF * (values + 0.044715 * values * values * values)
    return 0.5 * values * (1.0 + jnp.tanh(inner))


def gelu_slope(values):
    inner = GELU_COEF * (values + 0.044715 * values * values * values)
    tangent = jnp.tanh(inner)
    return 0.5 * (1.0 + tangent) + 0.5 * values * (1.0 - tangent * tangent) * GELU_COEF * (
        1.0 + 3.0 * 0.044715 * values * values
    )


def times_right(left_side, right_side):
    return jnp.dot(left_side, right_side, preferred_element_type=jnp.float32)


def times_transposed(left_side, right_side):
    return lax.dot_general(
        left_side, right_side, (((1,), (1,)), ((), ())), preferred_element_type=jnp.float32
    )


def transposed_times(left_side, right_side):
    return lax.dot_general(
        left_side, right_side, (((0,), (0,)), ((), ())), preferred_element_type=jnp.float32
    )


BOTH = ("seq", "ctx")
MESH = pl.DeviceIdType.MESH


def peers():
    seq = lax.axis_index("seq")
    ctx = lax.axis_index("ctx")
    return seq, ctx // 2, lax.rem(ctx, 2)


def greet(seq, place, core, chips):
    barrier = pltpu.get_barrier_semaphore()
    pl.semaphore_signal(
        barrier, inc=1, device_id=(seq, place * 2 + 1 - core), device_id_type=MESH
    )
    for k in range(1, chips):
        other = lax.rem(place + k, chips) * 2 + core
        pl.semaphore_signal(barrier, inc=1, device_id=(seq, other), device_id_type=MESH)
    pl.semaphore_wait(barrier, chips)


def send_to(source, target, send_sem, recv_sem, device):
    return pltpu.make_async_remote_copy(
        src_ref=source,
        dst_ref=target,
        send_sem=send_sem,
        recv_sem=recv_sem,
        device_id=device,
        device_id_type=MESH,
    )


def plane_of(seq):
    return seq + 1 - 2 * lax.rem(seq, 2), lax.rem(seq + 2, 4)


def slab_sum(seqs, ctx, seq, term, near, middle, part_of, slab_sems, own_sems):
    square = seqs == 4
    beside, across = plane_of(seq)
    low, high = part_of(0), part_of(1)

    def copy(j):
        if not square:
            row = lax.rem(seq + j, seqs)
            origin, goal, target = term.at[row], near.at[j], row
        elif j == 0:
            origin, goal, target = term.at[3 - seq, low], middle.at[0, low], beside
        elif j == 1:
            origin, goal, target = term.at[3 - seq, high], middle.at[0, high], across
        elif j == 2:
            origin, goal, target = term.at[across, high], near.at[2, high], across
        elif j == 3:
            origin, goal, target = term.at[beside, low], near.at[1, low], beside
        elif j == 4:
            origin, goal, target = middle.at[1, low], near.at[2, low], across
        else:
            origin, goal, target = middle.at[1, high], near.at[1, high], beside
        return send_to(origin, goal, slab_sems.at[0, j], slab_sems.at[1, j], (target, ctx))

    def own():
        return pltpu.make_async_copy(term.at[seq], near.at[0], own_sems.at[0])

    def between(half):
        part = part_of(half)
        row = across if half == 0 else beside
        return pltpu.make_async_copy(
            term.at[row, part], middle.at[1, part], own_sems.at[1 + half]
        )

    def start():
        for j in range(2) if square else range(1, seqs):
            copy(j).start()
        own().start()
        if square:
            between(0).start()
            between(1).start()

    def rest():
        if square:
            copy(2).start()
            copy(3).start()

    def relay():
        if square:
            for half in range(2):
                part = part_of(half)
                between(half).wait()
                copy(half).wait_recv()
                middle[1, part] = (
                    middle[1, part].astype(jnp.float32) + middle[0, part].astype(jnp.float32)
                ).astype(jnp.bfloat16)
                copy(4 + half).start()

    def finish():
        own().wait()
        for j in range(2, 6) if square else range(1, seqs):
            copy(j).wait_recv()

    def drain():
        for j in range(6) if square else range(1, seqs):
            copy(j).wait_send()

    return start, rest, relay, finish, drain


def feed_kernel(
    seqs,
    chips,
    fed_all,
    residual_ref,
    cot_ref,
    gain_ref,
    gate_ref,
    up_ref,
    down_ref,
    block_ref,
    grad_final_ref,
    fed_back_ref,
    grad_down_ref,
    grad_pair_ref,
    hidden_ref,
    gate_back_ref,
    up_back_ref,
    back_all,
    gate_values,
    up_values,
    part,
    hidden_back,
    own,
    grad_part,
    down_term,
    down_near,
    down_middle,
    to_sibling,
    from_sibling,
    to_chip,
    from_chip,
    gather_sems,
    forward_sems,
    sibling_sems,
    chip_sems,
    slab_sems,
    own_sems,
):
    seq, place, core = peers()
    ctx = place * 2 + core
    sibling = (seq, place * 2 + 1 - core)
    count = residual_ref.shape[0]
    pair_count = 2 * count
    chunk = min(64, pair_count)
    slab = down_near.shape[1]
    barrier = pltpu.get_barrier_semaphore()
    pl.semaphore_signal(barrier, inc=1, device_id=sibling, device_id_type=MESH)
    for k in range(1, chips):
        other = lax.rem(place + k, chips) * 2 + core
        pl.semaphore_signal(barrier, inc=1, device_id=(seq, other), device_id_type=MESH)
    for j in range(1, seqs):
        pl.semaphore_signal(
            barrier, inc=1, device_id=(lax.rem(seq + j, seqs), ctx), device_id_type=MESH
        )
    start_down, rest_down, relay_down, finish_down, drain_down = slab_sum(
        seqs,
        ctx,
        seq,
        down_term,
        down_near,
        down_middle,
        lambda half: pl.ds(half * (slab // 2), slab // 2),
        slab_sems,
        own_sems,
    )

    def rows_of(chip, which):
        return pl.ds(pl.multiple_of((chip * 2 + which) * count, count), count)

    def pair_of(chip):
        return pl.ds(pl.multiple_of(chip * pair_count, pair_count), pair_count)

    mine = rows_of(place, core)

    def line_copy(side, d):
        sign = 1 - 2 * side
        block = back_all.at[rows_of(place - sign * (d - 1), core)]
        return send_to(
            block,
            block,
            gather_sems.at[0, side, d],
            gather_sems.at[1, side, d],
            (seq, (place + sign) * 2 + core),
        )

    def pass_copy(side, d):
        sign = 1 - 2 * side
        block = back_all.at[rows_of(place - sign * d, core)]
        return send_to(
            block, block, forward_sems.at[0, side, d], forward_sems.at[1, side, d], sibling
        )

    def comes(side, d):
        return place - d >= 0 if side == 0 else place + d < chips

    def goes(side, d):
        if side == 0:
            return jnp.logical_and(place + 1 < chips, place - (d - 1) >= 0)
        return jnp.logical_and(place - 1 >= 0, place + (d - 1) < chips)

    def relay_line(d):
        for side in range(2):

            @pl.when(comes(side, d))
            def _():
                line_copy(side, d).wait_recv()
                pass_copy(side, d).start()

            @pl.when(jnp.logical_and(comes(side, d), goes(side, d + 1)))
            def _():
                line_copy(side, d + 1).start()

    def sibling_copy(index, k):
        return send_to(
            to_sibling.at[k],
            from_sibling.at[index, k],
            sibling_sems.at[0, index, k],
            sibling_sems.at[1, index, k],
            sibling,
        )

    def chip_copy(index, k):
        chip = lax.rem(place - k + chips, chips)
        return send_to(
            to_chip.at[k],
            from_chip.at[index, k],
            chip_sems.at[0, index, k],
            chip_sems.at[1, index, k],
            (seq, chip * 2 + core),
        )

    def pass_part(index, k):
        other_rows = pl.ds(pl.multiple_of((1 - core) * count, count), count)
        own_rows = pl.ds(pl.multiple_of(core * count, count), count)
        to_sibling[k] = part[other_rows, :].astype(jnp.bfloat16)
        sibling_copy(index, k).start()
        sibling_copy(index, k).wait_recv()
        total = part[own_rows, :] + from_sibling[index, k].astype(jnp.float32)

        @pl.when(k == 0)
        def _():
            own[...] = total

        @pl.when(k > 0)
        def _():
            to_chip[k] = total.astype(jnp.bfloat16)
            chip_copy(index, k).start()

    def collect(index):
        for k in range(1, chips):
            chip_copy(index, k).wait_recv()
            own[...] += from_chip[index, k].astype(jnp.float32)
        for k in range(chips):
            sibling_copy(index, k).wait_send()
        for k in range(1, chips):
            chip_copy(index, k).wait_send()

    def forward_step(i, carry):
        k = lax.rem(i + 1, chips)
        rows = pair_of(lax.rem(place - k + chips, chips))
        block = fed_all[rows, :]
        gate_values[rows, :] = times_right(block, gate_ref[...])
        up_values[rows, :] = times_right(block, up_ref[...])

        def gated(j, carry):
            here = pl.ds(pl.multiple_of(rows.start + j * chunk, chunk), chunk)
            hidden_ref[here, :] = (gelu_tanh(gate_values[here, :]) * up_values[here, :]).astype(
                jnp.bfloat16
            )
            return carry

        lax.fori_loop(0, pair_count // chunk, gated, 0)
        part[...] = times_right(hidden_ref[rows, :], down_ref[...])

        @pl.when(i == 0)
        def _():
            pl.semaphore_wait(barrier, chips + seqs - 1)

        pass_part(0, k)
        return carry

    def backward_work(k):
        rows = pair_of(lax.rem(place - k + chips, chips))
        hidden_back[...] = times_transposed(back_all[rows, :], down_ref[...])

        def gated(j, carry):
            here = pl.ds(pl.multiple_of(rows.start + j * chunk, chunk), chunk)
            local = pl.ds(pl.multiple_of(j * chunk, chunk), chunk)
            gate_now = gate_values[here, :]
            upper = hidden_back[local, :]
            gate_back_ref[here, :] = (upper * up_values[here, :] * gelu_slope(gate_now)).astype(
                jnp.bfloat16
            )
            up_back_ref[here, :] = (upper * gelu_tanh(gate_now)).astype(jnp.bfloat16)
            return carry

        lax.fori_loop(0, pair_count // chunk, gated, 0)
        part[...] = times_transposed(gate_back_ref[rows, :], gate_ref[...])
        part[...] += times_transposed(up_back_ref[rows, :], up_ref[...])
        pass_part(1, k)

    def backward_step(d, carry):
        @pl.when(jnp.logical_or(d == 1, place - (d - 1) < 0))
        def _():
            relay_line(d)

        @pl.when(d == chips - 1)
        def _():
            for side in range(2):

                @pl.when(comes(side, d))
                def _():
                    pass_copy(side, d).wait_recv()

            for s in range(seqs):
                down_term[s] = transposed_times(
                    hidden_ref[:, s * slab : (s + 1) * slab], back_all[...]
                ).astype(jnp.bfloat16)
            start_down()
            rest_down()

        @pl.when(comes(0, d))
        def _():
            @pl.when(d < chips - 1)
            def _():
                pass_copy(0, d).wait_recv()

            backward_work(d)

        @pl.when(jnp.logical_and(comes(0, d), d < chips - 1))
        def _():
            relay_line(d + 1)

        @pl.when(comes(1, d))
        def _():
            @pl.when(d < chips - 1)
            def _():
                pass_copy(1, d).wait_recv()

            backward_work(chips - d)

        return carry

    lax.fori_loop(0, chips, forward_step, 0)
    collect(0)
    down_values = own[...]
    down_factor = rms_factor(down_values)
    gain_final = gain_ref[3:4, :]
    cot_wide = cot_ref[...].astype(jnp.float32)
    back_all[mine, :] = norm_back(down_values, down_factor, gain_final, cot_wide).astype(
        jnp.bfloat16
    )
    for side in range(2):

        @pl.when(goes(side, 1))
        def _():
            line_copy(side, 1).start()

    pass_copy(0, 0).start()
    block_ref[...] = (residual_ref[...] + down_values * down_factor * gain_final).astype(
        jnp.bfloat16
    )
    grad_final_ref[...] = jnp.sum(cot_wide * down_values * down_factor, axis=0, keepdims=True)
    pass_copy(0, 0).wait_recv()
    backward_work(0)
    lax.fori_loop(1, chips, backward_step, 0)
    relay_down()
    slabs, _, slab_rows, _ = grad_pair_ref.shape
    tall = grad_part.shape[0]
    for b, source in ((0, gate_back_ref), (1, up_back_ref)):
        for c in range(slabs * slab_rows // tall):
            grad_part[...] = transposed_times(
                fed_all[:, c * tall : (c + 1) * tall], source[...]
            )
            for s in range(slabs):
                low = max(s * slab_rows, c * tall)
                high = min((s + 1) * slab_rows, (c + 1) * tall)
                if low < high:
                    grad_pair_ref[s, b, low - s * slab_rows : high - s * slab_rows] = grad_part[
                        low - c * tall : high - c * tall, :
                    ].astype(jnp.bfloat16)
    collect(1)
    fed_back_ref[...] = own[...]
    finish_down()
    total = down_near[0].astype(jnp.float32)
    for j in (1, 2) if seqs == 4 else range(1, seqs):
        total = total + down_near[j].astype(jnp.float32)
    grad_down_ref[...] = total[0 : grad_down_ref.shape[0]]
    drain_down()
    pass_copy(0, 0).wait_send()
    for d in range(1, chips):
        for side in range(2):

            @pl.when(comes(side, d))
            def _():
                pass_copy(side, d).wait_send()

            @pl.when(goes(side, d))
            def _():
                line_copy(side, d).wait_send()


def feed_call(fed, residual, cot, gain, gate, up, down, down_rows, seqs, chips):
    count, width = residual.shape
    total = 2 * chips * count
    units = down.shape[0]
    slab = units // seqs
    wide = jnp.float32
    half = jnp.bfloat16
    dma = pltpu.SemaphoreType.DMA
    shape = jax.ShapeDtypeStruct
    vmem = pl.BlockSpec(memory_space=pltpu.VMEM)
    near_slabs, middle_slabs = (3, 2) if seqs == 4 else (seqs, 1)
    return pl.pallas_call(
        functools.partial(feed_kernel, seqs, chips),
        out_shape=(
            shape((count, width), half),
            shape((1, width), wide),
            shape((count, width), wide),
            shape((down_rows, width), wide),
            shape((seqs, 2, width // seqs, units), half),
        ),
        in_specs=[vmem] * 7,
        out_specs=(vmem,) * 5,
        scratch_shapes=[
            pltpu.VMEM((total, units), half),
            pltpu.VMEM((total, units), half),
            pltpu.VMEM((total, units), half),
            pltpu.VMEM((total, width), half),
            pltpu.VMEM((total, units), wide),
            pltpu.VMEM((total, units), wide),
            pltpu.VMEM((2 * count, width), wide),
            pltpu.VMEM((2 * count, units), wide),
            pltpu.VMEM((count, width), wide),
            pltpu.VMEM((width // 3, units), wide),
            pltpu.VMEM((seqs, slab, width), half),
            pltpu.VMEM((near_slabs, slab, width), half),
            pltpu.VMEM((middle_slabs, slab, width), half),
            pltpu.VMEM((chips, count, width), half),
            pltpu.VMEM((2, chips, count, width), half),
            pltpu.VMEM((chips, count, width), half),
            pltpu.VMEM((2, chips, count, width), half),
            dma((2, 2, chips + 1)),
            dma((2, 2, chips + 1)),
            dma((2, 2, chips)),
            dma((2, 2, chips)),
            dma((2, max(seqs, 6))),
            dma((3,)),
        ],
        compiler_params=pltpu.CompilerParams(
            collective_id=1, has_side_effects=True, vmem_limit_bytes=58 * 2**20
        ),
        name="feed",
    )(fed, residual, cot, gain, gate, up, down)


def front_kernel(
    seqs,
    chips,
    inputs_ref,
    query_ref,
    key_ref,
    value_ref,
    small_ref,
    output_ref,
    gate_ref,
    up_ref,
    down_ref,
    cosine_ref,
    sinus_ref,
    place_ref,
    packets,
    outputs,
    gate_all,
    up_all,
    down_all,
    gains,
    places,
    spread_ref,
    queries_ref,
    key_rows_ref,
    query_rot_ref,
    both_ref,
    attended_ref,
    logsum_ref,
    mixed_ref,
    residual_ref,
    fed_all,
    wide_packet,
    own_packet,
    own_down,
    to_ctx,
    from_ctx,
    joined,
    packed,
    spread,
    spread_gain,
    own_pair,
    line_sems,
    plane_sems,
    core_sems,
    swap_sems,
    slab_sems,
    gather_sems,
    forward_sems,
    fed_sems,
    pass_sems,
):
    seq, place, core = peers()
    ctx = place * 2 + core
    sibling = (seq, place * 2 + 1 - core)
    ctxs = 2 * chips
    blocks = seqs * ctxs
    count, width = inputs_ref.shape
    rows = gate_ref.shape[0]
    head_rows = DH // blocks
    units = down_ref.shape[0]
    slab = own_down.shape[0]
    square = seqs == 4
    beside = seq + 1 - 2 * lax.rem(seq, 2)
    across = lax.rem(seq + 2, 4)
    direct = (1, 2) if square else range(1, seqs)
    barrier = pltpu.get_barrier_semaphore()
    for k in range(1, ctxs):
        pl.semaphore_signal(
            barrier, inc=1, device_id=(seq, lax.rem(ctx + k, ctxs)), device_id_type=MESH
        )
    for j in range(1, seqs):
        pl.semaphore_signal(
            barrier, inc=1, device_id=(lax.rem(seq + j, seqs), ctx), device_id_type=MESH
        )

    def index_of(row, chip, which):
        return row * ctxs + chip * 2 + which

    both = ((own_packet, packets), (output_ref, outputs))

    def line_copy(b, k):
        own, everything = both[b]
        chip = lax.rem(place + k, chips)
        return send_to(
            own,
            everything.at[index_of(seq, place, core)],
            line_sems.at[0, b, k],
            line_sems.at[1, b, k],
            (seq, chip * 2 + core),
        )

    def plane_copy(b, j, k):
        everything = both[b][1]
        chip = lax.rem(place - k + chips, chips)
        row, target = seq, lax.rem(seq + j, seqs)
        if square:
            even = lax.rem(jnp.int32(k), 2) == 0
            if j == 3:
                row = jnp.where(even, beside, across)
                target = jnp.where(even, across, beside)
            else:
                target = beside if j == 1 else across
        block = everything.at[index_of(row, chip, core)]
        return send_to(
            block,
            block,
            plane_sems.at[0, b, j, k],
            plane_sems.at[1, b, j, k],
            (target, ctx),
        )

    def core_copy(b, j, k):
        everything = both[b][1]
        row = (seq, beside, across, 3 - seq)[j] if square else lax.rem(seq - j + seqs, seqs)
        chip = lax.rem(place - k + chips, chips)
        block = everything.at[index_of(row, chip, core)]
        return send_to(
            block, block, core_sems.at[0, b, j, k], core_sems.at[1, b, j, k], sibling
        )

    def swap_copy(k):
        target = lax.rem(ctx + k, ctxs)
        return send_to(
            to_ctx.at[target],
            from_ctx.at[ctx],
            swap_sems.at[0, k],
            swap_sems.at[1, k],
            (seq, target),
        )

    def slab_copy(which, j):
        height = slab if which == 0 else ctxs * rows
        everything = (down_all, gate_all, up_all)[which]
        first, size, target = seq * height, height, lax.rem(seq + j, seqs)
        if square:
            half = height // 2
            if j == 0:
                target = beside
            elif j == 1:
                target = across
            elif j == 2:
                first, size, target = beside * height, half, across
            else:
                first, size, target = across * height + half, half, beside
            first = pl.multiple_of(first, half)
        else:
            first = pl.multiple_of(first, height)
        here = everything.at[pl.ds(first, size)]
        return send_to(
            here,
            here,
            slab_sems.at[0, which, j],
            slab_sems.at[1, which, j],
            (target, ctx),
        )

    def start_slab(which):
        for j in (0, 1) if square else range(1, seqs):
            slab_copy(which, j).start()

    def relay_slab(which):
        if square:
            slab_copy(which, 0).wait_recv()
            slab_copy(which, 2).start()
            slab_copy(which, 1).wait_recv()
            slab_copy(which, 3).start()

    def finish_slab(which):
        if square:
            slab_copy(which, 0).wait_send()
            slab_copy(which, 1).wait_send()
            slab_copy(which, 2).wait()
            slab_copy(which, 3).wait()
        else:
            for j in range(1, seqs):
                slab_copy(which, j).wait()

    def rows_of(chip):
        return pl.ds(pl.multiple_of((chip * 2 + core) * count, count), count)

    def gather_copy(k):
        chip = lax.rem(place + k, chips)
        return send_to(
            own_pair,
            both_ref.at[rows_of(place)],
            gather_sems.at[0, k],
            gather_sems.at[1, k],
            (seq, chip * 2 + core),
        )

    def forward_copy(k):
        chip = lax.rem(place - k + chips, chips)
        block = both_ref.at[rows_of(chip)]
        return send_to(block, block, forward_sems.at[0, k], forward_sems.at[1, k], sibling)

    def fed_copy(k):
        chip = lax.rem(place + k, chips)
        block = fed_all.at[rows_of(place)]
        return send_to(
            block, block, fed_sems.at[0, k], fed_sems.at[1, k], (seq, chip * 2 + core)
        )

    def pass_copy(k):
        chip = lax.rem(place - k + chips, chips)
        block = fed_all.at[rows_of(chip)]
        return send_to(block, block, pass_sems.at[0, k], pass_sems.at[1, k], sibling)

    def start_own(b):
        own, everything = both[b]
        for k in range(1, chips):
            line_copy(b, k).start()
        everything[index_of(seq, place, core)] = own[...]
        core_copy(b, 0, 0).start()

    def start_plane(b):
        for j in direct:
            plane_copy(b, j, 0).start()

    def line_step(b):
        def one(k, carry):
            line_copy(b, k).wait_recv()
            for j in direct:
                plane_copy(b, j, k).start()
            core_copy(b, 0, k).start()
            return carry

        lax.fori_loop(1, chips, one, 0)

    def plane_step(b):
        def one(k, carry):
            for j in direct:
                plane_copy(b, j, k).wait_recv()
            if square:
                plane_copy(b, 3, k).start()
            for j in direct:
                core_copy(b, j, k).start()
            return carry

        lax.fori_loop(0, chips, one, 0)

    def relay_step(b):
        def one(k, carry):
            plane_copy(b, 3, k).wait_recv()
            core_copy(b, 3, k).start()
            return carry

        if square:
            lax.fori_loop(0, chips, one, 0)

    def core_step(b):
        def one(k, carry):
            for j in range(seqs):
                core_copy(b, j, k).wait_recv()
            return carry

        lax.fori_loop(0, chips, one, 0)

    def drain(b):
        def one(k, carry):
            for j in range(seqs):
                core_copy(b, j, k).wait_send()
                if j > 0:
                    plane_copy(b, j, k).wait_send()
            return carry

        lax.fori_loop(0, chips, one, 0)
        for k in range(1, chips):
            line_copy(b, k).wait_send()

    wide_packet[...] = jnp.zeros_like(wide_packet)
    wide_packet[0:rows, 0 : H * DH] = query_ref[...].astype(jnp.float32)
    wide_packet[0:rows, H * DH : (H + 1) * DH] = key_ref[...].astype(jnp.float32)
    wide_packet[0:rows, (H + 1) * DH :] = value_ref[...].astype(jnp.float32)
    for g in range(4):
        wide_packet[rows : rows + 1, g * rows : (g + 1) * rows] = small_ref[g : g + 1, :rows]
    for g in range(2):
        first = 4 * rows + g * head_rows
        wide_packet[rows : rows + 1, first : first + head_rows] = small_ref[
            4 + g : 5 + g, :head_rows
        ]
    first = 4 * rows + 2 * head_rows
    wide_packet[rows : rows + 1, first : first + 1] = small_ref[6:7, 0:1]
    own_packet[...] = wide_packet[...].astype(jnp.bfloat16)
    own_down[...] = jnp.zeros_like(own_down)
    own_down[0:units, :] = down_ref[...].astype(jnp.float32)
    down_all[pl.ds(pl.multiple_of(seq * slab, slab), slab), :] = own_down[...].astype(
        jnp.bfloat16
    )
    pl.semaphore_wait(barrier, ctxs + seqs - 2)
    start_own(0)
    start_plane(0)
    start_slab(0)

    joined[...] = jnp.zeros_like(joined)
    for c in range(ctxs):
        for b, source in ((0, gate_ref), (1, up_ref)):
            for s in range(seqs):
                first = (s * ctxs + c) * units
                low = first // 128 * 128
                high = min(-(-(first + units) // 128) * 128, gate_ref.shape[1])
                wide = source[:, low:high].astype(jnp.float32)
                joined[b * rows : (b + 1) * rows, s * slab : s * slab + units] = wide[
                    :, first - low : first - low + units
                ]
        to_ctx[c] = joined[...].astype(jnp.bfloat16)
    line_step(0)
    for k in range(1, ctxs):
        swap_copy(k).start()
    from_ctx[ctx] = to_ctx[ctx]

    input_wide = inputs_ref[...].astype(jnp.float32)
    scaled = input_wide * rms_factor(input_wide)
    spread[...] = jnp.zeros_like(spread)
    step = packets.shape[1]
    for i in range(blocks):
        spread[:, i * step : i * step + rows] = scaled[:, i * rows : (i + 1) * rows]
    plane_step(0)
    relay_step(0)
    start_own(1)
    start_plane(1)
    core_step(0)

    gains[...] = jnp.zeros_like(gains)
    spread_gain[...] = jnp.zeros_like(spread_gain)
    base = rows // 8 * 8
    for i in range(blocks):
        line = packets[i, base:, :256].astype(jnp.float32)[rows - base : rows - base + 1]
        for g in range(4):
            gains[g : g + 1, i * rows : (i + 1) * rows] = line[:, g * rows : (g + 1) * rows]
        spread_gain[0:1, i * step : i * step + rows] = line[:, 0:rows]
        for g in range(2):
            first = 4 * rows + g * head_rows
            here = g * DH + i * head_rows
            gains[4:5, here : here + head_rows] = line[:, first : first + head_rows]
    number_at = 4 * rows + 2 * head_rows
    offsets = lax.broadcasted_iota(jnp.int32, (1, count), 1).astype(jnp.float32)
    for c in range(ctxs):
        line = packets[seq * ctxs + c, base:, :256].astype(jnp.float32)
        number = line[rows - base : rows - base + 1, number_at : number_at + 1]
        places[:, c * count : (c + 1) * count] = number * count + offsets
    spread_ref[...] = (spread[...] * spread_gain[0:1, :]).astype(jnp.bfloat16)
    joint = packets.reshape(blocks * step, (H + 2) * DH)
    cosine = cosine_ref[...]
    sinus = sinus_ref[...]
    pair = times_right(spread_ref[...], joint[:, H * DH :])
    key_rows = pair[:, :DH]
    key_rows_ref[...] = key_rows
    key_rot = rotate(key_rows * rms_factor(key_rows) * gains[4:5, DH : 2 * DH], cosine, sinus)
    own_pair[:, :DH] = key_rot.astype(jnp.bfloat16)
    own_pair[:, DH:] = pair[:, DH:].astype(jnp.bfloat16)
    both_ref[rows_of(place), :] = own_pair[...]
    for k in range(1, chips):
        gather_copy(k).start()
    forward_copy(0).start()
    for k in range(1, ctxs):
        swap_copy(k).wait_recv()
    for c in range(ctxs):
        joined[...] = from_ctx[c].astype(jnp.float32)
        for b in range(2):
            packed[b, c * rows : (c + 1) * rows, :] = joined[b * rows : (b + 1) * rows, :]
    height = ctxs * rows
    here = pl.ds(pl.multiple_of(seq * height, height), height)
    gate_all[here, :] = packed[0].astype(jnp.bfloat16)
    up_all[here, :] = packed[1].astype(jnp.bfloat16)
    start_slab(1)
    start_slab(2)
    relay_slab(0)
    line_step(1)
    for h in range(H):
        mine = slice(h * count, (h + 1) * count)
        queries = times_right(spread_ref[...], joint[:, h * DH : (h + 1) * DH])
        queries_ref[mine, :] = queries
        query_rot_ref[mine, :] = rotate(
            queries * rms_factor(queries) * gains[4:5, 0:DH], cosine, sinus
        ).astype(jnp.bfloat16)
    plane_step(1)
    for k in range(1, chips):
        gather_copy(k).wait_recv()
        forward_copy(k).start()
    for k in range(chips):
        forward_copy(k).wait_recv()
    scaling = 1.0 / math.sqrt(DH)

    def head(h, carry):
        mine = pl.ds(pl.multiple_of(h * count, count), count)
        columns = pl.ds(pl.multiple_of(h * DH, DH), DH)
        allowed = places[...] <= place_ref[...]
        scores = times_transposed(query_rot_ref[mine, :], both_ref[:, :DH]) * scaling
        expscore = jnp.where(allowed, jnp.exp(scores), 0.0)
        weight_sum = jnp.sum(expscore, axis=-1, keepdims=True)
        summed = times_right(expscore.astype(jnp.bfloat16), both_ref[:, DH:])
        attended_ref[:, columns] = (summed / weight_sum).astype(jnp.bfloat16)
        logsum_ref[mine, :] = jnp.log(weight_sum)
        return carry

    lax.fori_loop(0, H, head, 0)
    relay_slab(1)
    relay_step(1)
    core_step(1)
    mixed_ref[...] = times_right(attended_ref[...], outputs.reshape(H * DH, width)[...])
    mixed = mixed_ref[...]
    residual = inputs_ref[...].astype(jnp.float32) + mixed * rms_factor(mixed) * gains[1:2, :]
    residual_ref[...] = residual
    fed_all[rows_of(place), :] = (residual * rms_factor(residual) * gains[2:3, :]).astype(
        jnp.bfloat16
    )
    for k in range(1, chips):
        fed_copy(k).start()
    pass_copy(0).start()
    for b in range(2):
        drain(b)
    for k in range(1, ctxs):
        swap_copy(k).wait_send()
    for k in range(chips):
        forward_copy(k).wait_send()
    for k in range(1, chips):
        gather_copy(k).wait_send()
    relay_slab(2)
    for k in range(1, chips):
        fed_copy(k).wait_recv()
        pass_copy(k).start()
    for which in range(3):
        finish_slab(which)
    for k in range(chips):
        pass_copy(k).wait()
    for k in range(1, chips):
        fed_copy(k).wait_send()


def front_call(seqs, chips, *operands):
    inputs, query_weight = operands[:2]
    output, gate, _, down = operands[5:9]
    count, width = inputs.shape
    wide = jnp.float32
    half = jnp.bfloat16
    dma = pltpu.SemaphoreType.DMA
    shape = jax.ShapeDtypeStruct
    vmem = pl.BlockSpec(memory_space=pltpu.VMEM)
    ctxs = 2 * chips
    total = ctxs * count
    blocks = seqs * ctxs
    rows = gate.shape[0]
    packet_rows = -(-(rows + 1) // 16) * 16
    joint_width = (H + 2) * DH
    slab = -(-down.shape[0] // 16) * 16
    unit_count = seqs * slab
    padded = -(-2 * rows // 16) * 16
    return pl.pallas_call(
        functools.partial(front_kernel, seqs, chips),
        out_shape=(
            shape((blocks, packet_rows, joint_width), half),
            shape((blocks,) + output.shape, half),
            shape((width, unit_count), half),
            shape((width, unit_count), half),
            shape((unit_count, width), half),
            shape((8, width), wide),
            shape((1, total), wide),
            shape((count, blocks * packet_rows), half),
            shape((H * count, DH), wide),
            shape((count, DH), wide),
            shape((H * count, DH), half),
            shape((total, 2 * DH), half),
            shape((count, H * DH), half),
            shape((H * count, 1), wide),
            shape((count, width), wide),
            shape((count, width), wide),
            shape((total, width), half),
        ),
        in_specs=[vmem] * len(operands),
        out_specs=(vmem,) * 17,
        scratch_shapes=[
            pltpu.VMEM((packet_rows, joint_width), wide),
            pltpu.VMEM((packet_rows, joint_width), half),
            pltpu.VMEM((slab, width), wide),
            pltpu.VMEM((ctxs, padded, unit_count), half),
            pltpu.VMEM((ctxs, padded, unit_count), half),
            pltpu.VMEM((padded, unit_count), wide),
            pltpu.VMEM((2, ctxs * rows, unit_count), wide),
            pltpu.VMEM((count, blocks * packet_rows), wide),
            pltpu.VMEM((8, blocks * packet_rows), wide),
            pltpu.VMEM((count, 2 * DH), half),
            dma((2, 2, chips)),
            dma((2, 2, seqs, chips)),
            dma((2, 2, seqs, chips)),
            dma((2, ctxs)),
            dma((2, 3, max(seqs, 4))),
            dma((2, chips)),
            dma((2, chips)),
            dma((2, chips)),
            dma((2, chips)),
        ],
        compiler_params=pltpu.CompilerParams(
            collective_id=2, has_side_effects=True, vmem_limit_bytes=58 * 2**20
        ),
        name="front",
    )(*operands)


def back_kernel(
    seqs,
    chips,
    fed_back_ref,
    residual_ref,
    mixed_ref,
    cot_ref,
    inputs_ref,
    spread_ref,
    queries_ref,
    key_rows_ref,
    query_rot_ref,
    both_ref,
    attended_ref,
    logsum_ref,
    output_ref,
    joint_ref,
    grad_final_ref,
    gain_all_ref,
    cosine_ref,
    sinus_ref,
    place_ref,
    places_ref,
    pair_term_ref,
    input_grad_ref,
    grad_output_ref,
    grad_query_ref,
    grad_key_ref,
    grad_value_ref,
    gains_ref,
    grad_gate_ref,
    grad_up_ref,
    mixed_back,
    attended_back,
    upper_round,
    probs,
    score_back,
    normed_wide,
    input_wide_back,
    pair_part,
    pair_to_sibling,
    pair_from_sibling,
    pair_to_chip,
    pair_from_chip,
    joint_back,
    gain_term,
    gain_near,
    gain_chip,
    gain_plane,
    gain_row,
    gain_line,
    gate_near,
    gate_middle,
    gate_total,
    to_ctx,
    from_ctx,
    joined,
    *rest,
):
    seq, place, core = peers()
    ctx = place * 2 + core
    ctxs = 2 * chips
    sibling = (seq, place * 2 + 1 - core)
    count = cot_ref.shape[0]
    buffers = [rest[6 * b : 6 * b + 6] for b in range(3)]
    (
        pair_sibling_sems,
        pair_chip_sems,
        gain_near_sems,
        gain_plane_sems,
        gain_line_sems,
        near_sems,
        plane_sems,
        line_sems,
        slab_sems,
        own_sems,
        swap_sems,
    ) = rest[18:]
    barrier = pltpu.get_barrier_semaphore()
    for k in range(1, ctxs):
        pl.semaphore_signal(
            barrier, inc=1, device_id=(seq, lax.rem(ctx + k, ctxs)), device_id_type=MESH
        )
    for j in range(1, seqs):
        pl.semaphore_signal(
            barrier, inc=1, device_id=(lax.rem(seq + j, seqs), ctx), device_id_type=MESH
        )
    pl.semaphore_wait(barrier, ctxs + seqs - 2)
    rows_own, gate_width = grad_gate_ref.shape
    units = gate_width // (seqs * ctxs)
    slab = gate_near.shape[-1] // seqs

    square = seqs == 4
    beside = seq + 1 - 2 * lax.rem(seq, 2)
    across = lax.rem(seq + 2, 4)
    direct = (1, 2) if square else range(1, seqs)

    start_slab, rest_slab, relay_slab, finish_slab, drain_slab = slab_sum(
        seqs,
        ctx,
        seq,
        pair_term_ref,
        gate_near,
        gate_middle,
        lambda half: half,
        slab_sems,
        own_sems,
    )

    def swap_copy(k):
        target = lax.rem(ctx + k, ctxs)
        return send_to(
            to_ctx.at[target],
            from_ctx.at[ctx],
            swap_sems.at[0, k],
            swap_sems.at[1, k],
            (seq, target),
        )

    start_slab()

    def block_of(j, k, which):
        row = (seq, beside, across, 3 - seq)[j] if square else lax.rem(seq + j, seqs)
        chip = lax.rem(place + k, chips)
        return row * ctxs + chip * 2 + which

    def near_copy(b, j, k):
        term, near = buffers[b][:2]
        return send_to(
            term.at[block_of(j, k, 1 - core)],
            near.at[j, k],
            near_sems.at[0, b, j, k],
            near_sems.at[1, b, j, k],
            sibling,
        )

    def plane_copy(b, j, k):
        near, plane_from = buffers[b][1:3]
        target = lax.rem(seq + j, seqs)
        if square:
            even = lax.rem(jnp.int32(k), 2) == 0
            target = (seq, beside, across, jnp.where(even, beside, across))[j]
        return send_to(
            near.at[j, k],
            plane_from.at[j, k],
            plane_sems.at[0, b, j, k],
            plane_sems.at[1, b, j, k],
            (target, ctx),
        )

    def line_copy(b, k):
        line_to, line_from = buffers[b][3:5]
        return send_to(
            line_to.at[k],
            line_from.at[k],
            line_sems.at[0, b, k],
            line_sems.at[1, b, k],
            (seq, lax.rem(place + k, chips) * 2 + core),
        )

    def start_near(b):
        def one(k, carry):
            for j in range(seqs):
                near_copy(b, j, lax.rem(k + 1, chips)).start()
            return carry

        lax.fori_loop(0, chips, one, 0)

    def run_plane(b):
        term, near = buffers[b][:2]

        def one(i, carry):
            k = lax.rem(i + 1, chips)
            for j in range(seqs - 1, -1, -1):
                near_copy(b, j, k).wait_recv()
                near[j, k] = (
                    term[block_of(j, k, core)].astype(jnp.float32)
                    + near[j, k].astype(jnp.float32)
                ).astype(jnp.bfloat16)
                if j == 3 or (j > 0 and not square):
                    plane_copy(b, j, k).start()
            if square:

                @pl.when(lax.rem(k, 2) == 0)
                def _():
                    plane_copy(b, 1, k).start()

                @pl.when(lax.rem(k, 2) == 1)
                def _():
                    plane_copy(b, 2, k).start()

            return carry

        lax.fori_loop(0, chips, one, 0)

    def relay_plane(b):
        _, near, plane_from = buffers[b][:3]

        def one(i, carry):
            k = lax.rem(i + 1, chips)
            plane_copy(b, 3, k).wait_recv()

            def add(j):
                near[j, k] = (
                    near[j, k].astype(jnp.float32) + plane_from[3, k].astype(jnp.float32)
                ).astype(jnp.bfloat16)
                plane_copy(b, j, k).start()

            @pl.when(lax.rem(k, 2) == 0)
            def _():
                add(2)

            @pl.when(lax.rem(k, 2) == 1)
            def _():
                add(1)

            return carry

        if square:
            lax.fori_loop(0, chips, one, 0)

    def run_line(b):
        _, near, plane_from, line_to, _, own = buffers[b]

        def one(i, carry):
            k = lax.rem(i + 1, chips)
            total = near[0, k].astype(jnp.float32)
            for j in direct:
                plane_copy(b, j, k).wait_recv()
                total = total + plane_from[j, k].astype(jnp.float32)

            @pl.when(k > 0)
            def _():
                line_to[k] = total.astype(jnp.bfloat16)
                line_copy(b, k).start()

            @pl.when(k == 0)
            def _():
                own[...] = total

            return carry

        lax.fori_loop(0, chips, one, 0)

    def finish(b):
        _, _, _, _, line_from, own = buffers[b]
        total = own[...]
        for k in range(1, chips):
            line_copy(b, k).wait_recv()
            total = total + line_from[k].astype(jnp.float32)
        return total

    def drain(b):
        def one(k, carry):
            for j in range(seqs):
                near_copy(b, j, k).wait_send()
                if j > 0:
                    plane_copy(b, j, k).wait_send()
            return carry

        lax.fori_loop(0, chips, one, 0)
        for k in range(1, chips):
            line_copy(b, k).wait_send()

    def pair_rows(chip, which):
        return pl.ds(pl.multiple_of((chip * 2 + which) * count, count), count)

    def pair_sibling_copy(k):
        return send_to(
            pair_to_sibling.at[k],
            pair_from_sibling.at[k],
            pair_sibling_sems.at[0, k],
            pair_sibling_sems.at[1, k],
            sibling,
        )

    def pair_chip_copy(k):
        return send_to(
            pair_to_chip.at[k],
            pair_from_chip.at[k],
            pair_chip_sems.at[0, k],
            pair_chip_sems.at[1, k],
            (seq, lax.rem(place + k, chips) * 2 + core),
        )

    scaling = 1.0 / math.sqrt(DH)
    cosine = cosine_ref[...]
    sinus = sinus_ref[...]
    residual = residual_ref[...]
    residual_factor = rms_factor(residual)
    fed_back = fed_back_ref[...]
    gain_term[...] = jnp.zeros_like(gain_term)
    gain_term[3:4, :] = grad_final_ref[...]
    gain_term[2:3, :] = jnp.sum(fed_back * residual * residual_factor, axis=0, keepdims=True)
    residual_back = cot_ref[...].astype(jnp.float32) + norm_back(
        residual, residual_factor, gain_all_ref[2:3, :], fed_back
    )
    input_grad_ref[...] = residual_back
    mixed = mixed_ref[...]
    mixed_factor = rms_factor(mixed)
    gain_term[1:2, :] = jnp.sum(residual_back * mixed * mixed_factor, axis=0, keepdims=True)
    mixed_back[...] = norm_back(mixed, mixed_factor, gain_all_ref[1:2, :], residual_back).astype(
        jnp.bfloat16
    )
    output_term = buffers[0][0]
    output_rows = output_term.shape[1]
    for h in range(H):
        columns = slice(h * DH, (h + 1) * DH)
        part = transposed_times(attended_ref[:, columns], mixed_back[...])
        each = DH // output_rows
        for i in range(each):
            output_term[h * each + i] = part[i * output_rows : (i + 1) * output_rows].astype(
                jnp.bfloat16
            )
    start_near(0)
    attended_back[...] = times_transposed(mixed_back[...], output_ref[...])

    def head(h, carry):
        rows = pl.ds(pl.multiple_of(h * count, count), count)
        columns = pl.ds(pl.multiple_of(h * DH, DH), DH)
        upper = attended_back[:, columns]
        upper_round[rows, :] = upper.astype(jnp.bfloat16)
        row_delta = jnp.sum(
            upper * attended_ref[:, columns].astype(jnp.float32), axis=-1, keepdims=True
        )
        allowed = places_ref[...] <= place_ref[...]
        scores = times_transposed(query_rot_ref[rows, :], both_ref[:, :DH]) * scaling
        probability = jnp.where(allowed, jnp.exp(scores - logsum_ref[rows, :]), 0.0)
        probs[rows, :] = probability.astype(jnp.bfloat16)
        prob_back = times_transposed(upper_round[rows, :], both_ref[:, DH:])
        score_back[rows, :] = (probability * (prob_back - row_delta) * scaling).astype(
            jnp.bfloat16
        )
        return carry

    rest_slab()
    lax.fori_loop(0, H, head, 0)
    relay_slab()
    pair_part[:, :DH] = transposed_times(score_back[...], query_rot_ref[...])
    pair_part[:, DH:] = transposed_times(probs[...], upper_round[...])
    for i in range(chips):
        k = (i + 1) % chips
        chip = lax.rem(place + k, chips)
        pair_to_sibling[k] = pair_part[pair_rows(chip, 1 - core), :].astype(jnp.bfloat16)
        pair_sibling_copy(k).start()
    run_plane(0)
    for i in range(chips - 1):
        k = i + 1
        chip = lax.rem(place + k, chips)
        pair_sibling_copy(k).wait_recv()
        pair_to_chip[k] = (
            pair_part[pair_rows(chip, core), :] + pair_from_sibling[k].astype(jnp.float32)
        ).astype(jnp.bfloat16)
        pair_chip_copy(k).start()

    gain_query = gain_all_ref[4:5, 0:DH]
    grad_query_gain = jnp.zeros((1, DH), jnp.float32)
    for h in range(H):
        rows = slice(h * count, (h + 1) * count)
        upward = rotate_back(times_right(score_back[rows, :], both_ref[:, :DH]), cosine, sinus)
        queries = queries_ref[rows, :]
        factor = rms_factor(queries)
        grad_query_gain += jnp.sum(upward * queries * factor, axis=0, keepdims=True)
        joint_back[:, h * DH : (h + 1) * DH] = norm_back(
            queries, factor, gain_query, upward
        ).astype(jnp.bfloat16)
    gain_term[4:5, :DH] = grad_query_gain

    def joint_term(b, columns):
        term = buffers[b][0]
        blocks, rows, _ = term.shape
        group = 256 // rows if 256 % rows == 0 else 8
        while blocks % group:
            group -= 1
        wide = group * rows
        for g in range(blocks // group):
            part = transposed_times(
                spread_ref[:, g * wide : (g + 1) * wide], joint_back[:, columns]
            )
            for i in range(group):
                term[g * group + i] = part[i * rows : (i + 1) * rows].astype(jnp.bfloat16)

    joint_term(1, slice(0, H * DH))
    start_near(1)
    finish_slab()
    for b in range(2):
        total = gate_near[0, b].astype(jnp.float32)
        for j in direct:
            total = total + gate_near[j, b].astype(jnp.float32)
        gate_total[b] = total
    for c in range(ctxs):
        for b in range(2):
            joined[b * rows_own : (b + 1) * rows_own, :] = gate_total[
                b, c * rows_own : (c + 1) * rows_own, :
            ]
        to_ctx[c] = joined[...].astype(jnp.bfloat16)
    for k in range(1, ctxs):
        swap_copy(k).start()
    from_ctx[ctx] = to_ctx[ctx]
    run_plane(1)
    relay_plane(0)
    run_line(0)

    pair_sibling_copy(0).wait_recv()
    own_pair = pair_part[pair_rows(place, core), :] + pair_from_sibling[0].astype(jnp.float32)
    for k in range(1, chips):
        pair_chip_copy(k).wait_recv()
        own_pair = own_pair + pair_from_chip[k].astype(jnp.float32)
    key_up = rotate_back(own_pair[:, :DH], cosine, sinus)
    key_rows = key_rows_ref[...]
    key_factor = rms_factor(key_rows)
    gain_term[4:5, DH : 2 * DH] = jnp.sum(key_up * key_rows * key_factor, axis=0, keepdims=True)
    joint_back[:, H * DH : (H + 1) * DH] = norm_back(
        key_rows, key_factor, gain_all_ref[4:5, DH : 2 * DH], key_up
    ).astype(jnp.bfloat16)
    joint_back[:, (H + 1) * DH :] = own_pair[:, DH:].astype(jnp.bfloat16)
    joint_term(2, slice(H * DH, (H + 2) * DH))
    start_near(2)
    run_plane(2)
    relay_plane(1)
    run_line(1)
    normed_wide[...] = times_transposed(joint_back[...], joint_ref[...])
    spaced = spread_ref.shape[1] // (seqs * ctxs)
    for i in range(seqs * ctxs):
        input_wide_back[:, i * rows_own : (i + 1) * rows_own] = normed_wide[
            :, i * spaced : i * spaced + rows_own
        ]
    normed_back = input_wide_back[...]
    input_wide = inputs_ref[...].astype(jnp.float32)
    input_factor = rms_factor(input_wide)
    gain_term[0:1, :] = jnp.sum(normed_back * input_wide * input_factor, axis=0, keepdims=True)

    def gain_near_copy():
        return send_to(gain_term, gain_near, gain_near_sems.at[0], gain_near_sems.at[1], sibling)

    def gain_plane_copy(j):
        return send_to(
            gain_chip,
            gain_plane.at[j],
            gain_plane_sems.at[0, j],
            gain_plane_sems.at[1, j],
            (lax.rem(seq + j, seqs), ctx),
        )

    def gain_line_copy(k):
        return send_to(
            gain_row,
            gain_line.at[k],
            gain_line_sems.at[0, k],
            gain_line_sems.at[1, k],
            (seq, lax.rem(place + k, chips) * 2 + core),
        )

    gain_near_copy().start()
    gain_near_copy().wait_recv()
    gain_chip[...] = gain_term[...] + gain_near[...]
    for j in range(1, seqs):
        gain_plane_copy(j).start()
    input_grad_ref[...] += norm_back(
        input_wide, input_factor, gain_all_ref[0:1, :], normed_back
    )
    relay_plane(2)
    run_line(2)
    total = gain_chip[...]
    for j in range(1, seqs):
        gain_plane_copy(j).wait_recv()
        total = total + gain_plane[j]
    gain_row[...] = total
    for k in range(1, chips):
        gain_line_copy(k).start()
    for k in range(1, ctxs):
        swap_copy(k).wait_recv()
    for c in range(ctxs):
        joined[...] = from_ctx[c].astype(jnp.float32)
        for b, target in ((0, grad_gate_ref), (1, grad_up_ref)):
            for s in range(seqs):
                first = (s * ctxs + c) * units
                target[:, first : first + units] = joined[
                    b * rows_own : (b + 1) * rows_own, s * slab : s * slab + units
                ]
    grad_output_ref[...] = finish(0)
    grad_query_ref[...] = finish(1)[0:rows_own]
    total = finish(2)[0:rows_own]
    grad_key_ref[...] = total[:, :DH]
    grad_value_ref[...] = total[:, DH:]
    total = gain_row[...]
    for k in range(1, chips):
        gain_line_copy(k).wait_recv()
        total = total + gain_line[k]
    gains_ref[...] = total
    for b in range(3):
        drain(b)
    drain_slab()
    for k in range(1, ctxs):
        swap_copy(k).wait_send()
    for k in range(chips):
        pair_sibling_copy(k).wait_send()
    for k in range(1, chips):
        pair_chip_copy(k).wait_send()
        gain_line_copy(k).wait_send()
    gain_near_copy().wait_send()
    for j in range(1, seqs):
        gain_plane_copy(j).wait_send()


def back_call(seqs, chips, padded_rows, output_rows, width_rows, units, *operands):
    fed_back = operands[0]
    count, width = fed_back.shape
    ctxs = 2 * chips
    total = ctxs * count
    blocks = seqs * ctxs
    wide = jnp.float32
    half = jnp.bfloat16
    dma = pltpu.SemaphoreType.DMA
    shape = jax.ShapeDtypeStruct
    vmem = pl.BlockSpec(memory_space=pltpu.VMEM)
    pair_term = operands[-1]
    near_slabs, middle_slabs = (3, 2) if seqs == 4 else (seqs, 1)
    unit_count = pair_term.shape[-1]
    both_rows = -(-2 * width_rows // 16) * 16
    hbm = pl.BlockSpec(memory_space=pl.ANY)
    sizes = ((output_rows, width), (padded_rows, H * DH), (padded_rows, 2 * DH))
    scratch = [
        pltpu.VMEM((count, width), half),
        pltpu.VMEM((count, H * DH), wide),
        pltpu.VMEM((H * count, DH), half),
        pltpu.VMEM((H * count, total), half),
        pltpu.VMEM((H * count, total), half),
        pltpu.VMEM((count, blocks * padded_rows), wide),
        pltpu.VMEM((count, width), wide),
        pltpu.VMEM((total, 2 * DH), wide),
        pltpu.VMEM((chips, count, 2 * DH), half),
        pltpu.VMEM((chips, count, 2 * DH), half),
        pltpu.VMEM((chips, count, 2 * DH), half),
        pltpu.VMEM((chips, count, 2 * DH), half),
        pltpu.VMEM((count, (H + 2) * DH), half),
        pltpu.VMEM((8, width), wide),
        pltpu.VMEM((8, width), wide),
        pltpu.VMEM((8, width), wide),
        pltpu.VMEM((seqs, 8, width), wide),
        pltpu.VMEM((8, width), wide),
        pltpu.VMEM((chips, 8, width), wide),
        pltpu.VMEM((near_slabs,) + pair_term.shape[1:], half),
        pltpu.VMEM((middle_slabs,) + pair_term.shape[1:], half),
        pltpu.VMEM(pair_term.shape[1:], wide),
        pltpu.VMEM((ctxs, both_rows, unit_count), half),
        pltpu.VMEM((ctxs, both_rows, unit_count), half),
        pltpu.VMEM((both_rows, unit_count), wide),
    ]
    for rows, columns in sizes:
        scratch += [
            pltpu.VMEM((blocks, rows, columns), half),
            pltpu.VMEM((seqs, chips, rows, columns), half),
            pltpu.VMEM((seqs, chips, rows, columns), half),
            pltpu.VMEM((chips, rows, columns), half),
            pltpu.VMEM((chips, rows, columns), half),
            pltpu.VMEM((rows, columns), wide),
        ]
    scratch += [
        dma((2, chips)),
        dma((2, chips)),
        dma((2,)),
        dma((2, seqs)),
        dma((2, chips)),
        dma((2, 3, seqs, chips)),
        dma((2, 3, seqs, chips)),
        dma((2, 3, chips)),
        dma((2, max(seqs, 6))),
        dma((3,)),
        dma((2, ctxs)),
    ]
    return pl.pallas_call(
        functools.partial(back_kernel, seqs, chips),
        out_shape=(
            shape((count, width), wide),
            shape(sizes[0], wide),
            shape((width_rows, H * DH), wide),
            shape((width_rows, DH), wide),
            shape((width_rows, DH), wide),
            shape((8, width), wide),
            shape((width_rows, blocks * units), wide),
            shape((width_rows, blocks * units), wide),
        ),
        in_specs=[vmem] * (len(operands) - 1) + [hbm],
        out_specs=(vmem,) * 8,
        scratch_shapes=scratch,
        compiler_params=pltpu.CompilerParams(
            collective_id=4, has_side_effects=True, vmem_limit_bytes=58 * 2**20
        ),
        cost_estimate=pl.CostEstimate(
            flops=8 * count * width * (H + 2) * DH,
            bytes_accessed=200 * 2**20,
            transcendentals=H * count * total,
        ),
        name="back",
    )(*operands)


def per_device(
    inputs,
    positions,
    attention_gain,
    query_weight,
    key_weight,
    value_weight,
    query_gain,
    key_gain,
    output_weight,
    attention_post,
    feedfwd_gain,
    gate_weight,
    up_weight,
    down_weight,
    feedfwd_post,
    cotangent,
):
    seq_total = lax.axis_size("seq")
    ctx_total = lax.axis_size("ctx")
    device_total = seq_total * ctx_total
    token_count = inputs.shape[0]
    width_rows = query_weight.shape[0]
    head_rows = query_gain.shape[0]
    unit_rows = down_weight.shape[0]

    block_number = (positions[:1] // token_count).astype(jnp.float32)
    small_rows = jnp.stack(
        [
            jnp.pad(vector.astype(jnp.float32), (0, 128 - vector.shape[0]))
            for vector in (
                attention_gain,
                attention_post,
                feedfwd_gain,
                feedfwd_post,
                query_gain,
                key_gain,
                block_number,
            )
        ]
    )
    chips = ctx_total // 2
    padded_rows = -(-(width_rows + 1) // 16) * 16
    cosine, sinus = rotary(positions)
    place_wide = positions.astype(jnp.float32)[:, None]
    (
        packets,
        outputs,
        gate_all,
        up_all,
        down_all,
        gain_all,
        places,
        spread,
        queries,
        key_rows,
        query_rot,
        both_rows,
        attended,
        logsum,
        mixed_values,
        residual,
        fed_all,
    ) = front_call(
        seq_total,
        chips,
        inputs,
        query_weight,
        key_weight,
        value_weight,
        small_rows,
        output_weight,
        gate_weight,
        up_weight,
        down_weight,
        cosine,
        sinus,
        place_wide,
    )
    block_out, grad_final, fed_back, grad_down, pair_term = feed_call(
        fed_all,
        residual,
        cotangent,
        gain_all,
        gate_all,
        up_all,
        down_all,
        unit_rows,
        seq_total,
        chips,
    )
    (
        input_grad,
        grad_output,
        grad_query,
        grad_key,
        grad_value,
        gains,
        grad_gate,
        grad_up,
    ) = back_call(
        seq_total,
        chips,
        padded_rows,
        output_weight.shape[0],
        width_rows,
        unit_rows,
        fed_back,
        residual,
        mixed_values,
        cotangent,
        inputs,
        spread,
        queries,
        key_rows,
        query_rot,
        both_rows,
        attended,
        logsum,
        outputs.reshape(H * DH, D),
        packets.reshape(-1, (H + 2) * DH),
        grad_final,
        gain_all,
        cosine,
        sinus,
        place_wide,
        places,
        pair_term,
    )
    device = lax.axis_index("seq") * ctx_total + lax.axis_index("ctx")

    def own_gain(row, start, size):
        return lax.dynamic_slice(gains, (row, start + device * size), (1, size))[0]

    return (
        block_out,
        input_grad,
        own_gain(0, 0, width_rows),
        grad_query,
        grad_key,
        grad_value,
        own_gain(4, 0, head_rows),
        own_gain(4, DH, head_rows),
        grad_output,
        own_gain(1, 0, width_rows),
        own_gain(2, 0, width_rows),
        grad_gate,
        grad_up,
        grad_down,
        own_gain(3, 0, width_rows),
    )


def solution(mesh):
    return jax.shard_map(
        per_device,
        mesh=mesh,
        in_specs=(
            P(("seq", "ctx"), None),
            P(("seq", "ctx")),
            P(("seq", "ctx")),
            P(("seq", "ctx"), None),
            P(("seq", "ctx"), None),
            P(("seq", "ctx"), None),
            P(("seq", "ctx")),
            P(("seq", "ctx")),
            P(("seq", "ctx"), None),
            P(("seq", "ctx")),
            P(("seq", "ctx")),
            P(("seq", "ctx"), None),
            P(("seq", "ctx"), None),
            P(("seq", "ctx"), None),
            P(("seq", "ctx")),
            P(("seq", "ctx"), None),
        ),
        out_specs=(
            P(("seq", "ctx"), None),
            P(("seq", "ctx"), None),
            P(("seq", "ctx")),
            P(("seq", "ctx"), None),
            P(("seq", "ctx"), None),
            P(("seq", "ctx"), None),
            P(("seq", "ctx")),
            P(("seq", "ctx")),
            P(("seq", "ctx"), None),
            P(("seq", "ctx")),
            P(("seq", "ctx")),
            P(("seq", "ctx"), None),
            P(("seq", "ctx"), None),
            P(("seq", "ctx"), None),
            P(("seq", "ctx")),
        ),
        check_vma=False,
    )
```

```python
import functools
import math

import jax
import jax.numpy as jnp
from jax import lax
from jax.experimental import pallas as pl
from jax.experimental.pallas import tpu as pltpu
from jax.sharding import PartitionSpec as P

D = 1152
H = 4
DH = 256
FF = 6912


EPSILON = 1e-06
THETA = 1000000.0
GELU_COEF = math.sqrt(2.0 / math.pi)


def rms_factor(values):
    return lax.rsqrt(jnp.mean(values * values, axis=-1, keepdims=True) + EPSILON)


def norm_back(values, factor, gain_vector, upstream):
    scaled = gain_vector * upstream
    cubed = factor * factor * factor
    return factor * scaled - values * cubed * jnp.mean(scaled * values, axis=-1, keepdims=True)


def rotary(places):
    half_width = DH // 2
    exponent = jnp.arange(half_width, dtype=jnp.float32) * (-2.0 / DH)
    frequency = jnp.power(jnp.float32(THETA), exponent)
    angles = places.astype(jnp.float32)[:, None] * frequency[None, :]
    return (jnp.cos(angles), jnp.sin(angles))


def rotate(values, cosine, sinus):
    half_width = values.shape[-1] // 2
    first = values[..., :half_width]
    second = values[..., half_width:]
    return jnp.concatenate(
        [first * cosine - second * sinus, second * cosine + first * sinus], axis=-1
    )


def rotate_back(upstream, cosine, sinus):
    half_width = upstream.shape[-1] // 2
    first = upstream[..., :half_width]
    second = upstream[..., half_width:]
    return jnp.concatenate(
        [first * cosine + second * sinus, second * cosine - first * sinus], axis=-1
    )


def gelu_tanh(values):
    inner = GELU_COEF * (values + 0.044715 * values * values * values)
    return 0.5 * values * (1.0 + jnp.tanh(inner))


def gelu_slope(values):
    inner = GELU_COEF * (values + 0.044715 * values * values * values)
    tangent = jnp.tanh(inner)
    return 0.5 * (1.0 + tangent) + 0.5 * values * (1.0 - tangent * tangent) * GELU_COEF * (
        1.0 + 3.0 * 0.044715 * values * values
    )


def times_right(left_side, right_side):
    return jnp.dot(left_side, right_side, preferred_element_type=jnp.float32)


def times_transposed(left_side, right_side):
    return lax.dot_general(
        left_side, right_side, (((1,), (1,)), ((), ())), preferred_element_type=jnp.float32
    )


def transposed_times(left_side, right_side):
    return lax.dot_general(
        left_side, right_side, (((0,), (0,)), ((), ())), preferred_element_type=jnp.float32
    )


BOTH = ("seq", "ctx")
MESH = pl.DeviceIdType.MESH


def peers():
    seq = lax.axis_index("seq")
    ctx = lax.axis_index("ctx")
    return seq, ctx // 2, lax.rem(ctx, 2)


def greet(seq, place, core, chips):
    barrier = pltpu.get_barrier_semaphore()
    pl.semaphore_signal(
        barrier, inc=1, device_id=(seq, place * 2 + 1 - core), device_id_type=MESH
    )
    for k in range(1, chips):
        other = lax.rem(place + k, chips) * 2 + core
        pl.semaphore_signal(barrier, inc=1, device_id=(seq, other), device_id_type=MESH)
    pl.semaphore_wait(barrier, chips)


def send_to(source, target, send_sem, recv_sem, device):
    return pltpu.make_async_remote_copy(
        src_ref=source,
        dst_ref=target,
        send_sem=send_sem,
        recv_sem=recv_sem,
        device_id=device,
        device_id_type=MESH,
    )


def plane_of(seq):
    return seq + 1 - 2 * lax.rem(seq, 2), lax.rem(seq + 2, 4)


def slab_sum(seqs, ctx, seq, term, near, middle, part_of, slab_sems, own_sems):
    square = seqs == 4
    beside, across = plane_of(seq)
    low, high = part_of(0), part_of(1)

    def copy(j):
        if not square:
            row = lax.rem(seq + j, seqs)
            origin, goal, target = term.at[row], near.at[j], row
        elif j == 0:
            origin, goal, target = term.at[3 - seq, low], middle.at[0, low], beside
        elif j == 1:
            origin, goal, target = term.at[3 - seq, high], middle.at[0, high], across
        elif j == 2:
            origin, goal, target = term.at[across, high], near.at[2, high], across
        elif j == 3:
            origin, goal, target = term.at[beside, low], near.at[1, low], beside
        elif j == 4:
            origin, goal, target = middle.at[1, low], near.at[2, low], across
        else:
            origin, goal, target = middle.at[1, high], near.at[1, high], beside
        return send_to(origin, goal, slab_sems.at[0, j], slab_sems.at[1, j], (target, ctx))

    def own():
        return pltpu.make_async_copy(term.at[seq], near.at[0], own_sems.at[0])

    def between(half):
        part = part_of(half)
        row = across if half == 0 else beside
        return pltpu.make_async_copy(
            term.at[row, part], middle.at[1, part], own_sems.at[1 + half]
        )

    def start():
        for j in range(2) if square else range(1, seqs):
            copy(j).start()
        own().start()
        if square:
            between(0).start()
            between(1).start()

    def rest():
        if square:
            copy(2).start()
            copy(3).start()

    def relay():
        if square:
            for half in range(2):
                part = part_of(half)
                between(half).wait()
                copy(half).wait_recv()
                middle[1, part] = (
                    middle[1, part].astype(jnp.float32) + middle[0, part].astype(jnp.float32)
                ).astype(jnp.bfloat16)
                copy(4 + half).start()

    def finish():
        own().wait()
        for j in range(2, 6) if square else range(1, seqs):
            copy(j).wait_recv()

    def drain():
        for j in range(6) if square else range(1, seqs):
            copy(j).wait_send()

    return start, rest, relay, finish, drain


def feed_kernel(
    seqs,
    chips,
    fed_all,
    residual_ref,
    cot_ref,
    gain_ref,
    gate_ref,
    up_ref,
    down_ref,
    block_ref,
    grad_final_ref,
    fed_back_ref,
    grad_down_ref,
    grad_pair_ref,
    hidden_ref,
    gate_back_ref,
    up_back_ref,
    back_all,
    gate_values,
    up_values,
    part,
    hidden_back,
    own,
    grad_part,
    down_term,
    down_near,
    down_middle,
    to_sibling,
    from_sibling,
    to_chip,
    from_chip,
    gather_sems,
    forward_sems,
    sibling_sems,
    chip_sems,
    slab_sems,
    own_sems,
):
    seq, place, core = peers()
    ctx = place * 2 + core
    sibling = (seq, place * 2 + 1 - core)
    count = residual_ref.shape[0]
    pair_count = 2 * count
    chunk = min(64, pair_count)
    slab = down_near.shape[1]
    barrier = pltpu.get_barrier_semaphore()
    pl.semaphore_signal(barrier, inc=1, device_id=sibling, device_id_type=MESH)
    for k in range(1, chips):
        other = lax.rem(place + k, chips) * 2 + core
        pl.semaphore_signal(barrier, inc=1, device_id=(seq, other), device_id_type=MESH)
    for j in range(1, seqs):
        pl.semaphore_signal(
            barrier, inc=1, device_id=(lax.rem(seq + j, seqs), ctx), device_id_type=MESH
        )
    start_down, rest_down, relay_down, finish_down, drain_down = slab_sum(
        seqs,
        ctx,
        seq,
        down_term,
        down_near,
        down_middle,
        lambda half: pl.ds(half * (slab // 2), slab // 2),
        slab_sems,
        own_sems,
    )

    def rows_of(chip, which):
        return pl.ds(pl.multiple_of((chip * 2 + which) * count, count), count)

    def pair_of(chip):
        return pl.ds(pl.multiple_of(chip * pair_count, pair_count), pair_count)

    mine = rows_of(place, core)

    def line_copy(side, d):
        sign = 1 - 2 * side
        block = back_all.at[rows_of(place - sign * (d - 1), core)]
        return send_to(
            block,
            block,
            gather_sems.at[0, side, d],
            gather_sems.at[1, side, d],
            (seq, (place + sign) * 2 + core),
        )

    def pass_copy(side, d):
        sign = 1 - 2 * side
        block = back_all.at[rows_of(place - sign * d, core)]
        return send_to(
            block, block, forward_sems.at[0, side, d], forward_sems.at[1, side, d], sibling
        )

    def comes(side, d):
        return place - d >= 0 if side == 0 else place + d < chips

    def goes(side, d):
        if side == 0:
            return jnp.logical_and(place + 1 < chips, place - (d - 1) >= 0)
        return jnp.logical_and(place - 1 >= 0, place + (d - 1) < chips)

    def relay_line(d):
        for side in range(2):

            @pl.when(comes(side, d))
            def _():
                line_copy(side, d).wait_recv()
                pass_copy(side, d).start()

            @pl.when(jnp.logical_and(comes(side, d), goes(side, d + 1)))
            def _():
                line_copy(side, d + 1).start()

    def sibling_copy(index, k):
        return send_to(
            to_sibling.at[k],
            from_sibling.at[index, k],
            sibling_sems.at[0, index, k],
            sibling_sems.at[1, index, k],
            sibling,
        )

    def chip_copy(index, k):
        chip = lax.rem(place - k + chips, chips)
        return send_to(
            to_chip.at[k],
            from_chip.at[index, k],
            chip_sems.at[0, index, k],
            chip_sems.at[1, index, k],
            (seq, chip * 2 + core),
        )

    def pass_part(index, k):
        other_rows = pl.ds(pl.multiple_of((1 - core) * count, count), count)
        own_rows = pl.ds(pl.multiple_of(core * count, count), count)
        to_sibling[k] = part[other_rows, :].astype(jnp.bfloat16)
        sibling_copy(index, k).start()
        sibling_copy(index, k).wait_recv()
        total = part[own_rows, :] + from_sibling[index, k].astype(jnp.float32)

        @pl.when(k == 0)
        def _():
            own[...] = total

        @pl.when(k > 0)
        def _():
            to_chip[k] = total.astype(jnp.bfloat16)
            chip_copy(index, k).start()

    def collect(index):
        for k in range(1, chips):
            chip_copy(index, k).wait_recv()
            own[...] += from_chip[index, k].astype(jnp.float32)
        for k in range(chips):
            sibling_copy(index, k).wait_send()
        for k in range(1, chips):
            chip_copy(index, k).wait_send()

    def forward_step(i, carry):
        k = lax.rem(i + 1, chips)
        rows = pair_of(lax.rem(place - k + chips, chips))
        block = fed_all[rows, :]
        gate_values[rows, :] = times_right(block, gate_ref[...])
        up_values[rows, :] = times_right(block, up_ref[...])

        def gated(j, carry):
            here = pl.ds(pl.multiple_of(rows.start + j * chunk, chunk), chunk)
            hidden_ref[here, :] = (gelu_tanh(gate_values[here, :]) * up_values[here, :]).astype(
                jnp.bfloat16
            )
            return carry

        lax.fori_loop(0, pair_count // chunk, gated, 0)
        part[...] = times_right(hidden_ref[rows, :], down_ref[...])

        @pl.when(i == 0)
        def _():
            pl.semaphore_wait(barrier, chips + seqs - 1)

        pass_part(0, k)
        return carry

    def backward_work(k):
        rows = pair_of(lax.rem(place - k + chips, chips))
        hidden_back[...] = times_transposed(back_all[rows, :], down_ref[...])

        def gated(j, carry):
            here = pl.ds(pl.multiple_of(rows.start + j * chunk, chunk), chunk)
            local = pl.ds(pl.multiple_of(j * chunk, chunk), chunk)
            gate_now = gate_values[here, :]
            upper = hidden_back[local, :]
            gate_back_ref[here, :] = (upper * up_values[here, :] * gelu_slope(gate_now)).astype(
                jnp.bfloat16
            )
            up_back_ref[here, :] = (upper * gelu_tanh(gate_now)).astype(jnp.bfloat16)
            return carry

        lax.fori_loop(0, pair_count // chunk, gated, 0)
        part[...] = times_transposed(gate_back_ref[rows, :], gate_ref[...])
        part[...] += times_transposed(up_back_ref[rows, :], up_ref[...])
        pass_part(1, k)

    def backward_step(d, carry):
        @pl.when(jnp.logical_or(d == 1, place - (d - 1) < 0))
        def _():
            relay_line(d)

        @pl.when(d == chips - 1)
        def _():
            for side in range(2):

                @pl.when(comes(side, d))
                def _():
                    pass_copy(side, d).wait_recv()

            for s in range(seqs):
                down_term[s] = transposed_times(
                    hidden_ref[:, s * slab : (s + 1) * slab], back_all[...]
                ).astype(jnp.bfloat16)
            start_down()
            rest_down()

        @pl.when(comes(0, d))
        def _():
            @pl.when(d < chips - 1)
            def _():
                pass_copy(0, d).wait_recv()

            backward_work(d)

        @pl.when(jnp.logical_and(comes(0, d), d < chips - 1))
        def _():
            relay_line(d + 1)

        @pl.when(comes(1, d))
        def _():
            @pl.when(d < chips - 1)
            def _():
                pass_copy(1, d).wait_recv()

            backward_work(chips - d)

        return carry

    lax.fori_loop(0, chips, forward_step, 0)
    collect(0)
    down_values = own[...]
    down_factor = rms_factor(down_values)
    gain_final = gain_ref[3:4, :]
    cot_wide = cot_ref[...].astype(jnp.float32)
    back_all[mine, :] = norm_back(down_values, down_factor, gain_final, cot_wide).astype(
        jnp.bfloat16
    )
    for side in range(2):

        @pl.when(goes(side, 1))
        def _():
            line_copy(side, 1).start()

    pass_copy(0, 0).start()
    block_ref[...] = (residual_ref[...] + down_values * down_factor * gain_final).astype(
        jnp.bfloat16
    )
    grad_final_ref[...] = jnp.sum(cot_wide * down_values * down_factor, axis=0, keepdims=True)
    pass_copy(0, 0).wait_recv()
    backward_work(0)
    lax.fori_loop(1, chips, backward_step, 0)
    relay_down()
    slabs, _, slab_rows, _ = grad_pair_ref.shape
    tall = grad_part.shape[0]
    for b, source in ((0, gate_back_ref), (1, up_back_ref)):
        for c in range(slabs * slab_rows // tall):
            grad_part[...] = transposed_times(
                fed_all[:, c * tall : (c + 1) * tall], source[...]
            )
            for s in range(slabs):
                low = max(s * slab_rows, c * tall)
                high = min((s + 1) * slab_rows, (c + 1) * tall)
                if low < high:
                    grad_pair_ref[s, b, low - s * slab_rows : high - s * slab_rows] = grad_part[
                        low - c * tall : high - c * tall, :
                    ].astype(jnp.bfloat16)
    collect(1)
    fed_back_ref[...] = own[...]
    finish_down()
    total = down_near[0].astype(jnp.float32)
    for j in (1, 2) if seqs == 4 else range(1, seqs):
        total = total + down_near[j].astype(jnp.float32)
    grad_down_ref[...] = total[0 : grad_down_ref.shape[0]]
    drain_down()
    pass_copy(0, 0).wait_send()
    for d in range(1, chips):
        for side in range(2):

            @pl.when(comes(side, d))
            def _():
                pass_copy(side, d).wait_send()

            @pl.when(goes(side, d))
            def _():
                line_copy(side, d).wait_send()


def feed_call(fed, residual, cot, gain, gate, up, down, down_rows, seqs, chips):
    count, width = residual.shape
    total = 2 * chips * count
    units = down.shape[0]
    slab = units // seqs
    wide = jnp.float32
    half = jnp.bfloat16
    dma = pltpu.SemaphoreType.DMA
    shape = jax.ShapeDtypeStruct
    vmem = pl.BlockSpec(memory_space=pltpu.VMEM)
    near_slabs, middle_slabs = (3, 2) if seqs == 4 else (seqs, 1)
    return pl.pallas_call(
        functools.partial(feed_kernel, seqs, chips),
        out_shape=(
            shape((count, width), half),
            shape((1, width), wide),
            shape((count, width), wide),
            shape((down_rows, width), wide),
            shape((seqs, 2, width // seqs, units), half),
        ),
        in_specs=[vmem] * 7,
        out_specs=(vmem,) * 5,
        scratch_shapes=[
            pltpu.VMEM((total, units), half),
            pltpu.VMEM((total, units), half),
            pltpu.VMEM((total, units), half),
            pltpu.VMEM((total, width), half),
            pltpu.VMEM((total, units), wide),
            pltpu.VMEM((total, units), wide),
            pltpu.VMEM((2 * count, width), wide),
            pltpu.VMEM((2 * count, units), wide),
            pltpu.VMEM((count, width), wide),
            pltpu.VMEM((width // 3, units), wide),
            pltpu.VMEM((seqs, slab, width), half),
            pltpu.VMEM((near_slabs, slab, width), half),
            pltpu.VMEM((middle_slabs, slab, width), half),
            pltpu.VMEM((chips, count, width), half),
            pltpu.VMEM((2, chips, count, width), half),
            pltpu.VMEM((chips, count, width), half),
            pltpu.VMEM((2, chips, count, width), half),
            dma((2, 2, chips + 1)),
            dma((2, 2, chips + 1)),
            dma((2, 2, chips)),
            dma((2, 2, chips)),
            dma((2, max(seqs, 6))),
            dma((3,)),
        ],
        compiler_params=pltpu.CompilerParams(
            collective_id=1, has_side_effects=True, vmem_limit_bytes=58 * 2**20
        ),
        name="feed",
    )(fed, residual, cot, gain, gate, up, down)


def front_kernel(
    seqs,
    chips,
    inputs_ref,
    query_ref,
    key_ref,
    value_ref,
    small_ref,
    output_ref,
    gate_ref,
    up_ref,
    down_ref,
    cosine_ref,
    sinus_ref,
    place_ref,
    packets,
    outputs,
    gate_all,
    up_all,
    down_all,
    gains,
    places,
    spread_ref,
    queries_ref,
    key_rows_ref,
    query_rot_ref,
    both_ref,
    attended_ref,
    logsum_ref,
    mixed_ref,
    residual_ref,
    fed_all,
    wide_packet,
    own_packet,
    own_down,
    to_ctx,
    from_ctx,
    joined,
    packed,
    spread,
    spread_gain,
    own_pair,
    line_sems,
    plane_sems,
    core_sems,
    swap_sems,
    slab_sems,
    gather_sems,
    forward_sems,
    fed_sems,
    pass_sems,
):
    seq, place, core = peers()
    ctx = place * 2 + core
    sibling = (seq, place * 2 + 1 - core)
    ctxs = 2 * chips
    blocks = seqs * ctxs
    count, width = inputs_ref.shape
    rows = gate_ref.shape[0]
    head_rows = DH // blocks
    units = down_ref.shape[0]
    slab = own_down.shape[0]
    square = seqs == 4
    beside = seq + 1 - 2 * lax.rem(seq, 2)
    across = lax.rem(seq + 2, 4)
    direct = (1, 2) if square else range(1, seqs)
    barrier = pltpu.get_barrier_semaphore()
    for k in range(1, ctxs):
        pl.semaphore_signal(
            barrier, inc=1, device_id=(seq, lax.rem(ctx + k, ctxs)), device_id_type=MESH
        )
    for j in range(1, seqs):
        pl.semaphore_signal(
            barrier, inc=1, device_id=(lax.rem(seq + j, seqs), ctx), device_id_type=MESH
        )

    def index_of(row, chip, which):
        return row * ctxs + chip * 2 + which

    both = ((own_packet, packets), (output_ref, outputs))

    def line_copy(b, k):
        own, everything = both[b]
        chip = lax.rem(place + k, chips)
        return send_to(
            own,
            everything.at[index_of(seq, place, core)],
            line_sems.at[0, b, k],
            line_sems.at[1, b, k],
            (seq, chip * 2 + core),
        )

    def plane_copy(b, j, k):
        everything = both[b][1]
        chip = lax.rem(place - k + chips, chips)
        row, target = seq, lax.rem(seq + j, seqs)
        if square:
            even = lax.rem(jnp.int32(k), 2) == 0
            if j == 3:
                row = jnp.where(even, beside, across)
                target = jnp.where(even, across, beside)
            else:
                target = beside if j == 1 else across
        block = everything.at[index_of(row, chip, core)]
        return send_to(
            block,
            block,
            plane_sems.at[0, b, j, k],
            plane_sems.at[1, b, j, k],
            (target, ctx),
        )

    def core_copy(b, j, k):
        everything = both[b][1]
        row = (seq, beside, across, 3 - seq)[j] if square else lax.rem(seq - j + seqs, seqs)
        chip = lax.rem(place - k + chips, chips)
        block = everything.at[index_of(row, chip, core)]
        return send_to(
            block, block, core_sems.at[0, b, j, k], core_sems.at[1, b, j, k], sibling
        )

    def swap_copy(k):
        target = lax.rem(ctx + k, ctxs)
        return send_to(
            to_ctx.at[target],
            from_ctx.at[ctx],
            swap_sems.at[0, k],
            swap_sems.at[1, k],
            (seq, target),
        )

    def slab_copy(which, j):
        height = slab if which == 0 else ctxs * rows
        everything = (down_all, gate_all, up_all)[which]
        first, size, target = seq * height, height, lax.rem(seq + j, seqs)
        if square:
            half = height // 2
            if j == 0:
                target = beside
            elif j == 1:
                target = across
            elif j == 2:
                first, size, target = beside * height, half, across
            else:
                first, size, target = across * height + half, half, beside
            first = pl.multiple_of(first, half)
        else:
            first = pl.multiple_of(first, height)
        here = everything.at[pl.ds(first, size)]
        return send_to(
            here,
            here,
            slab_sems.at[0, which, j],
            slab_sems.at[1, which, j],
            (target, ctx),
        )

    def start_slab(which):
        for j in (0, 1) if square else range(1, seqs):
            slab_copy(which, j).start()

    def relay_slab(which):
        if square:
            slab_copy(which, 0).wait_recv()
            slab_copy(which, 2).start()
            slab_copy(which, 1).wait_recv()
            slab_copy(which, 3).start()

    def finish_slab(which):
        if square:
            slab_copy(which, 0).wait_send()
            slab_copy(which, 1).wait_send()
            slab_copy(which, 2).wait()
            slab_copy(which, 3).wait()
        else:
            for j in range(1, seqs):
                slab_copy(which, j).wait()

    def rows_of(chip):
        return pl.ds(pl.multiple_of((chip * 2 + core) * count, count), count)

    def gather_copy(k):
        chip = lax.rem(place + k, chips)
        return send_to(
            own_pair,
            both_ref.at[rows_of(place)],
            gather_sems.at[0, k],
            gather_sems.at[1, k],
            (seq, chip * 2 + core),
        )

    def forward_copy(k):
        chip = lax.rem(place - k + chips, chips)
        block = both_ref.at[rows_of(chip)]
        return send_to(block, block, forward_sems.at[0, k], forward_sems.at[1, k], sibling)

    def fed_copy(k):
        chip = lax.rem(place + k, chips)
        block = fed_all.at[rows_of(place)]
        return send_to(
            block, block, fed_sems.at[0, k], fed_sems.at[1, k], (seq, chip * 2 + core)
        )

    def pass_copy(k):
        chip = lax.rem(place - k + chips, chips)
        block = fed_all.at[rows_of(chip)]
        return send_to(block, block, pass_sems.at[0, k], pass_sems.at[1, k], sibling)

    def start_own(b):
        own, everything = both[b]
        for k in range(1, chips):
            line_copy(b, k).start()
        everything[index_of(seq, place, core)] = own[...]
        core_copy(b, 0, 0).start()

    def start_plane(b):
        for j in direct:
            plane_copy(b, j, 0).start()

    def line_step(b):
        def one(k, carry):
            line_copy(b, k).wait_recv()
            for j in direct:
                plane_copy(b, j, k).start()
            core_copy(b, 0, k).start()
            return carry

        lax.fori_loop(1, chips, one, 0)

    def plane_step(b):
        def one(k, carry):
            for j in direct:
                plane_copy(b, j, k).wait_recv()
            if square:
                plane_copy(b, 3, k).start()
            for j in direct:
                core_copy(b, j, k).start()
            return carry

        lax.fori_loop(0, chips, one, 0)

    def relay_step(b):
        def one(k, carry):
            plane_copy(b, 3, k).wait_recv()
            core_copy(b, 3, k).start()
            return carry

        if square:
            lax.fori_loop(0, chips, one, 0)

    def core_step(b):
        def one(k, carry):
            for j in range(seqs):
                core_copy(b, j, k).wait_recv()
            return carry

        lax.fori_loop(0, chips, one, 0)

    def drain(b):
        def one(k, carry):
            for j in range(seqs):
                core_copy(b, j, k).wait_send()
                if j > 0:
                    plane_copy(b, j, k).wait_send()
            return carry

        lax.fori_loop(0, chips, one, 0)
        for k in range(1, chips):
            line_copy(b, k).wait_send()

    wide_packet[...] = jnp.zeros_like(wide_packet)
    wide_packet[0:rows, 0 : H * DH] = query_ref[...].astype(jnp.float32)
    wide_packet[0:rows, H * DH : (H + 1) * DH] = key_ref[...].astype(jnp.float32)
    wide_packet[0:rows, (H + 1) * DH :] = value_ref[...].astype(jnp.float32)
    for g in range(4):
        wide_packet[rows : rows + 1, g * rows : (g + 1) * rows] = small_ref[g : g + 1, :rows]
    for g in range(2):
        first = 4 * rows + g * head_rows
        wide_packet[rows : rows + 1, first : first + head_rows] = small_ref[
            4 + g : 5 + g, :head_rows
        ]
    first = 4 * rows + 2 * head_rows
    wide_packet[rows : rows + 1, first : first + 1] = small_ref[6:7, 0:1]
    own_packet[...] = wide_packet[...].astype(jnp.bfloat16)
    own_down[...] = jnp.zeros_like(own_down)
    own_down[0:units, :] = down_ref[...].astype(jnp.float32)
    down_all[pl.ds(pl.multiple_of(seq * slab, slab), slab), :] = own_down[...].astype(
        jnp.bfloat16
    )
    pl.semaphore_wait(barrier, ctxs + seqs - 2)
    start_own(0)
    start_plane(0)
    start_slab(0)

    joined[...] = jnp.zeros_like(joined)
    for c in range(ctxs):
        for b, source in ((0, gate_ref), (1, up_ref)):
            for s in range(seqs):
                first = (s * ctxs + c) * units
                low = first // 128 * 128
                high = min(-(-(first + units) // 128) * 128, gate_ref.shape[1])
                wide = source[:, low:high].astype(jnp.float32)
                joined[b * rows : (b + 1) * rows, s * slab : s * slab + units] = wide[
                    :, first - low : first - low + units
                ]
        to_ctx[c] = joined[...].astype(jnp.bfloat16)
    line_step(0)
    for k in range(1, ctxs):
        swap_copy(k).start()
    from_ctx[ctx] = to_ctx[ctx]

    input_wide = inputs_ref[...].astype(jnp.float32)
    scaled = input_wide * rms_factor(input_wide)
    spread[...] = jnp.zeros_like(spread)
    step = packets.shape[1]
    for i in range(blocks):
        spread[:, i * step : i * step + rows] = scaled[:, i * rows : (i + 1) * rows]
    plane_step(0)
    relay_step(0)
    start_own(1)
    start_plane(1)
    core_step(0)

    gains[...] = jnp.zeros_like(gains)
    spread_gain[...] = jnp.zeros_like(spread_gain)
    base = rows // 8 * 8
    for i in range(blocks):
        line = packets[i, base:, :256].astype(jnp.float32)[rows - base : rows - base + 1]
        for g in range(4):
            gains[g : g + 1, i * rows : (i + 1) * rows] = line[:, g * rows : (g + 1) * rows]
        spread_gain[0:1, i * step : i * step + rows] = line[:, 0:rows]
        for g in range(2):
            first = 4 * rows + g * head_rows
            here = g * DH + i * head_rows
            gains[4:5, here : here + head_rows] = line[:, first : first + head_rows]
    number_at = 4 * rows + 2 * head_rows
    offsets = lax.broadcasted_iota(jnp.int32, (1, count), 1).astype(jnp.float32)
    for c in range(ctxs):
        line = packets[seq * ctxs + c, base:, :256].astype(jnp.float32)
        number = line[rows - base : rows - base + 1, number_at : number_at + 1]
        places[:, c * count : (c + 1) * count] = number * count + offsets
    spread_ref[...] = (spread[...] * spread_gain[0:1, :]).astype(jnp.bfloat16)
    joint = packets.reshape(blocks * step, (H + 2) * DH)
    cosine = cosine_ref[...]
    sinus = sinus_ref[...]
    pair = times_right(spread_ref[...], joint[:, H * DH :])
    key_rows = pair[:, :DH]
    key_rows_ref[...] = key_rows
    key_rot = rotate(key_rows * rms_factor(key_rows) * gains[4:5, DH : 2 * DH], cosine, sinus)
    own_pair[:, :DH] = key_rot.astype(jnp.bfloat16)
    own_pair[:, DH:] = pair[:, DH:].astype(jnp.bfloat16)
    both_ref[rows_of(place), :] = own_pair[...]
    for k in range(1, chips):
        gather_copy(k).start()
    forward_copy(0).start()
    for k in range(1, ctxs):
        swap_copy(k).wait_recv()
    for c in range(ctxs):
        joined[...] = from_ctx[c].astype(jnp.float32)
        for b in range(2):
            packed[b, c * rows : (c + 1) * rows, :] = joined[b * rows : (b + 1) * rows, :]
    height = ctxs * rows
    here = pl.ds(pl.multiple_of(seq * height, height), height)
    gate_all[here, :] = packed[0].astype(jnp.bfloat16)
    up_all[here, :] = packed[1].astype(jnp.bfloat16)
    start_slab(1)
    start_slab(2)
    relay_slab(0)
    line_step(1)
    for h in range(H):
        mine = slice(h * count, (h + 1) * count)
        queries = times_right(spread_ref[...], joint[:, h * DH : (h + 1) * DH])
        queries_ref[mine, :] = queries
        query_rot_ref[mine, :] = rotate(
            queries * rms_factor(queries) * gains[4:5, 0:DH], cosine, sinus
        ).astype(jnp.bfloat16)
    plane_step(1)
    for k in range(1, chips):
        gather_copy(k).wait_recv()
        forward_copy(k).start()
    for k in range(chips):
        forward_copy(k).wait_recv()
    scaling = 1.0 / math.sqrt(DH)

    def head(h, carry):
        mine = pl.ds(pl.multiple_of(h * count, count), count)
        columns = pl.ds(pl.multiple_of(h * DH, DH), DH)
        allowed = places[...] <= place_ref[...]
        scores = times_transposed(query_rot_ref[mine, :], both_ref[:, :DH]) * scaling
        expscore = jnp.where(allowed, jnp.exp(scores), 0.0)
        weight_sum = jnp.sum(expscore, axis=-1, keepdims=True)
        summed = times_right(expscore.astype(jnp.bfloat16), both_ref[:, DH:])
        attended_ref[:, columns] = (summed / weight_sum).astype(jnp.bfloat16)
        logsum_ref[mine, :] = jnp.log(weight_sum)
        return carry

    lax.fori_loop(0, H, head, 0)
    relay_slab(1)
    relay_step(1)
    core_step(1)
    mixed_ref[...] = times_right(attended_ref[...], outputs.reshape(H * DH, width)[...])
    mixed = mixed_ref[...]
    residual = inputs_ref[...].astype(jnp.float32) + mixed * rms_factor(mixed) * gains[1:2, :]
    residual_ref[...] = residual
    fed_all[rows_of(place), :] = (residual * rms_factor(residual) * gains[2:3, :]).astype(
        jnp.bfloat16
    )
    for k in range(1, chips):
        fed_copy(k).start()
    pass_copy(0).start()
    for b in range(2):
        drain(b)
    for k in range(1, ctxs):
        swap_copy(k).wait_send()
    for k in range(chips):
        forward_copy(k).wait_send()
    for k in range(1, chips):
        gather_copy(k).wait_send()
    relay_slab(2)
    for k in range(1, chips):
        fed_copy(k).wait_recv()
        pass_copy(k).start()
    for which in range(3):
        finish_slab(which)
    for k in range(chips):
        pass_copy(k).wait()
    for k in range(1, chips):
        fed_copy(k).wait_send()


def front_call(seqs, chips, *operands):
    inputs, query_weight = operands[:2]
    output, gate, _, down = operands[5:9]
    count, width = inputs.shape
    wide = jnp.float32
    half = jnp.bfloat16
    dma = pltpu.SemaphoreType.DMA
    shape = jax.ShapeDtypeStruct
    vmem = pl.BlockSpec(memory_space=pltpu.VMEM)
    ctxs = 2 * chips
    total = ctxs * count
    blocks = seqs * ctxs
    rows = gate.shape[0]
    packet_rows = -(-(rows + 1) // 16) * 16
    joint_width = (H + 2) * DH
    slab = -(-down.shape[0] // 16) * 16
    unit_count = seqs * slab
    padded = -(-2 * rows // 16) * 16
    return pl.pallas_call(
        functools.partial(front_kernel, seqs, chips),
        out_shape=(
            shape((blocks, packet_rows, joint_width), half),
            shape((blocks,) + output.shape, half),
            shape((width, unit_count), half),
            shape((width, unit_count), half),
            shape((unit_count, width), half),
            shape((8, width), wide),
            shape((1, total), wide),
            shape((count, blocks * packet_rows), half),
            shape((H * count, DH), wide),
            shape((count, DH), wide),
            shape((H * count, DH), half),
            shape((total, 2 * DH), half),
            shape((count, H * DH), half),
            shape((H * count, 1), wide),
            shape((count, width), wide),
            shape((count, width), wide),
            shape((total, width), half),
        ),
        in_specs=[vmem] * len(operands),
        out_specs=(vmem,) * 17,
        scratch_shapes=[
            pltpu.VMEM((packet_rows, joint_width), wide),
            pltpu.VMEM((packet_rows, joint_width), half),
            pltpu.VMEM((slab, width), wide),
            pltpu.VMEM((ctxs, padded, unit_count), half),
            pltpu.VMEM((ctxs, padded, unit_count), half),
            pltpu.VMEM((padded, unit_count), wide),
            pltpu.VMEM((2, ctxs * rows, unit_count), wide),
            pltpu.VMEM((count, blocks * packet_rows), wide),
            pltpu.VMEM((8, blocks * packet_rows), wide),
            pltpu.VMEM((count, 2 * DH), half),
            dma((2, 2, chips)),
            dma((2, 2, seqs, chips)),
            dma((2, 2, seqs, chips)),
            dma((2, ctxs)),
            dma((2, 3, max(seqs, 4))),
            dma((2, chips)),
            dma((2, chips)),
            dma((2, chips)),
            dma((2, chips)),
        ],
        compiler_params=pltpu.CompilerParams(
            collective_id=2, has_side_effects=True, vmem_limit_bytes=58 * 2**20
        ),
        name="front",
    )(*operands)


def back_kernel(
    seqs,
    chips,
    fed_back_ref,
    residual_ref,
    mixed_ref,
    cot_ref,
    inputs_ref,
    spread_ref,
    queries_ref,
    key_rows_ref,
    query_rot_ref,
    both_ref,
    attended_ref,
    logsum_ref,
    output_ref,
    joint_ref,
    grad_final_ref,
    gain_all_ref,
    cosine_ref,
    sinus_ref,
    place_ref,
    places_ref,
    pair_term_ref,
    input_grad_ref,
    grad_output_ref,
    grad_query_ref,
    grad_key_ref,
    grad_value_ref,
    gains_ref,
    grad_gate_ref,
    grad_up_ref,
    mixed_back,
    attended_back,
    upper_round,
    probs,
    score_back,
    normed_wide,
    input_wide_back,
    pair_part,
    pair_to_sibling,
    pair_from_sibling,
    pair_to_chip,
    pair_from_chip,
    joint_back,
    gain_term,
    gain_near,
    gain_chip,
    gain_plane,
    gain_row,
    gain_line,
    gate_near,
    gate_middle,
    gate_total,
    to_ctx,
    from_ctx,
    joined,
    joint_held,
    *rest,
):
    seq, place, core = peers()
    ctx = place * 2 + core
    ctxs = 2 * chips
    sibling = (seq, place * 2 + 1 - core)
    count = cot_ref.shape[0]
    buffers = [rest[6 * b : 6 * b + 6] for b in range(3)]
    (
        pair_sibling_sems,
        pair_chip_sems,
        gain_near_sems,
        gain_plane_sems,
        gain_line_sems,
        near_sems,
        plane_sems,
        line_sems,
        slab_sems,
        own_sems,
        swap_sems,
    ) = rest[18:]
    barrier = pltpu.get_barrier_semaphore()
    for k in range(1, ctxs):
        pl.semaphore_signal(
            barrier, inc=1, device_id=(seq, lax.rem(ctx + k, ctxs)), device_id_type=MESH
        )
    for j in range(1, seqs):
        pl.semaphore_signal(
            barrier, inc=1, device_id=(lax.rem(seq + j, seqs), ctx), device_id_type=MESH
        )
    pl.semaphore_wait(barrier, ctxs + seqs - 2)
    rows_own, gate_width = grad_gate_ref.shape
    units = gate_width // (seqs * ctxs)
    slab = gate_near.shape[-1] // seqs

    square = seqs == 4
    beside = seq + 1 - 2 * lax.rem(seq, 2)
    across = lax.rem(seq + 2, 4)
    direct = (1, 2) if square else range(1, seqs)

    start_slab, rest_slab, relay_slab, finish_slab, drain_slab = slab_sum(
        seqs,
        ctx,
        seq,
        pair_term_ref,
        gate_near,
        gate_middle,
        lambda half: half,
        slab_sems,
        own_sems,
    )

    def swap_copy(k):
        target = lax.rem(ctx + k, ctxs)
        return send_to(
            to_ctx.at[target],
            from_ctx.at[ctx],
            swap_sems.at[0, k],
            swap_sems.at[1, k],
            (seq, target),
        )

    start_slab()
    joint_copy = pltpu.make_async_copy(joint_ref, joint_held, own_sems.at[3])
    joint_copy.start()

    def block_of(j, k, which):
        row = (seq, beside, across, 3 - seq)[j] if square else lax.rem(seq + j, seqs)
        chip = lax.rem(place + k, chips)
        return row * ctxs + chip * 2 + which

    def near_copy(b, j, k):
        term, near = buffers[b][:2]
        return send_to(
            term.at[block_of(j, k, 1 - core)],
            near.at[j, k],
            near_sems.at[0, b, j, k],
            near_sems.at[1, b, j, k],
            sibling,
        )

    def plane_copy(b, j, k):
        near, plane_from = buffers[b][1:3]
        target = lax.rem(seq + j, seqs)
        if square:
            even = lax.rem(jnp.int32(k), 2) == 0
            target = (seq, beside, across, jnp.where(even, beside, across))[j]
        return send_to(
            near.at[j, k],
            plane_from.at[j, k],
            plane_sems.at[0, b, j, k],
            plane_sems.at[1, b, j, k],
            (target, ctx),
        )

    def line_copy(b, k):
        line_to, line_from = buffers[b][3:5]
        return send_to(
            line_to.at[k],
            line_from.at[k],
            line_sems.at[0, b, k],
            line_sems.at[1, b, k],
            (seq, lax.rem(place + k, chips) * 2 + core),
        )

    def start_near(b):
        def one(k, carry):
            for j in range(seqs):
                near_copy(b, j, lax.rem(k + 1, chips)).start()
            return carry

        lax.fori_loop(0, chips, one, 0)

    def run_plane(b):
        term, near = buffers[b][:2]

        def one(i, carry):
            k = lax.rem(i + 1, chips)
            for j in range(seqs - 1, -1, -1):
                near_copy(b, j, k).wait_recv()
                near[j, k] = (
                    term[block_of(j, k, core)].astype(jnp.float32)
                    + near[j, k].astype(jnp.float32)
                ).astype(jnp.bfloat16)
                if j == 3 or (j > 0 and not square):
                    plane_copy(b, j, k).start()
            if square:

                @pl.when(lax.rem(k, 2) == 0)
                def _():
                    plane_copy(b, 1, k).start()

                @pl.when(lax.rem(k, 2) == 1)
                def _():
                    plane_copy(b, 2, k).start()

            return carry

        lax.fori_loop(0, chips, one, 0)

    def relay_plane(b):
        _, near, plane_from = buffers[b][:3]

        def one(i, carry):
            k = lax.rem(i + 1, chips)
            plane_copy(b, 3, k).wait_recv()

            def add(j):
                near[j, k] = (
                    near[j, k].astype(jnp.float32) + plane_from[3, k].astype(jnp.float32)
                ).astype(jnp.bfloat16)
                plane_copy(b, j, k).start()

            @pl.when(lax.rem(k, 2) == 0)
            def _():
                add(2)

            @pl.when(lax.rem(k, 2) == 1)
            def _():
                add(1)

            return carry

        if square:
            lax.fori_loop(0, chips, one, 0)

    def run_line(b):
        _, near, plane_from, line_to, _, own = buffers[b]

        def one(i, carry):
            k = lax.rem(i + 1, chips)
            total = near[0, k].astype(jnp.float32)
            for j in direct:
                plane_copy(b, j, k).wait_recv()
                total = total + plane_from[j, k].astype(jnp.float32)

            @pl.when(k > 0)
            def _():
                line_to[k] = total.astype(jnp.bfloat16)
                line_copy(b, k).start()

            @pl.when(k == 0)
            def _():
                own[...] = total

            return carry

        lax.fori_loop(0, chips, one, 0)

    def finish(b):
        _, _, _, _, line_from, own = buffers[b]
        total = own[...]
        for k in range(1, chips):
            line_copy(b, k).wait_recv()
            total = total + line_from[k].astype(jnp.float32)
        return total

    def drain(b):
        def one(k, carry):
            for j in range(seqs):
                near_copy(b, j, k).wait_send()
                if j > 0:
                    plane_copy(b, j, k).wait_send()
            return carry

        lax.fori_loop(0, chips, one, 0)
        for k in range(1, chips):
            line_copy(b, k).wait_send()

    def pair_rows(chip, which):
        return pl.ds(pl.multiple_of((chip * 2 + which) * count, count), count)

    def pair_sibling_copy(k):
        return send_to(
            pair_to_sibling.at[k],
            pair_from_sibling.at[k],
            pair_sibling_sems.at[0, k],
            pair_sibling_sems.at[1, k],
            sibling,
        )

    def pair_chip_copy(k):
        return send_to(
            pair_to_chip.at[k],
            pair_from_chip.at[k],
            pair_chip_sems.at[0, k],
            pair_chip_sems.at[1, k],
            (seq, lax.rem(place + k, chips) * 2 + core),
        )

    scaling = 1.0 / math.sqrt(DH)
    cosine = cosine_ref[...]
    sinus = sinus_ref[...]
    residual = residual_ref[...]
    residual_factor = rms_factor(residual)
    fed_back = fed_back_ref[...]
    gain_term[...] = jnp.zeros_like(gain_term)
    gain_term[3:4, :] = grad_final_ref[...]
    gain_term[2:3, :] = jnp.sum(fed_back * residual * residual_factor, axis=0, keepdims=True)
    residual_back = cot_ref[...].astype(jnp.float32) + norm_back(
        residual, residual_factor, gain_all_ref[2:3, :], fed_back
    )
    input_grad_ref[...] = residual_back
    mixed = mixed_ref[...]
    mixed_factor = rms_factor(mixed)
    gain_term[1:2, :] = jnp.sum(residual_back * mixed * mixed_factor, axis=0, keepdims=True)
    mixed_back[...] = norm_back(mixed, mixed_factor, gain_all_ref[1:2, :], residual_back).astype(
        jnp.bfloat16
    )
    output_term = buffers[0][0]
    output_rows = output_term.shape[1]
    for h in range(H):
        columns = slice(h * DH, (h + 1) * DH)
        part = transposed_times(attended_ref[:, columns], mixed_back[...])
        each = DH // output_rows
        for i in range(each):
            output_term[h * each + i] = part[i * output_rows : (i + 1) * output_rows].astype(
                jnp.bfloat16
            )
    start_near(0)
    attended_back[...] = times_transposed(mixed_back[...], output_ref[...])

    def head(h, carry):
        rows = pl.ds(pl.multiple_of(h * count, count), count)
        columns = pl.ds(pl.multiple_of(h * DH, DH), DH)
        upper = attended_back[:, columns]
        upper_round[rows, :] = upper.astype(jnp.bfloat16)
        row_delta = jnp.sum(
            upper * attended_ref[:, columns].astype(jnp.float32), axis=-1, keepdims=True
        )
        allowed = places_ref[...] <= place_ref[...]
        scores = times_transposed(query_rot_ref[rows, :], both_ref[:, :DH]) * scaling
        probability = jnp.where(allowed, jnp.exp(scores - logsum_ref[rows, :]), 0.0)
        probs[rows, :] = probability.astype(jnp.bfloat16)
        prob_back = times_transposed(upper_round[rows, :], both_ref[:, DH:])
        score_back[rows, :] = (probability * (prob_back - row_delta) * scaling).astype(
            jnp.bfloat16
        )
        return carry

    rest_slab()
    lax.fori_loop(0, H, head, 0)
    relay_slab()
    pair_part[:, :DH] = transposed_times(score_back[...], query_rot_ref[...])
    pair_part[:, DH:] = transposed_times(probs[...], upper_round[...])
    for i in range(chips):
        k = (i + 1) % chips
        chip = lax.rem(place + k, chips)
        pair_to_sibling[k] = pair_part[pair_rows(chip, 1 - core), :].astype(jnp.bfloat16)
        pair_sibling_copy(k).start()
    run_plane(0)
    for i in range(chips - 1):
        k = i + 1
        chip = lax.rem(place + k, chips)
        pair_sibling_copy(k).wait_recv()
        pair_to_chip[k] = (
            pair_part[pair_rows(chip, core), :] + pair_from_sibling[k].astype(jnp.float32)
        ).astype(jnp.bfloat16)
        pair_chip_copy(k).start()

    gain_query = gain_all_ref[4:5, 0:DH]
    grad_query_gain = jnp.zeros((1, DH), jnp.float32)
    for h in range(H):
        rows = slice(h * count, (h + 1) * count)
        upward = rotate_back(times_right(score_back[rows, :], both_ref[:, :DH]), cosine, sinus)
        queries = queries_ref[rows, :]
        factor = rms_factor(queries)
        grad_query_gain += jnp.sum(upward * queries * factor, axis=0, keepdims=True)
        joint_back[:, h * DH : (h + 1) * DH] = norm_back(
            queries, factor, gain_query, upward
        ).astype(jnp.bfloat16)
    gain_term[4:5, :DH] = grad_query_gain

    def joint_term(b, columns):
        term = buffers[b][0]
        blocks, rows, _ = term.shape
        group = 256 // rows if 256 % rows == 0 else 8
        while blocks % group:
            group -= 1
        wide = group * rows
        for g in range(blocks // group):
            part = transposed_times(
                spread_ref[:, g * wide : (g + 1) * wide], joint_back[:, columns]
            )
            for i in range(group):
                term[g * group + i] = part[i * rows : (i + 1) * rows].astype(jnp.bfloat16)

    joint_term(1, slice(0, H * DH))
    start_near(1)
    finish_slab()
    for b in range(2):
        total = gate_near[0, b].astype(jnp.float32)
        for j in direct:
            total = total + gate_near[j, b].astype(jnp.float32)
        gate_total[b] = total
    for c in range(ctxs):
        for b in range(2):
            joined[b * rows_own : (b + 1) * rows_own, :] = gate_total[
                b, c * rows_own : (c + 1) * rows_own, :
            ]
        to_ctx[c] = joined[...].astype(jnp.bfloat16)
    for k in range(1, ctxs):
        swap_copy(k).start()
    from_ctx[ctx] = to_ctx[ctx]
    run_plane(1)
    relay_plane(0)
    run_line(0)

    pair_sibling_copy(0).wait_recv()
    own_pair = pair_part[pair_rows(place, core), :] + pair_from_sibling[0].astype(jnp.float32)
    for k in range(1, chips):
        pair_chip_copy(k).wait_recv()
        own_pair = own_pair + pair_from_chip[k].astype(jnp.float32)
    key_up = rotate_back(own_pair[:, :DH], cosine, sinus)
    key_rows = key_rows_ref[...]
    key_factor = rms_factor(key_rows)
    gain_term[4:5, DH : 2 * DH] = jnp.sum(key_up * key_rows * key_factor, axis=0, keepdims=True)
    joint_back[:, H * DH : (H + 1) * DH] = norm_back(
        key_rows, key_factor, gain_all_ref[4:5, DH : 2 * DH], key_up
    ).astype(jnp.bfloat16)
    joint_back[:, (H + 1) * DH :] = own_pair[:, DH:].astype(jnp.bfloat16)
    joint_term(2, slice(H * DH, (H + 2) * DH))
    start_near(2)
    run_plane(2)
    relay_plane(1)
    run_line(1)
    joint_copy.wait()
    normed_wide[...] = times_transposed(joint_back[...], joint_held[...])
    spaced = spread_ref.shape[1] // (seqs * ctxs)
    for i in range(seqs * ctxs):
        input_wide_back[:, i * rows_own : (i + 1) * rows_own] = normed_wide[
            :, i * spaced : i * spaced + rows_own
        ]
    normed_back = input_wide_back[...]
    input_wide = inputs_ref[...].astype(jnp.float32)
    input_factor = rms_factor(input_wide)
    gain_term[0:1, :] = jnp.sum(normed_back * input_wide * input_factor, axis=0, keepdims=True)

    def gain_near_copy():
        return send_to(gain_term, gain_near, gain_near_sems.at[0], gain_near_sems.at[1], sibling)

    def gain_plane_copy(j):
        return send_to(
            gain_chip,
            gain_plane.at[j],
            gain_plane_sems.at[0, j],
            gain_plane_sems.at[1, j],
            (lax.rem(seq + j, seqs), ctx),
        )

    def gain_line_copy(k):
        return send_to(
            gain_row,
            gain_line.at[k],
            gain_line_sems.at[0, k],
            gain_line_sems.at[1, k],
            (seq, lax.rem(place + k, chips) * 2 + core),
        )

    gain_near_copy().start()
    gain_near_copy().wait_recv()
    gain_chip[...] = gain_term[...] + gain_near[...]
    for j in range(1, seqs):
        gain_plane_copy(j).start()
    input_grad_ref[...] += norm_back(
        input_wide, input_factor, gain_all_ref[0:1, :], normed_back
    )
    relay_plane(2)
    run_line(2)
    total = gain_chip[...]
    for j in range(1, seqs):
        gain_plane_copy(j).wait_recv()
        total = total + gain_plane[j]
    gain_row[...] = total
    for k in range(1, chips):
        gain_line_copy(k).start()
    for k in range(1, ctxs):
        swap_copy(k).wait_recv()
    for c in range(ctxs):
        joined[...] = from_ctx[c].astype(jnp.float32)
        for b, target in ((0, grad_gate_ref), (1, grad_up_ref)):
            for s in range(seqs):
                first = (s * ctxs + c) * units
                target[:, first : first + units] = joined[
                    b * rows_own : (b + 1) * rows_own, s * slab : s * slab + units
                ]
    grad_output_ref[...] = finish(0)
    grad_query_ref[...] = finish(1)[0:rows_own]
    total = finish(2)[0:rows_own]
    grad_key_ref[...] = total[:, :DH]
    grad_value_ref[...] = total[:, DH:]
    total = gain_row[...]
    for k in range(1, chips):
        gain_line_copy(k).wait_recv()
        total = total + gain_line[k]
    gains_ref[...] = total
    for b in range(3):
        drain(b)
    drain_slab()
    for k in range(1, ctxs):
        swap_copy(k).wait_send()
    for k in range(chips):
        pair_sibling_copy(k).wait_send()
    for k in range(1, chips):
        pair_chip_copy(k).wait_send()
        gain_line_copy(k).wait_send()
    gain_near_copy().wait_send()
    for j in range(1, seqs):
        gain_plane_copy(j).wait_send()


def back_call(seqs, chips, padded_rows, output_rows, width_rows, units, *operands):
    fed_back = operands[0]
    count, width = fed_back.shape
    ctxs = 2 * chips
    total = ctxs * count
    blocks = seqs * ctxs
    wide = jnp.float32
    half = jnp.bfloat16
    dma = pltpu.SemaphoreType.DMA
    shape = jax.ShapeDtypeStruct
    vmem = pl.BlockSpec(memory_space=pltpu.VMEM)
    pair_term = operands[-1]
    near_slabs, middle_slabs = (3, 2) if seqs == 4 else (seqs, 1)
    unit_count = pair_term.shape[-1]
    both_rows = -(-2 * width_rows // 16) * 16
    hbm = pl.BlockSpec(memory_space=pl.ANY)
    sizes = ((output_rows, width), (padded_rows, H * DH), (padded_rows, 2 * DH))
    scratch = [
        pltpu.VMEM((count, width), half),
        pltpu.VMEM((count, H * DH), wide),
        pltpu.VMEM((H * count, DH), half),
        pltpu.VMEM((H * count, total), half),
        pltpu.VMEM((H * count, total), half),
        pltpu.VMEM((count, blocks * padded_rows), wide),
        pltpu.VMEM((count, width), wide),
        pltpu.VMEM((total, 2 * DH), wide),
        pltpu.VMEM((chips, count, 2 * DH), half),
        pltpu.VMEM((chips, count, 2 * DH), half),
        pltpu.VMEM((chips, count, 2 * DH), half),
        pltpu.VMEM((chips, count, 2 * DH), half),
        pltpu.VMEM((count, (H + 2) * DH), half),
        pltpu.VMEM((8, width), wide),
        pltpu.VMEM((8, width), wide),
        pltpu.VMEM((8, width), wide),
        pltpu.VMEM((seqs, 8, width), wide),
        pltpu.VMEM((8, width), wide),
        pltpu.VMEM((chips, 8, width), wide),
        pltpu.VMEM((near_slabs,) + pair_term.shape[1:], half),
        pltpu.VMEM((middle_slabs,) + pair_term.shape[1:], half),
        pltpu.VMEM(pair_term.shape[1:], wide),
        pltpu.VMEM((ctxs, both_rows, unit_count), half),
        pltpu.VMEM((ctxs, both_rows, unit_count), half),
        pltpu.VMEM((both_rows, unit_count), wide),
        pltpu.VMEM(operands[13].shape, half),
    ]
    for rows, columns in sizes:
        scratch += [
            pltpu.VMEM((blocks, rows, columns), half),
            pltpu.VMEM((seqs, chips, rows, columns), half),
            pltpu.VMEM((seqs, chips, rows, columns), half),
            pltpu.VMEM((chips, rows, columns), half),
            pltpu.VMEM((chips, rows, columns), half),
            pltpu.VMEM((rows, columns), wide),
        ]
    scratch += [
        dma((2, chips)),
        dma((2, chips)),
        dma((2,)),
        dma((2, seqs)),
        dma((2, chips)),
        dma((2, 3, seqs, chips)),
        dma((2, 3, seqs, chips)),
        dma((2, 3, chips)),
        dma((2, max(seqs, 6))),
        dma((4,)),
        dma((2, ctxs)),
    ]
    return pl.pallas_call(
        functools.partial(back_kernel, seqs, chips),
        out_shape=(
            shape((count, width), wide),
            shape(sizes[0], wide),
            shape((width_rows, H * DH), wide),
            shape((width_rows, DH), wide),
            shape((width_rows, DH), wide),
            shape((8, width), wide),
            shape((width_rows, blocks * units), wide),
            shape((width_rows, blocks * units), wide),
        ),
        in_specs=[vmem] * 13 + [hbm] + [vmem] * (len(operands) - 15) + [hbm],
        out_specs=(vmem,) * 8,
        scratch_shapes=scratch,
        compiler_params=pltpu.CompilerParams(
            collective_id=4, has_side_effects=True, vmem_limit_bytes=58 * 2**20
        ),
        cost_estimate=pl.CostEstimate(
            flops=8 * count * width * (H + 2) * DH,
            bytes_accessed=200 * 2**20,
            transcendentals=H * count * total,
        ),
        name="back",
    )(*operands)


def per_device(
    inputs,
    positions,
    attention_gain,
    query_weight,
    key_weight,
    value_weight,
    query_gain,
    key_gain,
    output_weight,
    attention_post,
    feedfwd_gain,
    gate_weight,
    up_weight,
    down_weight,
    feedfwd_post,
    cotangent,
):
    seq_total = lax.axis_size("seq")
    ctx_total = lax.axis_size("ctx")
    device_total = seq_total * ctx_total
    token_count = inputs.shape[0]
    width_rows = query_weight.shape[0]
    head_rows = query_gain.shape[0]
    unit_rows = down_weight.shape[0]

    block_number = (positions[:1] // token_count).astype(jnp.float32)
    small_rows = jnp.stack(
        [
            jnp.pad(vector.astype(jnp.float32), (0, 128 - vector.shape[0]))
            for vector in (
                attention_gain,
                attention_post,
                feedfwd_gain,
                feedfwd_post,
                query_gain,
                key_gain,
                block_number,
            )
        ]
    )
    chips = ctx_total // 2
    padded_rows = -(-(width_rows + 1) // 16) * 16
    cosine, sinus = rotary(positions)
    place_wide = positions.astype(jnp.float32)[:, None]
    (
        packets,
        outputs,
        gate_all,
        up_all,
        down_all,
        gain_all,
        places,
        spread,
        queries,
        key_rows,
        query_rot,
        both_rows,
        attended,
        logsum,
        mixed_values,
        residual,
        fed_all,
    ) = front_call(
        seq_total,
        chips,
        inputs,
        query_weight,
        key_weight,
        value_weight,
        small_rows,
        output_weight,
        gate_weight,
        up_weight,
        down_weight,
        cosine,
        sinus,
        place_wide,
    )
    block_out, grad_final, fed_back, grad_down, pair_term = feed_call(
        fed_all,
        residual,
        cotangent,
        gain_all,
        gate_all,
        up_all,
        down_all,
        unit_rows,
        seq_total,
        chips,
    )
    (
        input_grad,
        grad_output,
        grad_query,
        grad_key,
        grad_value,
        gains,
        grad_gate,
        grad_up,
    ) = back_call(
        seq_total,
        chips,
        padded_rows,
        output_weight.shape[0],
        width_rows,
        unit_rows,
        fed_back,
        residual,
        mixed_values,
        cotangent,
        inputs,
        spread,
        queries,
        key_rows,
        query_rot,
        both_rows,
        attended,
        logsum,
        outputs.reshape(H * DH, D),
        packets.reshape(-1, (H + 2) * DH),
        grad_final,
        gain_all,
        cosine,
        sinus,
        place_wide,
        places,
        pair_term,
    )
    device = lax.axis_index("seq") * ctx_total + lax.axis_index("ctx")

    def own_gain(row, start, size):
        return lax.dynamic_slice(gains, (row, start + device * size), (1, size))[0]

    return (
        block_out,
        input_grad,
        own_gain(0, 0, width_rows),
        grad_query,
        grad_key,
        grad_value,
        own_gain(4, 0, head_rows),
        own_gain(4, DH, head_rows),
        grad_output,
        own_gain(1, 0, width_rows),
        own_gain(2, 0, width_rows),
        grad_gate,
        grad_up,
        grad_down,
        own_gain(3, 0, width_rows),
    )


def solution(mesh):
    return jax.shard_map(
        per_device,
        mesh=mesh,
        in_specs=(
            P(("seq", "ctx"), None),
            P(("seq", "ctx")),
            P(("seq", "ctx")),
            P(("seq", "ctx"), None),
            P(("seq", "ctx"), None),
            P(("seq", "ctx"), None),
            P(("seq", "ctx")),
            P(("seq", "ctx")),
            P(("seq", "ctx"), None),
            P(("seq", "ctx")),
            P(("seq", "ctx")),
            P(("seq", "ctx"), None),
            P(("seq", "ctx"), None),
            P(("seq", "ctx"), None),
            P(("seq", "ctx")),
            P(("seq", "ctx"), None),
        ),
        out_specs=(
            P(("seq", "ctx"), None),
            P(("seq", "ctx"), None),
            P(("seq", "ctx")),
            P(("seq", "ctx"), None),
            P(("seq", "ctx"), None),
            P(("seq", "ctx"), None),
            P(("seq", "ctx")),
            P(("seq", "ctx")),
            P(("seq", "ctx"), None),
            P(("seq", "ctx")),
            P(("seq", "ctx")),
            P(("seq", "ctx"), None),
            P(("seq", "ctx"), None),
            P(("seq", "ctx"), None),
            P(("seq", "ctx")),
        ),
        check_vma=False,
    )
```
